32 devices in a mesh: dp: 16 (over z, x, core), tensor: 2 (over y).
Axes of the slice: x: 2, y: 2, z: 4, core: 2. Of those that a mesh axis runs over, the one named last changes fastest.
Arguments:
- tokens: bfloat16 [4096, 2048], P(('dp', 'tensor')), may hold values from -6 to 6
- segment_ids: int32 [16, 256], P('dp'), may hold values from 0 to 3, never falling along the last dimension, each value on 1 to 128 neighbouring positions
- w_query: bfloat16 [2048, 2048], P('dp', 'tensor'), may hold values from -0.125 to 0.125
- w_key: bfloat16 [2048, 2048], P('dp', 'tensor'), may hold values from -0.125 to 0.125
- w_value: bfloat16 [2048, 2048], P('dp', 'tensor'), may hold values from -0.125 to 0.125
- w_output: bfloat16 [2048, 2048], P('dp', 'tensor'), may hold values from -0.125 to 0.125
- w_gate: bfloat16 [2048, 8192], P('dp', 'tensor'), may hold values from -0.125 to 0.125
- w_up: bfloat16 [2048, 8192], P('dp', 'tensor'), may hold values from -0.125 to 0.125
- w_down: bfloat16 [2048, 8192], P('dp', 'tensor'), may hold values from -0.0625 to 0.0625
- query_gain: float32 [2048], P(('dp', 'tensor')), may hold values from 0.5 to 2
- key_gain: float32 [2048], P(('dp', 'tensor')), may hold values from 0.5 to 2
- attn_gain: float32 [2048], P(('dp', 'tensor')), may hold values from 0.1 to 1.9
- ffn_gain: float32 [2048], P(('dp', 'tensor')), may hold values from 0.1 to 1.9
- cotangent: bfloat16 [4096, 2048], P(('dp', 'tensor')), may hold values from -6 to 6
Outputs:
- output: bfloat16 [4096, 2048], P(('dp', 'tensor'))
- grad_tokens: float32 [4096, 2048], P(('dp', 'tensor'))
- grad_query: float32 [2048, 2048], P('dp', 'tensor')
- grad_key: float32 [2048, 2048], P('dp', 'tensor')
- grad_value: float32 [2048, 2048], P('dp', 'tensor')
- grad_output: float32 [2048, 2048], P('dp', 'tensor')
- grad_gate: float32 [2048, 8192], P('dp', 'tensor')
- grad_up: float32 [2048, 8192], P('dp', 'tensor')
- grad_down: float32 [2048, 8192], P('dp', 'tensor')
- grad_query_gain: float32 [2048], P(('dp', 'tensor'))
- grad_key_gain: float32 [2048], P(('dp', 'tensor'))
- grad_attn_gain: float32 [2048], P(('dp', 'tensor'))
- grad_ffn_gain: float32 [2048], P(('dp', 'tensor'))
The draws below stay inside these ranges and needn't reach their ends.
Inputs may be any that keep to these rules, and one draw needn't show every extreme that they name: `segment_ids`: within each sequence the ids never fall; each document has 1 to 128 tokens, and one has exactly 128.
All inputs are finite; a program needn't handle non-finite values.
Results may differ from the reference program's by a relative error of at most 0.015.
Values may be sent and summed in bfloat16 or wider, within the bound.
No kernel may reach another device: no remote copies, remote signals or barrier semaphores. Data moves between devices by JAX's collectives and lax.ppermute only.
A program may use at most 384 MiB of HBM per device.

```python
import math
import jax
import jax.numpy as jnp
import numpy as np
from jax import lax

D = 2048
H = 16
HD = 128
FF = 8192
SEQ = 256
DOCS = 4
SEQS = 16
TOKENS = 4096


def norm_gain_draw(base_key):
    uniform_level = jax.random.uniform(base_key, (D,), jnp.float32)
    return 0.5 + 1.5 * uniform_level


def draw_query_gain(key, part):
    return norm_gain_draw(jax.random.fold_in(key, 17))


def draw_key_gain(key, part):
    return norm_gain_draw(jax.random.fold_in(key, 29))


def raised(array, own_key, source, target, parts, factor):
    owner, partner = [(jnp.arange(array.shape[position]) // (array.shape[position] // parts)).reshape([-1 if axis == position else 1 for axis in range(array.ndim)]) for position in (source, target)]
    chosen = jax.random.permutation(own_key, parts)[partner]
    strong = (owner == chosen) | (owner == (partner + parts // 2) % parts)
    return jnp.where(strong, factor * array, array)


def block_scale(own_key, shape, pieces, low, largest):
    def one(dim, blocks):
        steps = jax.random.uniform(jax.random.fold_in(jax.random.fold_in(own_key, 6), dim), (blocks,), jnp.float32, low / len(pieces), largest / len(pieces))
        return jnp.repeat(jnp.exp(steps), shape[dim] // blocks).reshape((-1,) + (1,) * (len(shape) - dim - 1))

    gain = one(*pieces[0])
    for cut in pieces[1:]:
        gain = gain * one(*cut)
    return gain


def length_profile(count, total, most, lean):
    loads = [(1 << 20) // math.isqrt(standing ** lean) + 1 for standing in range(2, count + 1)]
    rest, holding = total - most - (count - 1), [1] * (count - 1)
    while rest > 0:
        free = [i for i in range(count - 1) if holding[i] < most]
        mass, remaining = sum([loads[i] for i in free]), rest
        for i in free:
            extra = min(most - holding[i], max(1, remaining * loads[i] // mass), rest)
            holding[i] = holding[i] + extra
            rest = rest - extra
    return np.array([most] + holding)


def ragged_sizes(own_key, amount, total, most, skew):
    if amount == 2:
        one = jax.random.randint(own_key, (), max(1, total - most), min(most, total - 1) + 1)
        return jnp.stack([one, total - one])
    sizes = jnp.asarray(length_profile(amount, total, most, skew), jnp.int32)
    couples = (amount - 1) // 2
    donor, sink = sizes[1:1 + 2 * couples:2], sizes[2:2 + 2 * couples:2]
    room = jnp.minimum(donor - 1, most - sink)
    passed = jax.random.randint(jax.random.fold_in(own_key, 1), (couples,), 0, 1 << 20) % (room + 1)
    sizes = sizes.at[1:1 + 2 * couples:2].set(donor - passed).at[2:2 + 2 * couples:2].set(sink + passed)
    return sizes[jax.random.permutation(jax.random.fold_in(own_key, 2), amount)]


def noise(key, extent, width, most, cuts=(), held_as=jnp.bfloat16):
    values = jax.random.normal(key, extent, jnp.float32) * width
    if len(cuts) > 0:
        values = block_scale(key, extent, cuts, -0.22, 0.18) * values
    return jnp.clip(values, min=-most, max=most).astype(held_as)


def bell_draw_with(key, shape, spread, limit, cuts, heavy, kind=jnp.bfloat16):
    array = spread * jax.random.normal(key, shape, jnp.float32)
    if cuts:
        array = array * block_scale(key, shape, cuts, -0.22, 0.18)
    return jnp.clip(raised(array, jax.random.fold_in(key, 3), *heavy), -limit, limit).astype(kind)


def setup_inputs(seed: int = 0) -> dict:
    splits = jax.random.split(jax.random.key(seed), 15)
    return {
        "tokens": bell_draw_with(splits[0], (TOKENS, D), 1.0, 6.0, ((0, 32),), (0, 1, 32, 2.75)),
        "segment_ids": jax.vmap(lambda own: jnp.searchsorted(jnp.cumsum(ragged_sizes(own, DOCS, SEQ, SEQ // 2, 0)), jnp.arange(SEQ), side="right"))(jax.random.split(splits[1], SEQS)).reshape((SEQS, SEQ)).astype(jnp.int32),
        "w_query": noise(splits[2], (D, D), D ** -0.5, 0.125, ((0, 16), (1, 2))),
        "w_key": noise(splits[3], (D, D), D ** -0.5, 0.125, ((0, 16), (1, 2))),
        "w_value": noise(splits[4], (D, D), D ** -0.5, 0.125, ((0, 16), (1, 2))),
        "w_output": noise(splits[5], (D, D), D ** -0.5, 0.125, ((0, 16), (1, 2))),
        "w_gate": noise(splits[6], (D, FF), D ** -0.5, 0.125, ((0, 16), (1, 2))),
        "w_up": noise(splits[7], (D, FF), D ** -0.5, 0.125, ((0, 16), (1, 2))),
        "w_down": noise(splits[8], (D, FF), FF ** -0.5, 0.0625, ((0, 16), (1, 2))),
        "query_gain": draw_query_gain(jax.random.fold_in(splits[14], 71), 0),
        "key_gain": draw_key_gain(jax.random.fold_in(splits[14], 71), 0),
        "attn_gain": jnp.clip(1.0 + 0.18 * jax.random.normal(splits[11], (D,), jnp.float32), 0.1, 1.9),
        "ffn_gain": jnp.clip(1.0 + 0.18 * jax.random.normal(splits[12], (D,), jnp.float32), 0.1, 1.9),
        "cotangent": bell_draw_with(splits[13], (TOKENS, D), 1.0, 6.0, ((0, 32),), (0, 1, 32, 2.75)),
    }


EPSILON = 1e-06
NEGATIVE = -1e+30

def rms_scale(values):
    return lax.rsqrt(lax.optimization_barrier(jnp.mean(values * values, axis=-1, keepdims=True)) + EPSILON)

def widen(values):
    return lax.optimization_barrier(values).astype(jnp.float32)

def reference(tokens, segment_ids, w_query, w_key, w_value, w_output, w_gate, w_up, w_down, query_gain, key_gain, attn_gain, ffn_gain, cotangent):
    score_scale = 1.0 / math.sqrt(HD)
    seq_tokens = tokens.reshape(SEQS, SEQ, D)
    seq_cotangent = cotangent.reshape(SEQS, SEQ, D)
    positions = jnp.arange(SEQ)
    causal = positions[:, None] >= positions[None, :]

    def one_sequence(totals, inputs):
        seq_x, seq_ids, seq_dy = inputs
        visible = causal & (seq_ids[:, None] == seq_ids[None, :])
        query = jnp.dot(seq_x, w_query, preferred_element_type=jnp.float32)
        key_proj = jnp.dot(seq_x, w_key, preferred_element_type=jnp.float32)
        value_bf = jnp.dot(seq_x, w_value, preferred_element_type=jnp.float32).astype(jnp.bfloat16)
        q_rms = rms_scale(query)
        k_rms = rms_scale(key_proj)
        normed_query = (query * q_rms * query_gain).astype(jnp.bfloat16)
        normed_key = (key_proj * k_rms * key_gain).astype(jnp.bfloat16)
        query_heads = widen(normed_query).reshape(SEQ, H, HD)
        key_heads = widen(normed_key).reshape(SEQ, H, HD)
        value_heads = widen(value_bf).reshape(SEQ, H, HD)
        scores = jnp.einsum('qhd,khd->hqk', query_heads, key_heads) * score_scale
        scores = jnp.where(visible[None], scores, NEGATIVE)
        peak = lax.optimization_barrier(jnp.max(scores, axis=-1, keepdims=True))
        expo = jnp.exp(scores - peak)
        total = lax.optimization_barrier(jnp.sum(expo, axis=-1, keepdims=True))
        log_total = peak + jnp.log(total)
        prob_bf = (expo / total).astype(jnp.bfloat16)
        attn = jnp.einsum('hqk,khd->qhd', widen(prob_bf), value_heads).reshape(SEQ, D).astype(jnp.bfloat16)
        proj = jnp.dot(attn, w_output.T, preferred_element_type=jnp.float32)
        attn_rms = rms_scale(proj)
        resid = seq_x.astype(jnp.float32) + proj * attn_rms * attn_gain
        resid_bf = resid.astype(jnp.bfloat16)
        gate = jnp.dot(resid_bf, w_gate, preferred_element_type=jnp.float32)
        up_proj = jnp.dot(resid_bf, w_up, preferred_element_type=jnp.float32)
        sigma = jax.nn.sigmoid(gate)
        act = (gate * sigma * up_proj).astype(jnp.bfloat16)
        ffn = jnp.dot(act, w_down.T, preferred_element_type=jnp.float32)
        ffn_rms = rms_scale(ffn)
        output = (resid + ffn * ffn_rms * ffn_gain).astype(jnp.bfloat16)
        d_out = seq_dy.astype(jnp.float32)
        ffn_gain_term = lax.optimization_barrier(jnp.sum(d_out * ffn * ffn_rms, axis=0))
        scaled_out = d_out * ffn_gain
        d_ffn = (ffn_rms * (scaled_out - ffn * ffn_rms * ffn_rms * lax.optimization_barrier(jnp.mean(scaled_out * ffn, axis=-1, keepdims=True)))).astype(jnp.bfloat16)
        down_term = jnp.dot(d_ffn.T, act, preferred_element_type=jnp.float32)
        d_act = jnp.dot(d_ffn, w_down, preferred_element_type=jnp.float32)
        d_gate = (d_act * up_proj * sigma * (1.0 + gate * (1.0 - sigma))).astype(jnp.bfloat16)
        d_up = (d_act * gate * sigma).astype(jnp.bfloat16)
        gate_term = jnp.dot(resid_bf.T, d_gate, preferred_element_type=jnp.float32)
        up_term = jnp.dot(resid_bf.T, d_up, preferred_element_type=jnp.float32)
        d_hidden = jnp.dot(d_gate, w_gate.T, preferred_element_type=jnp.float32) + jnp.dot(d_up, w_up.T, preferred_element_type=jnp.float32)
        d_resid = d_out + d_hidden
        attn_gain_term = lax.optimization_barrier(jnp.sum(d_resid * proj * attn_rms, axis=0))
        scaled_resid = d_resid * attn_gain
        d_proj = (attn_rms * (scaled_resid - proj * attn_rms * attn_rms * lax.optimization_barrier(jnp.mean(scaled_resid * proj, axis=-1, keepdims=True)))).astype(jnp.bfloat16)
        output_term = jnp.dot(d_proj.T, attn, preferred_element_type=jnp.float32)
        d_attn = jnp.dot(d_proj, w_output, preferred_element_type=jnp.float32).astype(jnp.bfloat16)
        d_attn_heads = widen(d_attn).reshape(SEQ, H, HD)
        attn_heads = widen(attn).reshape(SEQ, H, HD)
        back_prob = jnp.where(visible[None], jnp.exp(scores - log_total), 0.0)
        back_bf = back_prob.astype(jnp.bfloat16)
        d_value = jnp.einsum('hqk,qhd->khd', widen(back_bf), d_attn_heads).reshape(SEQ, D).astype(jnp.bfloat16)
        d_prob = jnp.einsum('qhd,khd->hqk', d_attn_heads, value_heads)
        delta = jnp.einsum('qhd,qhd->hq', d_attn_heads, attn_heads)[..., None]
        d_score = (back_prob * (d_prob - delta)).astype(jnp.bfloat16)
        d_nq = jnp.einsum('hqk,khd->qhd', widen(d_score), key_heads).reshape(SEQ, D) * score_scale
        d_nk = jnp.einsum('hqk,qhd->khd', widen(d_score), query_heads).reshape(SEQ, D) * score_scale
        query_gain_term = lax.optimization_barrier(jnp.sum(d_nq * query * q_rms, axis=0))
        key_gain_term = lax.optimization_barrier(jnp.sum(d_nk * key_proj * k_rms, axis=0))
        scaled_q = d_nq * query_gain
        scaled_k = d_nk * key_gain
        d_query = (q_rms * (scaled_q - query * q_rms * q_rms * lax.optimization_barrier(jnp.mean(scaled_q * query, axis=-1, keepdims=True)))).astype(jnp.bfloat16)
        d_key = (k_rms * (scaled_k - key_proj * k_rms * k_rms * lax.optimization_barrier(jnp.mean(scaled_k * key_proj, axis=-1, keepdims=True)))).astype(jnp.bfloat16)
        query_term = jnp.dot(seq_x.T, d_query, preferred_element_type=jnp.float32)
        key_term = jnp.dot(seq_x.T, d_key, preferred_element_type=jnp.float32)
        value_term = jnp.dot(seq_x.T, d_value, preferred_element_type=jnp.float32)
        back_input = jnp.dot(d_query, w_query.T, preferred_element_type=jnp.float32) + jnp.dot(d_key, w_key.T, preferred_element_type=jnp.float32) + jnp.dot(d_value, w_value.T, preferred_element_type=jnp.float32)
        grad_input = d_resid + back_input
        terms = (query_term, key_term, value_term, output_term, gate_term, up_term, down_term, query_gain_term, key_gain_term, attn_gain_term, ffn_gain_term)
        totals = tuple((total_now + term for total_now, term in zip(totals, terms)))
        return (totals, (output, grad_input))
    square_zero = jnp.zeros((D, D), jnp.float32)
    wide_zero = jnp.zeros((D, FF), jnp.float32)
    gain_zero = jnp.zeros((D,), jnp.float32)
    initial = (square_zero, square_zero, square_zero, square_zero, wide_zero, wide_zero, wide_zero, gain_zero, gain_zero, gain_zero, gain_zero)
    totals, (outputs, grad_inputs) = lax.scan(one_sequence, initial, (seq_tokens, segment_ids, seq_cotangent))
    return (outputs.reshape(TOKENS, D), grad_inputs.reshape(TOKENS, D), totals[0], totals[1], totals[2], totals[3], totals[4], totals[5], totals[6], totals[7], totals[8], totals[9], totals[10])
```

```python
import math

import jax
import jax.numpy as jnp
from jax import lax
from jax.sharding import Mesh, PartitionSpec as P

HD = 128

EPSILON = 1e-06
NEGATIVE = -1e30
FLIP = [(0, 1), (1, 0)]
BF = jnp.bfloat16
F32 = jnp.float32


def swap(value, axis):
    return lax.ppermute(value, axis, FLIP)


def bit(axis):
    return lax.axis_index(axis)


def pick(axis, low, high):
    return jnp.where(bit(axis) == 0, low, high)


def ordered(axis, own, other, dim=0):
    return jnp.concatenate([pick(axis, own, other), pick(axis, other, own)], axis=dim)


def split(value, axis, dim):
    half = value.shape[dim] // 2
    low = lax.slice_in_dim(value, 0, half, axis=dim)
    high = lax.slice_in_dim(value, half, 2 * half, axis=dim)
    return pick(axis, low, high), pick(axis, high, low)


def dot(a, b):
    return jnp.dot(a, b, preferred_element_type=F32)


def dot_nt(a, b):
    return jnp.einsum("sc,rc->sr", a, b, preferred_element_type=F32)


def dot_tn(a, b):
    return jnp.einsum("sr,sc->rc", a, b, preferred_element_type=F32)


def rms_scale(values):
    return lax.rsqrt(jnp.mean(values * values, axis=1, keepdims=True) + EPSILON)


def build(high_bits):
    def to_relative(value):
        rows, width = value.shape
        count = 2 ** (len(high_bits) + 2)
        run = width // count
        pieces = [value[:, i * run : (i + 1) * run] for i in range(count)]
        names = list(high_bits) + ["zl", "x"]
        for position, name in enumerate(names):
            if name == "zl":
                continue
            mask = 1 << (len(names) - 1 - position)
            pieces = [pick(name, pieces[i], pieces[i ^ mask]) for i in range(count)]
        order = []
        for xr in range(2):
            for rest in range(count // 2):
                order.append(rest * 2 + xr)
        return jnp.concatenate([pieces[i] for i in order], axis=1)

    def to_natural(value):
        rows, width = value.shape
        count = 2 ** (len(high_bits) + 2)
        run = width // count
        moved = [value[:, i * run : (i + 1) * run] for i in range(count)]
        pieces = [None] * count
        place = 0
        for xr in range(2):
            for rest in range(count // 2):
                pieces[rest * 2 + xr] = moved[place]
                place += 1
        names = list(high_bits) + ["zl", "x"]
        for position, name in enumerate(names):
            if name == "zl":
                continue
            mask = 1 << (len(names) - 1 - position)
            pieces = [pick(name, pieces[i], pieces[i ^ mask]) for i in range(count)]
        return jnp.concatenate(pieces, axis=1)

    def gather_attn_weight(w):
        own, sent = split(w, "core", 1)
        rows = ordered("core", own, swap(sent, "core"))
        for name in high_bits[::-1]:
            rows = jnp.concatenate([rows, swap(rows, name)], axis=0)
        blocks = 2 ** len(high_bits)
        run = rows.shape[0] // blocks
        other = swap(rows, "zl")
        parts = []
        for b in range(blocks):
            parts.append(ordered("zl", rows[b * run : (b + 1) * run], other[b * run : (b + 1) * run]))
        rows = jnp.concatenate(parts, axis=0)
        return rows, swap(rows, "x")

    def gather_ffn_weight(w):
        own, sent = split(w, "core", 1)
        rows = ordered("core", own, swap(sent, "core"))
        own, sent = split(rows, "zl", 1)
        rows = ordered("zl", own, swap(sent, "zl"))
        for name in high_bits[::-1]:
            rows = jnp.concatenate([rows, swap(rows, name)], axis=0)
        return rows, swap(rows, "x")

    def scatter_high(total):
        for name in high_bits:
            half = total.shape[0] // 2
            total = total[:half] + swap(total[half:].astype(BF), name).astype(F32)
        return total

    def scatter_attn_grad(keep, send):
        total = keep + swap(send.astype(BF), "x").astype(F32)
        blocks = 2 ** len(high_bits)
        run = total.shape[0] // blocks
        pairs = [split(total[b * run : (b + 1) * run], "zl", 0) for b in range(blocks)]
        own = jnp.concatenate([p[0] for p in pairs], axis=0)
        sent = jnp.concatenate([p[1] for p in pairs], axis=0)
        total = own + swap(sent.astype(BF), "zl").astype(F32)
        total = scatter_high(total)
        own, sent = split(total, "core", 0)
        return ordered("core", own, swap(sent, "core"), dim=1)

    def scatter_ffn_grad(keep, send):
        total = keep + swap(send.astype(BF), "x").astype(F32)
        total = scatter_high(total)
        own, sent = split(total, "zl", 0)
        total = ordered("zl", own, swap(sent.astype(BF), "zl").astype(F32), dim=1)
        own, sent = split(total, "core", 0)
        return ordered("core", own, swap(sent.astype(BF), "core").astype(F32), dim=1)

    def gather_pair(value):
        value = ordered("tensor", value, swap(value, "tensor"))
        return jnp.concatenate([value, swap(value, "core")], axis=0)

    def scatter_pair(low, high):
        total = low + swap(high.astype(BF), "core").astype(F32)
        own, sent = split(total, "tensor", 0)
        return own + swap(sent.astype(BF), "tensor").astype(F32)

    def gather_ffn_rows(value):
        half = value.shape[1] // 2
        left, right = value[:, :half], value[:, half:]
        left = jnp.concatenate([left, swap(left, "tensor")], axis=0)
        left = jnp.concatenate([left, swap(left, "zl")], axis=0)
        rows = right.shape[0]
        right = jnp.concatenate([right, swap(right, "zl")], axis=0)
        right_other = swap(right, "tensor")
        right = jnp.concatenate(
            [right[:rows], right_other[:rows], right[rows:], right_other[rows:]], axis=0
        )
        both = jnp.concatenate([left, right], axis=1)
        return jnp.concatenate([both, swap(both, "core")], axis=0)

    def scatter_ffn_rows(low, high):
        quarter = low.shape[0] // 2
        left = low[:quarter] + swap(low[quarter:].astype(BF), "core").astype(F32)
        right = high[:quarter] + swap(high[quarter:].astype(BF), "core").astype(F32)
        half = quarter // 2
        left = left[:half] + swap(left[half:].astype(BF), "zl").astype(F32)
        half = half // 2
        left = left[:half] + swap(left[half:].astype(BF), "tensor").astype(F32)
        own = jnp.concatenate([right[:half], right[2 * half : 3 * half]], axis=0)
        sent = jnp.concatenate([right[half : 2 * half], right[3 * half :]], axis=0)
        right = own + swap(sent.astype(BF), "tensor").astype(F32)
        right = right[:half] + swap(right[half:].astype(BF), "zl").astype(F32)
        return jnp.concatenate([left, right], axis=1)

    def pair_sum(values):
        half = values.shape[1] // 2
        other = swap(values, "core")
        values = values + jnp.concatenate([other[:, half:], other[:, :half]], axis=1)
        return values + swap(values, "tensor")

    def gather_gains(gains):
        gains = ordered("tensor", gains, swap(gains, "tensor"), dim=1)
        gains = ordered("core", gains, swap(gains, "core"), dim=1)
        gains = ordered("zl", gains, swap(gains, "zl"), dim=1)
        for name in list(high_bits)[::-1] + ["x"]:
            gains = jnp.concatenate([gains, swap(gains, name)], axis=1)
        return gains

    def scatter_gains(gains):
        for name in ["x"] + list(high_bits):
            half = gains.shape[1] // 2
            gains = gains[:, :half] + swap(gains[:, half:], name)
        for name in ("zl", "core", "tensor"):
            own, sent = split(gains, name, 1)
            gains = own + swap(sent, name)
        return gains

    def shards(
        tokens,
        segment_ids,
        w_query,
        w_key,
        w_value,
        w_output,
        w_gate,
        w_up,
        w_down,
        query_gain,
        key_gain,
        attn_gain,
        ffn_gain,
        cotangent,
    ):
        own_tokens, model_width = tokens.shape
        half_width = model_width // 2
        seq_length = own_tokens * 2
        pair_tokens = seq_length * 2
        head_width = w_query.shape[1] // 2
        local_heads = head_width // HD
        score_scale = 1.0 / math.sqrt(HD)

        tokens_rel = to_relative(tokens)
        tokens_f = tokens_rel.astype(F32)
        whole_input = gather_pair(tokens_rel)
        wq0, wq1 = gather_attn_weight(w_query)
        wk0, wk1 = gather_attn_weight(w_key)
        wv0, wv1 = gather_attn_weight(w_value)
        wo0, wo1 = gather_attn_weight(w_output)
        wg0, wg1 = gather_ffn_weight(w_gate)
        wu0, wu1 = gather_ffn_weight(w_up)
        wd0, wd1 = gather_ffn_weight(w_down)
        gains = gather_gains(jnp.stack([query_gain, key_gain, attn_gain, ffn_gain]))
        attn_scale = gains[2]
        ffn_scale = gains[3]
        head_gains = to_natural(gains[:2])
        head_start = (bit("tensor") * 2 + bit("core")) * head_width
        head_gains = lax.dynamic_slice_in_dim(head_gains, head_start, head_width, axis=1)
        query_scale, key_scale = head_gains[0], head_gains[1]
        d_out = to_relative(cotangent).astype(F32)

        seq_ids = jnp.concatenate([segment_ids, swap(segment_ids, "core")], axis=0)
        positions = jnp.arange(seq_length)
        visible = (positions[:, None] >= positions[None, :])[None] & (
            seq_ids[:, :, None] == seq_ids[:, None, :]
        )
        visible = visible[:, None]

        in0, in1 = whole_input[:, :half_width], whole_input[:, half_width:]
        query = dot(in0, wq0) + dot(in1, wq1)
        key_proj = dot(in0, wk0) + dot(in1, wk1)
        value_bf = (dot(in0, wv0) + dot(in1, wv1)).astype(BF)
        squares = pair_sum(
            jnp.stack([jnp.sum(query * query, axis=1), jnp.sum(key_proj * key_proj, axis=1)])
        )
        q_rms = lax.rsqrt(squares[0] / model_width + EPSILON)[:, None]
        k_rms = lax.rsqrt(squares[1] / model_width + EPSILON)[:, None]
        normed_query = (query * q_rms * query_scale).astype(BF)
        normed_key = (key_proj * k_rms * key_scale).astype(BF)
        heads = (2, seq_length, local_heads, HD)
        query_heads = normed_query.reshape(heads)
        key_heads = normed_key.reshape(heads)
        value_heads = value_bf.reshape(heads)
        scores = (
            jnp.einsum("bqhd,bkhd->bhqk", query_heads, key_heads, preferred_element_type=F32)
            * score_scale
        )
        scores = jnp.where(visible, scores, NEGATIVE)
        peak = jnp.max(scores, axis=-1, keepdims=True)
        expo = jnp.exp(scores - peak)
        total = jnp.sum(expo, axis=-1, keepdims=True)
        prob = expo / total
        prob_bf = prob.astype(BF)
        attn_heads = jnp.einsum(
            "bhqk,bkhd->bqhd", prob_bf, value_heads, preferred_element_type=F32
        ).astype(BF)
        attn = attn_heads.reshape(pair_tokens, head_width)

        def out_proj(rows, w0, w1):
            return jnp.concatenate([dot_nt(rows, w0), dot_nt(rows, w1)], axis=1)

        proj = scatter_pair(
            out_proj(attn[:seq_length], wo0, wo1), out_proj(attn[seq_length:], wo0, wo1)
        )
        attn_rms = rms_scale(proj)
        resid = tokens_f + proj * attn_rms * attn_scale
        hidden = gather_ffn_rows(resid.astype(BF))
        h0, h1 = hidden[:, :half_width], hidden[:, half_width:]
        gate = dot(h0, wg0) + dot(h1, wg1)
        up = dot(h0, wu0) + dot(h1, wu1)
        sigma = jax.nn.sigmoid(gate)
        act = (gate * sigma * up).astype(BF)
        ffn = scatter_ffn_rows(dot_nt(act, wd0), dot_nt(act, wd1))
        ffn_rms = rms_scale(ffn)
        output = to_natural((resid + ffn * ffn_rms * ffn_scale).astype(BF))
        ffn_gain_term = jnp.sum(d_out * ffn * ffn_rms, axis=0)
        scaled_out = d_out * ffn_scale
        d_ffn = (
            ffn_rms
            * (
                scaled_out
                - ffn * ffn_rms * ffn_rms * jnp.mean(scaled_out * ffn, axis=1, keepdims=True)
            )
        ).astype(BF)
        whole_dffn = gather_ffn_rows(d_ffn)
        f0, f1 = whole_dffn[:, :half_width], whole_dffn[:, half_width:]
        grad_down = scatter_ffn_grad(dot_tn(f0, act), dot_tn(f1, act))
        d_act = dot(f0, wd0) + dot(f1, wd1)
        d_gate = (d_act * up * sigma * (1.0 + gate * (1.0 - sigma))).astype(BF)
        d_up = (d_act * gate * sigma).astype(BF)
        d_hidden = scatter_ffn_rows(
            dot_nt(d_gate, wg0) + dot_nt(d_up, wu0), dot_nt(d_gate, wg1) + dot_nt(d_up, wu1)
        )
        grad_gate = scatter_ffn_grad(dot_tn(h0, d_gate), dot_tn(h1, d_gate))
        grad_up = scatter_ffn_grad(dot_tn(h0, d_up), dot_tn(h1, d_up))
        d_resid = d_out + d_hidden
        attn_gain_term = jnp.sum(d_resid * proj * attn_rms, axis=0)
        scaled_resid = d_resid * attn_scale
        d_proj = (
            attn_rms
            * (
                scaled_resid
                - proj * attn_rms * attn_rms * jnp.mean(scaled_resid * proj, axis=1, keepdims=True)
            )
        ).astype(BF)
        whole_dproj = gather_pair(d_proj)
        p0, p1 = whole_dproj[:, :half_width], whole_dproj[:, half_width:]
        d_attn = (dot(p0, wo0) + dot(p1, wo1)).astype(BF)
        grad_output = scatter_attn_grad(dot_tn(p0, attn), dot_tn(p1, attn))
        d_attn_heads = d_attn.reshape(heads)
        d_value = (
            jnp.einsum("bhqk,bqhd->bkhd", prob_bf, d_attn_heads, preferred_element_type=F32)
            .reshape(pair_tokens, head_width)
            .astype(BF)
        )
        grad_value = scatter_attn_grad(dot_tn(in0, d_value), dot_tn(in1, d_value))
        d_prob = jnp.einsum(
            "bqhd,bkhd->bhqk", d_attn_heads, value_heads, preferred_element_type=F32
        )
        delta = jnp.einsum(
            "bqhd,bqhd->bhq", d_attn_heads, attn_heads, preferred_element_type=F32
        )[..., None]
        d_score = (prob * (d_prob - delta)).astype(BF)
        d_nq = (
            jnp.einsum("bhqk,bkhd->bqhd", d_score, key_heads, preferred_element_type=F32).reshape(
                pair_tokens, head_width
            )
            * score_scale
        )
        d_nk = (
            jnp.einsum("bhqk,bqhd->bkhd", d_score, query_heads, preferred_element_type=F32).reshape(
                pair_tokens, head_width
            )
            * score_scale
        )
        query_gain_term = jnp.sum(d_nq * query * q_rms, axis=0)
        key_gain_term = jnp.sum(d_nk * key_proj * k_rms, axis=0)
        scaled_q = d_nq * query_scale
        scaled_k = d_nk * key_scale
        inner = pair_sum(
            jnp.stack([jnp.sum(scaled_q * query, axis=1), jnp.sum(scaled_k * key_proj, axis=1)])
        )
        d_query = (
            q_rms * (scaled_q - query * q_rms * q_rms * (inner[0] / model_width)[:, None])
        ).astype(BF)
        d_key = (
            k_rms * (scaled_k - key_proj * k_rms * k_rms * (inner[1] / model_width)[:, None])
        ).astype(BF)
        grad_query = scatter_attn_grad(dot_tn(in0, d_query), dot_tn(in1, d_query))
        grad_key = scatter_attn_grad(dot_tn(in0, d_key), dot_tn(in1, d_key))

        def in_proj(rows):
            return jnp.concatenate(
                [
                    dot_nt(d_query[rows], wq) + dot_nt(d_key[rows], wk) + dot_nt(d_value[rows], wv)
                    for wq, wk, wv in ((wq0, wk0, wv0), (wq1, wk1, wv1))
                ],
                axis=1,
            )

        d_tokens = scatter_pair(
            in_proj(slice(0, seq_length)), in_proj(slice(seq_length, pair_tokens))
        )
        grad_tokens = to_natural(d_resid + d_tokens)

        zero = jnp.zeros((2, model_width), F32)
        placed = lax.dynamic_update_slice_in_dim(
            zero, jnp.stack([query_gain_term, key_gain_term]), head_start, 1
        )
        gain_parts = scatter_gains(
            jnp.concatenate(
                [to_relative(placed), jnp.stack([attn_gain_term, ffn_gain_term])], axis=0
            )
        )
        return (
            output,
            grad_tokens,
            grad_query,
            grad_key,
            grad_value,
            grad_output,
            grad_gate,
            grad_up,
            grad_down,
            gain_parts[0],
            gain_parts[1],
            gain_parts[2],
            gain_parts[3],
        )

    return shards


def solution(mesh):
    dp = mesh.shape["dp"]
    high = max(dp.bit_length() - 4, 0)
    high_bits = tuple(f"z{i}" for i in range(high))
    names = high_bits + ("zl", "x", "core", "tensor")
    fine = Mesh(mesh.devices.reshape((2,) * len(names)), names)
    rows = names[:-1]
    both = names
    mapped = jax.shard_map(
        build(high_bits),
        mesh=fine,
        in_specs=(
            P(both, None),
            P(rows, None),
            P(rows, "tensor"),
            P(rows, "tensor"),
            P(rows, "tensor"),
            P(rows, "tensor"),
            P(rows, "tensor"),
            P(rows, "tensor"),
            P(rows, "tensor"),
            P(both),
            P(both),
            P(both),
            P(both),
            P(both, None),
        ),
        out_specs=(
            P(both, None),
            P(both, None),
            P(rows, "tensor"),
            P(rows, "tensor"),
            P(rows, "tensor"),
            P(rows, "tensor"),
            P(rows, "tensor"),
            P(rows, "tensor"),
            P(rows, "tensor"),
            P(both),
            P(both),
            P(both),
            P(both),
        ),
        check_vma=False,
    )
    return mapped
```

```python
import math

import jax
import jax.numpy as jnp
from jax import lax
from jax.sharding import Mesh, PartitionSpec as P

HD = 128

EPSILON = 1e-06
NEGATIVE = -1e30
FLIP = [(0, 1), (1, 0)]
BF = jnp.bfloat16
F32 = jnp.float32


def swap(value, axis):
    return lax.ppermute(value, axis, FLIP)


def bit(axis):
    return lax.axis_index(axis)


def pick(axis, low, high):
    return jnp.where(bit(axis) == 0, low, high)


def ordered(axis, own, other, dim=0):
    return jnp.concatenate([pick(axis, own, other), pick(axis, other, own)], axis=dim)


def split(value, axis, dim):
    half = value.shape[dim] // 2
    low = lax.slice_in_dim(value, 0, half, axis=dim)
    high = lax.slice_in_dim(value, half, 2 * half, axis=dim)
    return pick(axis, low, high), pick(axis, high, low)


def dot(a, b):
    return jnp.dot(a, b, preferred_element_type=F32)


def dot_nt(a, b):
    return jnp.einsum("sc,rc->sr", a, b, preferred_element_type=F32)


def dot_tn(a, b):
    return jnp.einsum("sr,sc->rc", a, b, preferred_element_type=F32)


def rms_scale(values):
    return lax.rsqrt(jnp.mean(values * values, axis=1, keepdims=True) + EPSILON)


def build(high_bits):
    def to_relative(value):
        rows, width = value.shape
        count = 2 ** (len(high_bits) + 2)
        run = width // count
        pieces = [value[:, i * run : (i + 1) * run] for i in range(count)]
        names = list(high_bits) + ["zl", "x"]
        for position, name in enumerate(names):
            if name == "zl":
                continue
            mask = 1 << (len(names) - 1 - position)
            pieces = [pick(name, pieces[i], pieces[i ^ mask]) for i in range(count)]
        order = []
        for xr in range(2):
            for rest in range(count // 2):
                order.append(rest * 2 + xr)
        return jnp.concatenate([pieces[i] for i in order], axis=1)

    def to_natural(value):
        rows, width = value.shape
        count = 2 ** (len(high_bits) + 2)
        run = width // count
        moved = [value[:, i * run : (i + 1) * run] for i in range(count)]
        pieces = [None] * count
        place = 0
        for xr in range(2):
            for rest in range(count // 2):
                pieces[rest * 2 + xr] = moved[place]
                place += 1
        names = list(high_bits) + ["zl", "x"]
        for position, name in enumerate(names):
            if name == "zl":
                continue
            mask = 1 << (len(names) - 1 - position)
            pieces = [pick(name, pieces[i], pieces[i ^ mask]) for i in range(count)]
        return jnp.concatenate(pieces, axis=1)

    class Chain:
        def __init__(self, token):
            self.token = token

        def sync(self, *values):
            out = lax.optimization_barrier((self.token,) + values)
            self.token = out[0]
            return out[1] if len(values) == 1 else out[1:]

        def start(self, value, axis):
            return swap(self.sync(value), axis)

        def start_high(self, rows):
            for name in high_bits[:0:-1]:
                rows = jnp.concatenate([rows, self.sync(self.start(rows, name))], axis=0)
            return rows, (self.start(rows, high_bits[0]) if high_bits else None)

        def end_high(self, pending):
            rows, sent = pending
            return rows if sent is None else jnp.concatenate([rows, self.sync(sent)], axis=0)

        def start_high_sum(self, total):
            for name in high_bits[:-1]:
                half = total.shape[0] // 2
                total = total[:half] + self.sync(self.start(total[half:].astype(BF), name)).astype(F32)
            if not high_bits:
                return total, None
            half = total.shape[0] // 2
            return total[:half], self.start(total[half:].astype(BF), high_bits[-1])

        def end_high_sum(self, pending):
            total, sent = pending
            return total if sent is None else total + self.sync(sent).astype(F32)

    high_blocks = 2 ** len(high_bits)

    def split_lines(rows, outer):
        run = rows.shape[0] // outer
        pairs = [split(rows[b * run : (b + 1) * run], "zl", 0) for b in range(outer)]
        if outer == 1:
            return pairs[0]
        return tuple(jnp.concatenate([p[i] for p in pairs], axis=0) for i in range(2))

    def join_lines(own, other, outer):
        run = own.shape[0] // outer
        parts = [
            ordered("zl", own[b * run : (b + 1) * run], other[b * run : (b + 1) * run])
            for b in range(outer)
        ]
        return parts[0] if outer == 1 else jnp.concatenate(parts, axis=0)

    def gather_gains(c, gains):
        gains = ordered("tensor", gains, c.sync(c.start(gains, "tensor")), dim=1)
        gains = ordered("core", gains, c.sync(c.start(gains, "core")), dim=1)
        gains = ordered("zl", gains, c.sync(c.start(gains, "zl")), dim=1)
        for name in list(high_bits)[::-1] + ["x"]:
            gains = jnp.concatenate([gains, c.sync(c.start(gains, name))], axis=1)
        return gains

    def pair_sum(c, values):
        half = values.shape[1] // 2
        other = c.sync(c.start(values, "core"))
        values = values + jnp.concatenate([other[:, half:], other[:, :half]], axis=1)
        return values + c.sync(c.start(values, "tensor"))

    def scatter_gains(c, gains):
        for name in ["x"] + list(high_bits):
            half = gains.shape[1] // 2
            gains = gains[:, :half] + c.sync(c.start(gains[:, half:], name))
        for name in ("zl", "core", "tensor"):
            own, sent = split(gains, name, 1)
            gains = own + c.sync(c.start(sent, name))
        return gains

    def stack2(low, high):
        return jnp.concatenate([low, high], axis=0)

    def shards(
        tokens,
        segment_ids,
        w_query,
        w_key,
        w_value,
        w_output,
        w_gate,
        w_up,
        w_down,
        query_gain,
        key_gain,
        attn_gain,
        ffn_gain,
        cotangent,
    ):
        own_tokens, model_width = tokens.shape
        half_width = model_width // 2
        seq_length = own_tokens * 2
        pair_tokens = seq_length * 2
        head_width = w_query.shape[1] // 2
        ffn_width = w_gate.shape[1] // 4
        local_heads = head_width // HD
        score_scale = 1.0 / math.sqrt(HD)
        c = Chain(query_gain)

        attn_split = [split(w, "core", 1) for w in (w_query, w_key, w_value, w_output)]
        attn_sent = c.start(jnp.concatenate([s[1] for s in attn_split], axis=1), "core")
        tokens_rel = to_relative(tokens)
        tokens_sent = c.start(tokens_rel, "tensor")
        ffn_split = [split(w, "core", 1) for w in (w_gate, w_up, w_down)]
        ffn_sent = c.start(jnp.concatenate([s[1] for s in ffn_split], axis=1), "core")

        attn_sent = c.sync(attn_sent)
        q_rows, k_rows, v_rows, o_rows = [
            ordered("core", s[0], attn_sent[:, i * head_width : (i + 1) * head_width])
            for i, s in enumerate(attn_split)
        ]
        k_high = c.start_high(k_rows)
        q_x = c.start(q_rows, "x")
        ffn_sent = c.sync(ffn_sent)
        g_rows, u_rows, d_rows = [
            split(
                ordered("core", s[0], ffn_sent[:, i * 2 * ffn_width : (i + 1) * 2 * ffn_width]),
                "zl",
                1,
            )
            for i, s in enumerate(ffn_split)
        ]
        g_line = c.start(g_rows[1], "zl")
        q_x = c.sync(q_x)
        q_rows2 = jnp.concatenate([q_rows, q_x], axis=1)
        segments_other = swap(segment_ids, "core")
        gains = gather_gains(c, jnp.stack([query_gain, key_gain, attn_gain, ffn_gain]))
        tokens_sent = c.sync(tokens_sent)
        own_seq = ordered("tensor", tokens_rel, tokens_sent)
        tokens_sent = c.start(own_seq, "core")
        k_rows = c.end_high(k_high)
        v_high = c.start_high(v_rows)
        g_rows = ordered("zl", g_rows[0], c.sync(g_line))
        k_line = c.start(k_rows, "zl")
        whole_input = stack2(own_seq, c.sync(tokens_sent))
        k_rows = join_lines(k_rows, c.sync(k_line), high_blocks)
        k_x = c.start(k_rows, "x")
        v_rows = c.end_high(v_high)
        q_high = c.start_high(q_rows2)
        v_line = c.start(v_rows, "zl")
        v_rows = join_lines(v_rows, c.sync(v_line), high_blocks)
        u_line = c.start(u_rows[1], "zl")

        attn_scale = gains[2]
        ffn_scale = gains[3]
        head_gains = to_natural(gains[:2])
        head_start = (bit("tensor") * 2 + bit("core")) * head_width
        head_gains = lax.dynamic_slice_in_dim(head_gains, head_start, head_width, axis=1)
        query_scale, key_scale = head_gains[0], head_gains[1]
        tokens_f = tokens_rel.astype(F32)
        d_out = to_relative(cotangent).astype(F32)
        seq_ids = stack2(segment_ids, segments_other)
        positions = jnp.arange(seq_length)
        visible = (positions[:, None] >= positions[None, :])[None] & (
            seq_ids[:, :, None] == seq_ids[:, None, :]
        )
        visible = visible[:, None]
        in0, in1 = whole_input[:, :half_width], whole_input[:, half_width:]

        k_x = c.sync(k_x)
        v_x = c.start(v_rows, "x")
        key_proj = dot(in0, k_rows) + dot(in1, k_x)
        q_rows2 = c.end_high(q_high)
        u_rows = ordered("zl", u_rows[0], c.sync(u_line))
        q_line = c.start(q_rows2, "zl")
        o_high = c.start_high(o_rows)
        o_rows = c.end_high(o_high)
        g_high = c.start_high(g_rows)
        q_rows2 = join_lines(q_rows2, c.sync(q_line), high_blocks)
        o_line = c.start(o_rows, "zl")
        wq0, wq1 = q_rows2[:, :head_width], q_rows2[:, head_width:]
        query = dot(in0, wq0) + dot(in1, wq1)
        v_x = c.sync(v_x)
        wk0, wk1, wv0, wv1 = k_rows, k_x, v_rows, v_x
        value_bf = (dot(in0, wv0) + dot(in1, wv1)).astype(BF)
        squares = pair_sum(
            c, jnp.stack([jnp.sum(query * query, axis=1), jnp.sum(key_proj * key_proj, axis=1)])
        )
        o_rows = join_lines(o_rows, c.sync(o_line), high_blocks)
        o_x = c.start(o_rows, "x")
        d_line = c.start(d_rows[1], "zl")
        q_rms = lax.rsqrt(squares[0] / model_width + EPSILON)[:, None]
        k_rms = lax.rsqrt(squares[1] / model_width + EPSILON)[:, None]
        normed_query = (query * q_rms * query_scale).astype(BF)
        normed_key = (key_proj * k_rms * key_scale).astype(BF)
        heads = (2, seq_length, local_heads, HD)
        query_heads = normed_query.reshape(heads)
        key_heads = normed_key.reshape(heads)
        value_heads = value_bf.reshape(heads)
        scores = (
            jnp.einsum("bqhd,bkhd->bhqk", query_heads, key_heads, preferred_element_type=F32)
            * score_scale
        )
        scores = jnp.where(visible, scores, NEGATIVE)
        peak = jnp.max(scores, axis=-1, keepdims=True)
        expo = jnp.exp(scores - peak)
        total = jnp.sum(expo, axis=-1, keepdims=True)
        prob = expo / total
        prob_bf = prob.astype(BF)
        attn_heads = jnp.einsum(
            "bhqk,bkhd->bqhd", prob_bf, value_heads, preferred_element_type=F32
        ).astype(BF)
        attn = c.sync(attn_heads.reshape(pair_tokens, head_width))
        d_rows = ordered("zl", d_rows[0], c.sync(d_line))
        o_x = c.sync(o_x)
        wo0, wo1 = o_rows, o_x
        g_rows = c.end_high(g_high)
        g_x = c.start(g_rows, "x")
        u_high = c.start_high(u_rows)

        def columns(parts):
            return jnp.concatenate(parts, axis=1)

        def scatter_pair(low, high):
            sent = c.start(high().astype(BF), "core")
            total = low() + c.sync(sent).astype(F32)
            own, sent = split(total, "tensor", 0)
            return own + c.sync(c.start(sent.astype(BF), "tensor")).astype(F32)

        def out_proj(rows):
            return columns([dot_nt(rows, wo0), dot_nt(rows, wo1)])

        proj = scatter_pair(
            lambda: out_proj(attn[:seq_length]), lambda: out_proj(attn[seq_length:])
        )
        attn_rms = rms_scale(proj)
        resid = tokens_f + proj * attn_rms * attn_scale

        def gather_rows(value):
            left, right = value[:, :half_width], value[:, half_width:]
            left_sent = c.start(left, "tensor")
            right_sent = c.start(right, "zl")
            left = stack2(left, c.sync(left_sent))
            right = stack2(right, c.sync(right_sent))
            left_sent = c.start(left, "zl")
            right_sent = c.start(right, "tensor")
            left = stack2(left, c.sync(left_sent))
            right_sent = c.sync(right_sent)
            rows = own_tokens
            right = jnp.concatenate(
                [right[:rows], right_sent[:rows], right[rows:], right_sent[rows:]], axis=0
            )
            left_sent = c.start(left, "core")
            right_sent = c.start(right, "core")
            return left, right, left_sent, right_sent

        h0a, h1a, h0b, h1b = gather_rows(resid.astype(BF))
        h0b, h1b = c.sync(h0b, h1b)
        g_x = c.sync(g_x)
        u_rows = c.end_high(u_high)
        u_x = c.start(u_rows, "x")
        d_high = c.start_high(d_rows)
        wg0, wg1, wu0 = g_rows, g_x, u_rows
        gate_a = dot(h0a, wg0) + dot(h1a, wg1)
        gate_b = dot(h0b, wg0) + dot(h1b, wg1)
        gate_a, gate_b = c.sync(gate_a, gate_b)
        wd0 = c.end_high(d_high)
        wu1 = c.sync(u_x)
        d_x = c.start(wd0, "x")
        up_a = dot(h0a, wu0) + dot(h1a, wu1)
        up_b = dot(h0b, wu0) + dot(h1b, wu1)
        sigma_a, sigma_b = jax.nn.sigmoid(gate_a), jax.nn.sigmoid(gate_b)
        act_a = (gate_a * sigma_a * up_a).astype(BF)
        act_b = (gate_b * sigma_b * up_b).astype(BF)

        def halve(total, axis):
            half = total.shape[0] // 2
            return total[:half], c.start(total[half:].astype(BF), axis)

        def added(pair):
            return pair[0] + c.sync(pair[1]).astype(F32)

        def cross(total):
            rows = own_tokens
            own = stack2(total[:rows], total[2 * rows : 3 * rows])
            sent = stack2(total[rows : 2 * rows], total[3 * rows :])
            return own, c.start(sent.astype(BF), "tensor")

        left_sent = c.start(dot_nt(act_b, wd0).astype(BF), "core")
        left = dot_nt(act_a, wd0) + c.sync(left_sent).astype(F32)
        left = added(halve(left, "zl"))
        left = added(halve(left, "tensor"))
        wd1 = c.sync(d_x)
        right_sent = c.start(dot_nt(act_b, wd1).astype(BF), "core")
        right = dot_nt(act_a, wd1) + c.sync(right_sent).astype(F32)
        right = added(cross(right))
        right = added(halve(right, "zl"))
        ffn = columns([left, right])

        ffn_rms = rms_scale(ffn)
        output = to_natural((resid + ffn * ffn_rms * ffn_scale).astype(BF))
        ffn_gain_term = jnp.sum(d_out * ffn * ffn_rms, axis=0)
        scaled_out = d_out * ffn_scale
        d_ffn = (
            ffn_rms
            * (
                scaled_out
                - ffn * ffn_rms * ffn_rms * jnp.mean(scaled_out * ffn, axis=1, keepdims=True)
            )
        ).astype(BF)
        f0a, f1a, f0b, f1b = gather_rows(d_ffn)
        f0b, f1b = c.sync(f0b, f1b)
        part = ffn_width // 2

        class FfnGrad:
            def __init__(self, kept, sent):
                self.kept, self.sent = kept, sent
                self.moving, self.high, self.sums = [None, None], [None, None], [None, None]

            def product(self, pair, i):
                left, right = pair
                cols = slice(i * part, (i + 1) * part)
                return dot_tn(left[0], right[0][:, cols]) + dot_tn(left[1], right[1][:, cols])

            def start_x(self, i):
                self.moving[i] = c.start(self.product(self.sent, i).astype(BF), "x")

            def end_x(self, i):
                moved = c.sync(self.moving[i])
                self.sums[i] = self.product(self.kept, i) + moved.astype(F32)

            def start_high(self, i):
                self.high[i] = c.start_high_sum(self.sums[i])

            def end_high(self, i):
                self.sums[i] = c.end_high_sum(self.high[i])

            def start_line(self):
                self.own, sent = split(columns(self.sums), "zl", 0)
                self.line = c.start(sent.astype(BF), "zl")

            def end_line(self):
                moved = c.sync(self.line).astype(F32)
                total = ordered("zl", self.own, moved, dim=1)
                self.own, sent = split(total, "core", 0)
                self.core = c.start(sent.astype(BF), "core")

            def result(self):
                return ordered("core", self.own, c.sync(self.core).astype(F32), dim=1)

        class AttnGrad:
            def __init__(self, kept, sent, right):
                self.kept, self.sent = kept, sent
                self.right = right

            def start_x(self):
                self.x = c.start(dot_tn(self.sent, self.right).astype(BF), "x")

            def end_x(self):
                moved = c.sync(self.x)
                self.total = dot_tn(self.kept, self.right) + moved.astype(F32)

            def start_line(self):
                self.own, sent = split_lines(self.total, high_blocks)
                self.line = c.start(sent.astype(BF), "zl")

            def end_line(self):
                self.total = self.own + c.sync(self.line).astype(F32)

            def start_high(self):
                self.high = c.start_high_sum(self.total)

            def end_high(self):
                self.total = c.end_high_sum(self.high)

            def start_core(self):
                self.own, sent = split(self.total, "core", 0)
                self.core = c.start(sent.astype(BF), "core")

            def result(self):
                return ordered("core", self.own, c.sync(self.core).astype(F32), dim=1)

        down = FfnGrad(((f0a, f0b), (act_a, act_b)), ((f1a, f1b), (act_a, act_b)))
        down.start_x(0)

        def backward_gate(f0, f1, gate, up, sigma):
            d_act = dot(f0, wd0) + dot(f1, wd1)
            d_gate = (d_act * up * sigma * (1.0 + gate * (1.0 - sigma))).astype(BF)
            return d_gate, (d_act * gate * sigma).astype(BF)

        dg_b, du_b = backward_gate(f0b, f1b, gate_b, up_b, sigma_b)
        left_sent = c.start((dot_nt(dg_b, wg0) + dot_nt(du_b, wu0)).astype(BF), "core")
        right_sent = c.start((dot_nt(dg_b, wg1) + dot_nt(du_b, wu1)).astype(BF), "core")
        dg_a, du_a = backward_gate(f0a, f1a, gate_a, up_a, sigma_a)
        left = dot_nt(dg_a, wg0) + dot_nt(du_a, wu0)
        right = dot_nt(dg_a, wg1) + dot_nt(du_a, wu1)
        left = left + c.sync(left_sent).astype(F32)
        right = right + c.sync(right_sent).astype(F32)
        down.end_x(0)
        down.start_x(1)
        left_pair = halve(left, "zl")
        right_pair = cross(right)
        down.start_high(0)
        left = added(left_pair)
        right = added(right_pair)
        left_pair = halve(left, "tensor")
        right_pair = halve(right, "zl")
        gate_grad = FfnGrad(((h0a, h0b), (dg_a, dg_b)), ((h1a, h1b), (dg_a, dg_b)))
        up_grad = FfnGrad(((h0a, h0b), (du_a, du_b)), ((h1a, h1b), (du_a, du_b)))
        left = added(left_pair)
        right = added(right_pair)
        d_resid = d_out + columns([left, right])
        attn_gain_term = jnp.sum(d_resid * proj * attn_rms, axis=0)
        scaled_resid = d_resid * attn_scale
        d_proj = (
            attn_rms
            * (
                scaled_resid
                - proj * attn_rms * attn_rms * jnp.mean(scaled_resid * proj, axis=1, keepdims=True)
            )
        ).astype(BF)
        dproj_sent = c.start(d_proj, "tensor")
        down.end_high(0)
        down.end_x(1)
        gate_grad.start_x(0)
        down.start_high(1)
        own_dproj = ordered("tensor", d_proj, c.sync(dproj_sent))
        dproj_sent = c.start(own_dproj, "core")
        whole_dproj = stack2(own_dproj, c.sync(dproj_sent))
        p0, p1 = whole_dproj[:, :half_width], whole_dproj[:, half_width:]
        d_attn = (dot(p0, wo0) + dot(p1, wo1)).astype(BF)
        d_attn = c.sync(d_attn)
        gate_grad.end_x(0)
        gate_grad.start_x(1)
        down.end_high(1)
        gate_grad.start_high(0)
        down.start_line()

        d_attn_heads = d_attn.reshape(heads)
        d_value = (
            jnp.einsum("bhqk,bqhd->bkhd", prob_bf, d_attn_heads, preferred_element_type=F32)
            .reshape(pair_tokens, head_width)
            .astype(BF)
        )
        d_prob = jnp.einsum(
            "bqhd,bkhd->bhqk", d_attn_heads, value_heads, preferred_element_type=F32
        )
        delta = jnp.einsum(
            "bqhd,bqhd->bhq", d_attn_heads, attn.reshape(heads), preferred_element_type=F32
        )[..., None]
        d_score = (prob * (d_prob - delta)).astype(BF)
        d_nq = (
            jnp.einsum("bhqk,bkhd->bqhd", d_score, key_heads, preferred_element_type=F32).reshape(
                pair_tokens, head_width
            )
            * score_scale
        )
        d_nk = (
            jnp.einsum("bhqk,bqhd->bkhd", d_score, query_heads, preferred_element_type=F32).reshape(
                pair_tokens, head_width
            )
            * score_scale
        )
        query_gain_term = jnp.sum(d_nq * query * q_rms, axis=0)
        key_gain_term = jnp.sum(d_nk * key_proj * k_rms, axis=0)
        scaled_q = d_nq * query_scale
        scaled_k = d_nk * key_scale
        inner = pair_sum(
            c, jnp.stack([jnp.sum(scaled_q * query, axis=1), jnp.sum(scaled_k * key_proj, axis=1)])
        )
        d_query = (
            q_rms * (scaled_q - query * q_rms * q_rms * (inner[0] / model_width)[:, None])
        ).astype(BF)
        d_key = (
            k_rms * (scaled_k - key_proj * k_rms * k_rms * (inner[1] / model_width)[:, None])
        ).astype(BF)
        query_grad = AttnGrad(in0, in1, d_query)
        key_grad = AttnGrad(in0, in1, d_key)
        value_grad = AttnGrad(in0, in1, d_value)
        output_grad = AttnGrad(p0, p1, attn)

        def in_proj(rows):
            return columns(
                [
                    dot_nt(d_query[rows], wq) + dot_nt(d_key[rows], wk) + dot_nt(d_value[rows], wv)
                    for wq, wk, wv in ((wq0, wk0, wv0), (wq1, wk1, wv1))
                ]
            )

        query_whole = stack2(
            dot_tn(query_grad.kept, query_grad.right), dot_tn(query_grad.sent, query_grad.right)
        )
        query_own, query_sent = split_lines(query_whole, 2 * high_blocks)
        query_line = c.start(query_sent.astype(BF), "zl")
        tok_sent = c.start(in_proj(slice(seq_length, pair_tokens)).astype(BF), "core")
        gate_grad.end_x(1)
        up_grad.start_x(0)
        gate_grad.end_high(0)
        gate_grad.start_high(1)
        total = in_proj(slice(0, seq_length)) + c.sync(tok_sent).astype(F32)
        own, sent = split(total, "tensor", 0)
        tok_sent = c.start(sent.astype(BF), "tensor")
        down.end_line()
        query_total = query_own + c.sync(query_line).astype(F32)
        d_tokens = own + c.sync(tok_sent).astype(F32)
        grad_tokens = to_natural(d_resid + d_tokens)
        grad_down = down.result()
        up_grad.end_x(0)
        up_grad.start_x(1)
        gate_grad.end_high(1)
        up_grad.start_high(0)
        gate_grad.start_line()

        zero = jnp.zeros((2, model_width), F32)
        placed = lax.dynamic_update_slice_in_dim(
            zero, jnp.stack([query_gain_term, key_gain_term]), head_start, 1
        )
        gain_parts = scatter_gains(
            c,
            jnp.concatenate(
                [to_relative(placed), jnp.stack([attn_gain_term, ffn_gain_term])], axis=0
            ),
        )
        gate_grad.end_line()
        grad_gate = gate_grad.result()
        up_grad.end_x(1)
        output_grad.start_x()
        up_grad.end_high(0)
        up_grad.start_high(1)
        output_grad.end_x()
        value_grad.start_x()
        output_grad.start_line()
        up_grad.end_high(1)
        half = query_total.shape[0] // 2
        query_high = [
            c.start_high_sum(
                columns([query_total[:half], query_total[half:]])
            )
        ]
        output_grad.end_line()
        up_grad.start_line()
        up_grad.end_line()
        value_grad.end_x()
        key_grad.start_x()
        value_grad.start_line()
        query_total = c.end_high_sum(query_high[0])
        output_grad.start_high()
        query_x = c.start(query_total[:, head_width:].astype(BF), "x")
        grad_up = up_grad.result()
        value_grad.end_line()
        output_grad.end_high()
        value_grad.start_high()
        output_grad.start_core()
        key_grad.end_x()
        key_grad.start_line()
        query_grad.total = query_total[:, :head_width] + c.sync(query_x).astype(F32)
        query_grad.start_core()
        grad_output = output_grad.result()
        value_grad.end_high()
        value_grad.start_core()
        key_grad.end_line()
        key_grad.start_high()
        grad_query = query_grad.result()
        grad_value = value_grad.result()
        key_grad.end_high()
        key_grad.start_core()
        grad_key = key_grad.result()
        return (
            output,
            grad_tokens,
            grad_query,
            grad_key,
            grad_value,
            grad_output,
            grad_gate,
            grad_up,
            grad_down,
            gain_parts[0],
            gain_parts[1],
            gain_parts[2],
            gain_parts[3],
        )

    return shards


def solution(mesh):
    dp = mesh.shape["dp"]
    high = max(dp.bit_length() - 4, 0)
    high_bits = tuple(f"z{i}" for i in range(high))
    names = high_bits + ("zl", "x", "core", "tensor")
    fine = Mesh(mesh.devices.reshape((2,) * len(names)), names)
    rows = names[:-1]
    both = names
    mapped = jax.shard_map(
        build(high_bits),
        mesh=fine,
        in_specs=(
            P(both, None),
            P(rows, None),
            P(rows, "tensor"),
            P(rows, "tensor"),
            P(rows, "tensor"),
            P(rows, "tensor"),
            P(rows, "tensor"),
            P(rows, "tensor"),
            P(rows, "tensor"),
            P(both),
            P(both),
            P(both),
            P(both),
            P(both, None),
        ),
        out_specs=(
            P(both, None),
            P(both, None),
            P(rows, "tensor"),
            P(rows, "tensor"),
            P(rows, "tensor"),
            P(rows, "tensor"),
            P(rows, "tensor"),
            P(rows, "tensor"),
            P(rows, "tensor"),
            P(both),
            P(both),
            P(both),
            P(both),
        ),
        check_vma=False,
    )
    return mapped
```

```python
import math

import jax
import jax.numpy as jnp
from jax import lax
from jax.sharding import Mesh, PartitionSpec as P

HD = 128

EPSILON = 1e-06
NEGATIVE = -1e30
FLIP = [(0, 1), (1, 0)]
BF = jnp.bfloat16
F32 = jnp.float32


def swap(value, axis):
    return lax.ppermute(value, axis, FLIP)


def bit(axis):
    return lax.axis_index(axis)


def pick(axis, low, high):
    return jnp.where(bit(axis) == 0, low, high)


def ordered(axis, own, other, dim=0):
    return jnp.concatenate([pick(axis, own, other), pick(axis, other, own)], axis=dim)


def split(value, axis, dim):
    half = value.shape[dim] // 2
    low = lax.slice_in_dim(value, 0, half, axis=dim)
    high = lax.slice_in_dim(value, half, 2 * half, axis=dim)
    return pick(axis, low, high), pick(axis, high, low)


def dot(a, b):
    return jnp.dot(a, b, preferred_element_type=F32)


def dot_nt(a, b):
    return jnp.einsum("sc,rc->sr", a, b, preferred_element_type=F32)


def dot_tn(a, b):
    return jnp.einsum("sr,sc->rc", a, b, preferred_element_type=F32)


def rms_scale(values):
    return lax.rsqrt(jnp.mean(values * values, axis=1, keepdims=True) + EPSILON)


def build(high_bits):
    def to_relative(value):
        rows, width = value.shape
        count = 2 ** (len(high_bits) + 2)
        run = width // count
        pieces = [value[:, i * run : (i + 1) * run] for i in range(count)]
        names = list(high_bits) + ["zl", "x"]
        for position, name in enumerate(names):
            if name == "zl":
                continue
            mask = 1 << (len(names) - 1 - position)
            pieces = [pick(name, pieces[i], pieces[i ^ mask]) for i in range(count)]
        order = []
        for xr in range(2):
            for rest in range(count // 2):
                order.append(rest * 2 + xr)
        return jnp.concatenate([pieces[i] for i in order], axis=1)

    def to_natural(value):
        rows, width = value.shape
        count = 2 ** (len(high_bits) + 2)
        run = width // count
        moved = [value[:, i * run : (i + 1) * run] for i in range(count)]
        pieces = [None] * count
        place = 0
        for xr in range(2):
            for rest in range(count // 2):
                pieces[rest * 2 + xr] = moved[place]
                place += 1
        names = list(high_bits) + ["zl", "x"]
        for position, name in enumerate(names):
            if name == "zl":
                continue
            mask = 1 << (len(names) - 1 - position)
            pieces = [pick(name, pieces[i], pieces[i ^ mask]) for i in range(count)]
        return jnp.concatenate(pieces, axis=1)

    class Chain:
        def __init__(self, token):
            self.token = token

        def sync(self, *values):
            out = lax.optimization_barrier((self.token,) + values)
            self.token = out[0]
            return out[1] if len(values) == 1 else out[1:]

        def start(self, value, axis):
            return swap(self.sync(value), axis)

        def start_high(self, rows):
            for name in high_bits[:0:-1]:
                rows = jnp.concatenate([rows, self.sync(self.start(rows, name))], axis=0)
            return rows, (self.start(rows, high_bits[0]) if high_bits else None)

        def end_high(self, pending):
            rows, sent = pending
            return rows if sent is None else jnp.concatenate([rows, self.sync(sent)], axis=0)

        def start_high_sum(self, total):
            for name in high_bits[:-1]:
                half = total.shape[0] // 2
                total = total[:half] + self.sync(self.start(total[half:].astype(BF), name)).astype(F32)
            if not high_bits:
                return total, None
            half = total.shape[0] // 2
            return total[:half], self.start(total[half:].astype(BF), high_bits[-1])

        def end_high_sum(self, pending):
            total, sent = pending
            return total if sent is None else total + self.sync(sent).astype(F32)

    def gather_gains(c, gains):
        gains = ordered("tensor", gains, c.sync(c.start(gains, "tensor")), dim=1)
        gains = ordered("core", gains, c.sync(c.start(gains, "core")), dim=1)
        gains = ordered("zl", gains, c.sync(c.start(gains, "zl")), dim=1)
        for name in list(high_bits)[::-1] + ["x"]:
            gains = jnp.concatenate([gains, c.sync(c.start(gains, name))], axis=1)
        return gains

    def pair_sum(c, values):
        count, width = values.shape
        for level, axis in enumerate(("core", "zl", "tensor")):
            run = width >> (level + 1)
            other = c.sync(c.start(values, axis))
            blocks = [other[:, i * run : (i + 1) * run] for i in range(width // run)]
            values = values + jnp.concatenate([blocks[i ^ 1] for i in range(len(blocks))], axis=1)
        return values

    def scatter_gains(c, gains):
        for name in ["x"] + list(high_bits):
            half = gains.shape[1] // 2
            gains = gains[:, :half] + c.sync(c.start(gains[:, half:], name))
        for name in ("zl", "core", "tensor"):
            own, sent = split(gains, name, 1)
            gains = own + c.sync(c.start(sent, name))
        return gains

    def stack2(low, high):
        return jnp.concatenate([low, high], axis=0)

    def shards(
        tokens,
        segment_ids,
        w_query,
        w_key,
        w_value,
        w_output,
        w_gate,
        w_up,
        w_down,
        query_gain,
        key_gain,
        attn_gain,
        ffn_gain,
        cotangent,
    ):
        own_tokens, model_width = tokens.shape
        half_width = model_width // 2
        seq_length = own_tokens * 2
        core_tokens = seq_length * 2
        group_tokens = core_tokens * 2
        head_width = w_query.shape[1] // 4
        part = w_gate.shape[1] // 8
        local_heads = head_width // HD
        score_scale = 1.0 / math.sqrt(HD)
        c = Chain(query_gain)

        def columns(parts):
            return jnp.concatenate(parts, axis=1)

        attn_split = [split(w, "core", 1) for w in (w_query, w_key, w_value, w_output)]
        attn_sent = c.start(columns([s[1] for s in attn_split]), "core")
        tokens_rel = to_relative(tokens)
        left, right = tokens_rel[:, :half_width], tokens_rel[:, half_width:]
        left_sent = c.start(left, "tensor")
        ffn_split = [split(w, "core", 1) for w in (w_gate, w_up, w_down)]
        ffn_sent = c.start(columns([s[1] for s in ffn_split]), "core")

        attn_sent = c.sync(attn_sent)
        attn_pairs = [
            split(
                ordered("core", s[0], attn_sent[:, i * 2 * head_width : (i + 1) * 2 * head_width]),
                "zl",
                1,
            )
            for i, s in enumerate(attn_split)
        ]
        qk_line = c.start(columns([p[1] for p in attn_pairs[:2]]), "zl")
        right_sent = c.start(right, "zl")

        def line_rows(pairs, sent):
            own = columns([p[0] for p in pairs])
            return ordered("zl", own, sent)

        class WeightStream:
            def __init__(self):
                self.waiting, self.high, self.x, self.rows = [], [], [], []

            def add(self, *chunks):
                self.waiting.extend(chunks)

            def feed(self):
                self.high.append(c.start_high(self.waiting[len(self.high)]))

            def step(self):
                k = len(self.rows)
                rows = c.end_high(self.high[k])
                if len(self.high) < len(self.waiting):
                    self.feed()
                self.rows.append(rows)
                if k > 0:
                    self.x[k - 1] = c.sync(self.x[k - 1])
                self.x.append(c.start(rows, "x"))

            def end(self):
                self.x[-1] = c.sync(self.x[-1])

        stream = WeightStream()
        qk_rows = line_rows(attn_pairs[:2], c.sync(qk_line))
        stream.add(qk_rows)
        stream.feed()
        vo_line = c.start(columns([p[1] for p in attn_pairs[2:]]), "zl")
        ffn_sent = c.sync(ffn_sent)
        g_pair, u_pair, d_pair = [
            split(
                ordered("core", s[0], ffn_sent[:, i * 4 * part : (i + 1) * 4 * part]),
                "zl",
                1,
            )
            for i, s in enumerate(ffn_split)
        ]
        g_line = c.start(g_pair[1], "zl")
        left = stack2(left, c.sync(left_sent))
        right = stack2(right, c.sync(right_sent))

        def rows_second(left, right):
            left_sent = c.start(left, "zl")
            right_sent = c.start(right, "tensor")
            left = stack2(left, c.sync(left_sent))
            right_sent = c.sync(right_sent)
            rows = own_tokens
            right = jnp.concatenate(
                [right[:rows], right_sent[:rows], right[rows:], right_sent[rows:]], axis=0
            )
            left_sent = c.start(left, "core")
            right_sent = c.start(right, "core")
            return stack2(left, c.sync(left_sent)), stack2(right, c.sync(right_sent))

        def gather_rows(value):
            left, right = value[:, :half_width], value[:, half_width:]
            left_sent = c.start(left, "tensor")
            right_sent = c.start(right, "zl")
            left = stack2(left, c.sync(left_sent))
            right = stack2(right, c.sync(right_sent))
            return rows_second(left, right)

        vo_rows = line_rows(attn_pairs[2:], c.sync(vo_line))
        stream.add(vo_rows)
        stream.feed()
        in0, in1 = rows_second(left, right)
        g_rows = line_rows([g_pair], c.sync(g_line))
        stream.add(g_rows[:, :part], g_rows[:, part:])
        u_line = c.start(u_pair[1], "zl")
        ids = jnp.concatenate(
            [
                pick("tensor", segment_ids[:, :own_tokens], segment_ids[:, own_tokens:]),
                pick("tensor", segment_ids[:, own_tokens:], segment_ids[:, :own_tokens]),
            ],
            axis=1,
        )
        gains = jnp.stack([query_gain, key_gain, attn_gain, ffn_gain])
        gains = gather_gains(c, gains)
        stream.step()
        seq_ids = stack2(ids, c.sync(c.start(ids, "zl")))
        seq_ids = stack2(seq_ids, c.sync(c.start(seq_ids, "core")))
        u_rows = line_rows([u_pair], c.sync(u_line))
        stream.add(u_rows[:, :part], u_rows[:, part:])
        d_line = c.start(d_pair[1], "zl")

        attn_scale = gains[2]
        ffn_scale = gains[3]
        head_gains = to_natural(gains[:2])
        head_start = (bit("tensor") * 4 + bit("core") * 2 + bit("zl")) * head_width
        head_gains = lax.dynamic_slice_in_dim(head_gains, head_start, head_width, axis=1)
        query_scale, key_scale = head_gains[0], head_gains[1]
        tokens_f = tokens_rel.astype(F32)
        d_out = to_relative(cotangent).astype(F32)
        places = jnp.arange(own_tokens)
        positions = jnp.concatenate(
            [places + bit("tensor") * own_tokens, places + (1 - bit("tensor")) * own_tokens]
        )
        visible = (positions[:, None] >= positions[None, :])[None] & (
            seq_ids[:, :, None] == seq_ids[:, None, :]
        )
        visible = visible[:, None]

        d_rows = line_rows([d_pair], c.sync(d_line))
        stream.add(d_rows[:, :part], d_rows[:, part:])
        stream.step()
        wqk0, wqk1 = stream.rows[0], stream.x[0]
        qk = dot(in0, wqk0) + dot(in1, wqk1)
        query, key_proj = qk[:, :head_width], qk[:, head_width:]
        squares = pair_sum(
            c, jnp.stack([jnp.sum(query * query, axis=1), jnp.sum(key_proj * key_proj, axis=1)])
        )
        q_rms = lax.rsqrt(squares[0] / model_width + EPSILON)[:, None]
        k_rms = lax.rsqrt(squares[1] / model_width + EPSILON)[:, None]
        normed_query = (query * q_rms * query_scale).astype(BF)
        normed_key = (key_proj * k_rms * key_scale).astype(BF)
        stream.step()
        wv0, wo0 = stream.rows[1][:, :head_width], stream.rows[1][:, head_width:]
        wv1, wo1 = stream.x[1][:, :head_width], stream.x[1][:, head_width:]
        value_bf = (dot(in0, wv0) + dot(in1, wv1)).astype(BF)
        heads = (4, seq_length, local_heads, HD)
        query_heads = normed_query.reshape(heads)
        key_heads = normed_key.reshape(heads)
        value_heads = value_bf.reshape(heads)
        scores = (
            jnp.einsum("bqhd,bkhd->bhqk", query_heads, key_heads, preferred_element_type=F32)
            * score_scale
        )
        scores = jnp.where(visible, scores, NEGATIVE)
        peak = jnp.max(scores, axis=-1, keepdims=True)
        expo = jnp.exp(scores - peak)
        total = jnp.sum(expo, axis=-1, keepdims=True)
        prob = expo / total
        prob_bf = prob.astype(BF)
        attn_heads = jnp.einsum(
            "bhqk,bkhd->bqhd", prob_bf, value_heads, preferred_element_type=F32
        ).astype(BF)
        attn = attn_heads.reshape(group_tokens, head_width)

        def halve(total, axis):
            half = total.shape[0] // 2
            return total[:half], c.start(total[half:].astype(BF), axis)

        def added(pair):
            return pair[0] + c.sync(pair[1]).astype(F32)

        def cross(total):
            rows = own_tokens
            own = stack2(total[:rows], total[2 * rows : 3 * rows])
            sent = stack2(total[rows : 2 * rows], total[3 * rows :])
            return own, c.start(sent.astype(BF), "tensor")

        def scatter_rows(left_of, right_of, between=None):
            own, other = slice(0, core_tokens), slice(core_tokens, group_tokens)
            left_sent = c.start(left_of(other).astype(BF), "core")
            right_sent = c.start(right_of(other).astype(BF), "core")
            left = halve(left_of(own) + c.sync(left_sent).astype(F32), "zl")
            right = cross(right_of(own) + c.sync(right_sent).astype(F32))
            if between:
                between()
            left, right = added(left), added(right)
            left, right = halve(left, "tensor"), halve(right, "zl")
            return columns([added(left), added(right)])

        proj = scatter_rows(
            lambda rows: dot_nt(attn[rows], wo0), lambda rows: dot_nt(attn[rows], wo1), stream.step
        )
        attn_rms = rms_scale(proj)
        resid = tokens_f + proj * attn_rms * attn_scale
        h0, h1 = gather_rows(resid.astype(BF))
        stream.step()
        chunks = range(2)
        wg0, wu0, wd0 = [None, None], [None, None], [None, None]
        wg1, wu1, wd1 = [None, None], [None, None], [None, None]
        gate, up = [None, None], [None, None]
        wg0[0], wg1[0] = stream.rows[2], stream.x[2]
        gate[0] = dot(h0, wg0[0]) + dot(h1, wg1[0])
        stream.step()
        wg0[1], wg1[1] = stream.rows[3], stream.x[3]
        gate[1] = dot(h0, wg0[1]) + dot(h1, wg1[1])
        stream.step()
        wu0[0], wu1[0] = stream.rows[4], stream.x[4]
        up[0] = dot(h0, wu0[0]) + dot(h1, wu1[0])
        stream.step()
        wu0[1], wu1[1] = stream.rows[5], stream.x[5]
        up[1] = dot(h0, wu0[1]) + dot(h1, wu1[1])
        sigma = [jax.nn.sigmoid(g) for g in gate]
        act = [(gate[j] * sigma[j] * up[j]).astype(BF) for j in chunks]
        wd0[0], wd0[1] = stream.rows[6], stream.rows[7]

        own, other = slice(0, core_tokens), slice(core_tokens, group_tokens)

        def down(rows, w):
            return dot_nt(act[0][rows], w[0]) + dot_nt(act[1][rows], w[1])

        left_sent = c.start(down(other, wd0).astype(BF), "core")
        left = halve(down(own, wd0) + c.sync(left_sent).astype(F32), "zl")
        wd1[0] = stream.x[6]
        left = halve(added(left), "tensor")
        left = added(left)
        stream.end()
        wd1[1] = stream.x[7]
        right_sent = c.start(down(other, wd1).astype(BF), "core")
        right = cross(down(own, wd1) + c.sync(right_sent).astype(F32))
        right = halve(added(right), "zl")
        ffn = columns([left, added(right)])

        ffn_rms = rms_scale(ffn)
        output = to_natural((resid + ffn * ffn_rms * ffn_scale).astype(BF))
        ffn_gain_term = jnp.sum(d_out * ffn * ffn_rms, axis=0)
        scaled_out = d_out * ffn_scale
        d_ffn = (
            ffn_rms
            * (
                scaled_out
                - ffn * ffn_rms * ffn_rms * jnp.mean(scaled_out * ffn, axis=1, keepdims=True)
            )
        ).astype(BF)
        f0, f1 = gather_rows(d_ffn)

        class Grad:
            def __init__(self, count):
                self.parts, self.count = [], count

            def collect(self, total):
                self.parts.append(total)
                if len(self.parts) < self.count:
                    return False
                total = self.parts[0] if self.count == 1 else columns(self.parts)
                self.own, sent = split(total, "zl", 0)
                self.line = c.start(sent.astype(BF), "zl")
                return True

            def end_line(self):
                moved = c.sync(self.line).astype(F32)
                total = ordered("zl", self.own, moved, dim=1)
                self.own, sent = split(total, "core", 0)
                self.core = c.start(sent.astype(BF), "core")

            def end(self):
                self.result = ordered("core", self.own, c.sync(self.core).astype(F32), dim=1)

        class GradStream:
            def __init__(self):
                self.jobs, self.x = [], []
                self.at, self.high, self.lines, self.cores = 0, None, [], []

            def add(self, grad, kept, sent, right):
                self.jobs.append((grad, kept, sent, right))

            def feed(self):
                grad, kept, sent, right = self.jobs[len(self.x)]
                self.x.append(c.start(dot_tn(sent, right).astype(BF), "x"))

            def step(self):
                if self.at < len(self.x):
                    grad, kept, sent, right = self.jobs[self.at]
                    moved = c.sync(self.x[self.at])
                    if len(self.x) < len(self.jobs):
                        self.feed()
                    total = dot_tn(kept, right) + moved.astype(F32)
                    high = (grad, c.start_high_sum(total))
                    self.at += 1
                else:
                    high = None
                cores, lines = self.cores, self.lines
                self.cores, self.lines = [], []
                for grad in cores:
                    grad.end()
                for grad in lines:
                    grad.end_line()
                    self.cores.append(grad)
                if self.high is not None:
                    grad, pending = self.high
                    if grad.collect(c.end_high_sum(pending)):
                        self.lines.append(grad)
                self.high = high

            def idle(self):
                return self.high is None and not self.lines and not self.cores

        grads = GradStream()
        down_grad, gate_grad, up_grad = Grad(2), Grad(2), Grad(2)
        for j in chunks:
            grads.add(down_grad, f0, f1, act[j])
        grads.feed()
        grads.feed()
        d_gate, d_up = [None, None], [None, None]
        for j in chunks:
            d_act = dot(f0, wd0[j]) + dot(f1, wd1[j])
            d_gate[j] = (d_act * up[j] * sigma[j] * (1.0 + gate[j] * (1.0 - sigma[j]))).astype(BF)
            d_up[j] = (d_act * gate[j] * sigma[j]).astype(BF)
        for j in chunks:
            grads.add(gate_grad, h0, h1, d_gate[j])
            grads.add(up_grad, h0, h1, d_up[j])

        def hidden(rows, wg, wu):
            return (
                dot_nt(d_gate[0][rows], wg[0])
                + dot_nt(d_up[0][rows], wu[0])
                + dot_nt(d_gate[1][rows], wg[1])
                + dot_nt(d_up[1][rows], wu[1])
            )

        d_resid = d_out + scatter_rows(
            lambda rows: hidden(rows, wg0, wu0), lambda rows: hidden(rows, wg1, wu1), grads.step
        )
        attn_gain_term = jnp.sum(d_resid * proj * attn_rms, axis=0)
        scaled_resid = d_resid * attn_scale
        d_proj = (
            attn_rms
            * (
                scaled_resid
                - proj * attn_rms * attn_rms * jnp.mean(scaled_resid * proj, axis=1, keepdims=True)
            )
        ).astype(BF)
        grads.step()
        p0, p1 = gather_rows(d_proj)
        out_grad, value_grad, query_grad, key_grad = Grad(1), Grad(1), Grad(1), Grad(1)
        grads.add(out_grad, p0, p1, attn)
        d_attn = (dot(p0, wo0) + dot(p1, wo1)).astype(BF)
        grads.step()

        d_attn_heads = d_attn.reshape(heads)
        d_value = (
            jnp.einsum("bhqk,bqhd->bkhd", prob_bf, d_attn_heads, preferred_element_type=F32)
            .reshape(group_tokens, head_width)
            .astype(BF)
        )
        grads.add(value_grad, in0, in1, d_value)
        d_prob = jnp.einsum(
            "bqhd,bkhd->bhqk", d_attn_heads, value_heads, preferred_element_type=F32
        )
        delta = jnp.einsum(
            "bqhd,bqhd->bhq", d_attn_heads, attn.reshape(heads), preferred_element_type=F32
        )[..., None]
        d_score = (prob * (d_prob - delta)).astype(BF)
        d_nq = (
            jnp.einsum("bhqk,bkhd->bqhd", d_score, key_heads, preferred_element_type=F32).reshape(
                group_tokens, head_width
            )
            * score_scale
        )
        d_nk = (
            jnp.einsum("bhqk,bqhd->bkhd", d_score, query_heads, preferred_element_type=F32).reshape(
                group_tokens, head_width
            )
            * score_scale
        )
        query_gain_term = jnp.sum(d_nq * query * q_rms, axis=0)
        key_gain_term = jnp.sum(d_nk * key_proj * k_rms, axis=0)
        scaled_q = d_nq * query_scale
        scaled_k = d_nk * key_scale
        inner = pair_sum(
            c, jnp.stack([jnp.sum(scaled_q * query, axis=1), jnp.sum(scaled_k * key_proj, axis=1)])
        )
        grads.step()
        d_query = (
            q_rms * (scaled_q - query * q_rms * q_rms * (inner[0] / model_width)[:, None])
        ).astype(BF)
        d_key = (
            k_rms * (scaled_k - key_proj * k_rms * k_rms * (inner[1] / model_width)[:, None])
        ).astype(BF)
        grads.add(query_grad, in0, in1, d_query)
        grads.add(key_grad, in0, in1, d_key)
        d_qk = columns([d_query, d_key])

        d_tokens = scatter_rows(
            lambda rows: dot_nt(d_qk[rows], wqk0) + dot_nt(d_value[rows], wv0),
            lambda rows: dot_nt(d_qk[rows], wqk1) + dot_nt(d_value[rows], wv1),
            grads.step,
        )
        grad_tokens = to_natural(d_resid + d_tokens)
        grads.step()

        zero = jnp.zeros((2, model_width), F32)
        placed = lax.dynamic_update_slice_in_dim(
            zero, jnp.stack([query_gain_term, key_gain_term]), head_start, 1
        )
        gain_parts = scatter_gains(
            c,
            jnp.concatenate(
                [to_relative(placed), jnp.stack([attn_gain_term, ffn_gain_term])], axis=0
            ),
        )
        while grads.at < len(grads.jobs) or not grads.idle():
            grads.step()
        return (
            output,
            grad_tokens,
            query_grad.result,
            key_grad.result,
            value_grad.result,
            out_grad.result,
            gate_grad.result,
            up_grad.result,
            down_grad.result,
            gain_parts[0],
            gain_parts[1],
            gain_parts[2],
            gain_parts[3],
        )

    return shards


def solution(mesh):
    dp = mesh.shape["dp"]
    high = max(dp.bit_length() - 4, 0)
    high_bits = tuple(f"z{i}" for i in range(high))
    names = high_bits + ("zl", "x", "core", "tensor")
    fine = Mesh(mesh.devices.reshape((2,) * len(names)), names)
    rows = names[:-1]
    both = names
    mapped = jax.shard_map(
        build(high_bits),
        mesh=fine,
        in_specs=(
            P(both, None),
            P(rows, None),
            P(rows, "tensor"),
            P(rows, "tensor"),
            P(rows, "tensor"),
            P(rows, "tensor"),
            P(rows, "tensor"),
            P(rows, "tensor"),
            P(rows, "tensor"),
            P(both),
            P(both),
            P(both),
            P(both),
            P(both, None),
        ),
        out_specs=(
            P(both, None),
            P(both, None),
            P(rows, "tensor"),
            P(rows, "tensor"),
            P(rows, "tensor"),
            P(rows, "tensor"),
            P(rows, "tensor"),
            P(rows, "tensor"),
            P(rows, "tensor"),
            P(both),
            P(both),
            P(both),
            P(both),
        ),
        check_vma=False,
    )
    return mapped
```

```python
import math

import jax
import jax.numpy as jnp
from jax import lax
from jax.sharding import Mesh, PartitionSpec as P

HD = 128

EPSILON = 1e-06
NEGATIVE = -1e30
FLIP = [(0, 1), (1, 0)]
BF = jnp.bfloat16
F32 = jnp.float32


def swap(value, axis):
    return lax.ppermute(value, axis, FLIP)


def bit(axis):
    return lax.axis_index(axis)


def pick(axis, low, high):
    return jnp.where(bit(axis) == 0, low, high)


def ordered(axis, own, other, dim=0):
    return jnp.concatenate([pick(axis, own, other), pick(axis, other, own)], axis=dim)


def split(value, axis, dim):
    half = value.shape[dim] // 2
    low = lax.slice_in_dim(value, 0, half, axis=dim)
    high = lax.slice_in_dim(value, half, 2 * half, axis=dim)
    return pick(axis, low, high), pick(axis, high, low)


def dot(a, b):
    return jnp.dot(a, b, preferred_element_type=F32)


def dot_nt(a, b):
    return jnp.einsum("sc,rc->sr", a, b, preferred_element_type=F32)


def dot_tn(a, b):
    return jnp.einsum("sr,sc->rc", a, b, preferred_element_type=F32)


def rms_scale(values):
    return lax.rsqrt(jnp.mean(values * values, axis=1, keepdims=True) + EPSILON)


def build(high_bits):
    def to_relative(value):
        rows, width = value.shape
        count = 2 ** (len(high_bits) + 2)
        run = width // count
        pieces = [value[:, i * run : (i + 1) * run] for i in range(count)]
        names = list(high_bits) + ["zl", "x"]
        for position, name in enumerate(names):
            if name == "zl":
                continue
            mask = 1 << (len(names) - 1 - position)
            pieces = [pick(name, pieces[i], pieces[i ^ mask]) for i in range(count)]
        order = []
        for xr in range(2):
            for rest in range(count // 2):
                order.append(rest * 2 + xr)
        return jnp.concatenate([pieces[i] for i in order], axis=1)

    def to_natural(value):
        rows, width = value.shape
        count = 2 ** (len(high_bits) + 2)
        run = width // count
        moved = [value[:, i * run : (i + 1) * run] for i in range(count)]
        pieces = [None] * count
        place = 0
        for xr in range(2):
            for rest in range(count // 2):
                pieces[rest * 2 + xr] = moved[place]
                place += 1
        names = list(high_bits) + ["zl", "x"]
        for position, name in enumerate(names):
            if name == "zl":
                continue
            mask = 1 << (len(names) - 1 - position)
            pieces = [pick(name, pieces[i], pieces[i ^ mask]) for i in range(count)]
        return jnp.concatenate(pieces, axis=1)

    class Chain:
        def __init__(self, token):
            self.token = token
            self.zero = jnp.int32(0)

        def sync(self, *values):
            out = lax.optimization_barrier((self.token,) + values)
            self.token = out[0]
            return out[1] if len(values) == 1 else out[1:]

        def start(self, value, axis):
            return swap(self.sync(value), axis)

        def fence(self, *values):
            moved = self.sync(self.start(jnp.full((1, HD), bit("core"), jnp.int32), "core"))
            self.zero = self.zero + (moved[0, 0] + bit("core") - 1)
            return self.sync(*values)

    def gather_gains(c, gains):
        for name in ("tensor", "core", "zl"):
            sent = c.start(gains, name)
            yield
            gains = ordered(name, gains, c.sync(sent), dim=1)
        for name in list(high_bits)[::-1] + ["x"]:
            sent = c.start(gains, name)
            yield
            gains = jnp.concatenate([gains, c.sync(sent)], axis=1)
        return gains

    def pair_sum(c, values, between=None):
        count, width = values.shape
        for level, axis in ((1, "zl"), (2, "tensor"), (0, "core")):
            run = width >> (level + 1)
            other = c.sync(c.start(values, axis))
            blocks = [other[:, i * run : (i + 1) * run] for i in range(width // run)]
            values = values + jnp.concatenate([blocks[i ^ 1] for i in range(len(blocks))], axis=1)
            if between and axis == "zl":
                between()
        return values

    def scatter_gains(c, gains):
        for name in ["x"] + list(high_bits):
            half = gains.shape[1] // 2
            sent = c.start(gains[:, half:], name)
            yield
            gains = gains[:, :half] + c.sync(sent)
        for name in ("zl", "core", "tensor"):
            own, sent = split(gains, name, 1)
            sent = c.start(sent, name)
            yield
            gains = own + c.sync(sent)
        return gains

    class Steps:
        def __init__(self, stages):
            self.stages, self.done = stages, False
            self()

        def __call__(self):
            if not self.done:
                try:
                    next(self.stages)
                except StopIteration as end:
                    self.value, self.done = end.value, True

        def finish(self):
            while not self.done:
                self()
            return self.value

    def stack2(low, high):
        return jnp.concatenate([low, high], axis=0)

    def shards(
        tokens,
        segment_ids,
        w_query,
        w_key,
        w_value,
        w_output,
        w_gate,
        w_up,
        w_down,
        query_gain,
        key_gain,
        attn_gain,
        ffn_gain,
        cotangent,
    ):
        own_tokens, model_width = tokens.shape
        half_width = model_width // 2
        block_width = half_width // 2
        seq_length = own_tokens * 2
        core_tokens = seq_length * 2
        group_tokens = core_tokens * 2
        head_width = w_query.shape[1] // 4
        local_heads = head_width // HD
        score_scale = 1.0 / math.sqrt(HD)
        own, other = slice(0, core_tokens), slice(core_tokens, group_tokens)
        c = Chain(query_gain)

        def columns(parts):
            return parts[0] if len(parts) == 1 else jnp.concatenate(parts, axis=1)

        class Weight:
            def __init__(self, matrices, sent):
                width = sent.shape[1] // len(matrices)
                pairs = [
                    split(ordered("core", m, sent[:, i * width : (i + 1) * width]), "zl", 1)
                    for i, m in enumerate(matrices)
                ]
                self.own = columns([p[0] for p in pairs])
                self.sent = columns([p[1] for p in pairs])
                self.blocks = [[None, None], [None, None]]

            def start_line(self):
                self.line = c.start(self.sent, "zl")

            def end_line(self):
                rows = ordered("zl", self.own, c.sync(self.line))
                for name in high_bits[:0:-1]:
                    rows = stack2(rows, c.sync(c.start(rows, name)))
                self.blocks[0][0] = rows

            def start_high(self):
                self.high = c.start(self.blocks[0][0], high_bits[0])

            def end_high(self):
                self.blocks[0][1] = c.sync(self.high)

            def start_x(self, block):
                self.blocks[1][block] = c.start(self.blocks[0][block], "x")

            def end_x(self, block):
                self.blocks[1][block] = c.sync(self.blocks[1][block])

            def rows(self, side):
                return stack2(*self.blocks[side])

        attn_split = [split(w, "core", 1) for w in (w_query, w_key, w_value, w_output)]
        attn_sent = c.start(columns([s[1] for s in attn_split]), "core")
        gains = jnp.stack([query_gain, key_gain, attn_gain, ffn_gain])
        gain_steps = Steps(gather_gains(c, gains))
        tokens_rel = to_relative(tokens)
        left, right = tokens_rel[:, :half_width], tokens_rel[:, half_width:]
        left_sent = c.start(left, "tensor")
        ffn_split = [split(w, "core", 1) for w in (w_gate, w_up, w_down)]
        ffn_sent = c.start(columns([s[1] for s in ffn_split]), "core")
        gain_steps()

        attn_sent = c.sync(attn_sent)
        pair_width = 4 * head_width
        qk = Weight([s[0] for s in attn_split[:2]], attn_sent[:, :pair_width])
        vo = Weight([s[0] for s in attn_split[2:]], attn_sent[:, pair_width:])
        qk.start_line()
        gain_steps()
        ids = jnp.concatenate(
            [
                pick("tensor", segment_ids[:, :own_tokens], segment_ids[:, own_tokens:]),
                pick("tensor", segment_ids[:, own_tokens:], segment_ids[:, :own_tokens]),
            ],
            axis=1,
        )
        ids_sent = c.start(ids, "zl")
        right_sent = c.start(right, "zl")
        qk.end_line()
        gain_steps()
        qk.start_x(0)
        qk.start_high()
        vo.start_line()
        left = stack2(left, c.sync(left_sent))
        seq_ids = stack2(ids, c.sync(ids_sent))
        ids_sent = c.start(seq_ids, "core")
        right = stack2(right, c.sync(right_sent))

        def rows_second(left, right, between=None, last=None):
            left_sent = c.start(left, "zl")
            right_sent = c.start(right, "tensor")
            if between:
                between()
            left = stack2(left, c.sync(left_sent))
            right_sent = c.sync(right_sent)
            rows = own_tokens
            right = jnp.concatenate(
                [right[:rows], right_sent[:rows], right[rows:], right_sent[rows:]], axis=0
            )
            if last:
                last()
            left_sent = c.start(left, "core")
            right_sent = c.start(right, "core")
            return stack2(left, c.sync(left_sent)), stack2(right, c.sync(right_sent))

        def gather_rows(value, between=None):
            left, right = value[:, :half_width], value[:, half_width:]
            left_sent = c.start(left, "tensor")
            right_sent = c.start(right, "zl")
            left = stack2(left, c.sync(left_sent))
            right = stack2(right, c.sync(right_sent))
            return rows_second(left, right, between)

        ffn_sent = c.sync(ffn_sent)
        width = ffn_sent.shape[1] // 3
        gate_w, up_w, down_w = [
            Weight([s[0]], ffn_sent[:, i * width : (i + 1) * width])
            for i, s in enumerate(ffn_split)
        ]

        def tokens_between():
            vo.end_line()
            gate_w.start_line()
            gain_steps()
            qk.end_x(0)
            vo.start_x(0)

        def tokens_last():
            qk.end_high()
            qk.start_x(1)
            vo.start_high()

        in0, in1 = rows_second(left, right, tokens_between, tokens_last)
        seq_ids = stack2(seq_ids, c.sync(ids_sent))
        gate_w.end_line()
        gate_w.start_x(0)
        gains = gain_steps.finish()
        qk.end_x(1)

        attn_scale = gains[2]
        ffn_scale = gains[3]
        head_gains = to_natural(gains[:2])
        head_start = (bit("tensor") * 4 + bit("core") * 2 + bit("zl")) * head_width
        head_gains = lax.dynamic_slice_in_dim(head_gains, head_start, head_width, axis=1)
        query_scale, key_scale = head_gains[0], head_gains[1]
        tokens_f = tokens_rel.astype(F32)
        d_out = to_relative(cotangent).astype(F32)
        places = jnp.arange(own_tokens)
        positions = jnp.concatenate(
            [places + bit("tensor") * own_tokens, places + (1 - bit("tensor")) * own_tokens]
        )
        visible = (positions[:, None] >= positions[None, :])[None] & (
            seq_ids[:, :, None] == seq_ids[:, None, :]
        )
        visible = visible[:, None]

        wqk0, wqk1 = qk.rows(0), qk.rows(1)
        projected = dot(in0, wqk0) + dot(in1, wqk1)
        query, key_proj = projected[:, :head_width], projected[:, head_width:]
        squares = pair_sum(
            c,
            jnp.stack([jnp.sum(query * query, axis=1), jnp.sum(key_proj * key_proj, axis=1)]),
            up_w.start_line,
        )
        q_rms = lax.rsqrt(squares[0] / model_width + EPSILON)[:, None]
        k_rms = lax.rsqrt(squares[1] / model_width + EPSILON)[:, None]
        normed_query = (query * q_rms * query_scale).astype(BF)
        normed_key = (key_proj * k_rms * key_scale).astype(BF)
        vo.end_high()
        vo.end_x(0)
        vo.start_x(1)
        gate_w.start_high()
        up_w.end_line()
        down_w.start_line()
        gate_w.end_x(0)
        up_w.start_x(0)
        vo.end_x(1)
        normed_query, normed_key = c.sync(normed_query, normed_key)
        wvo0, wvo1 = vo.rows(0), vo.rows(1)
        wv0, wo0 = wvo0[:, :head_width], wvo0[:, head_width:]
        wv1, wo1 = wvo1[:, :head_width], wvo1[:, head_width:]
        value_bf = (dot(in0, wv0) + dot(in1, wv1)).astype(BF)
        heads = (4, seq_length, local_heads, HD)
        query_heads = normed_query.reshape(heads)
        key_heads = normed_key.reshape(heads)
        value_heads = value_bf.reshape(heads)
        scores = (
            jnp.einsum("bqhd,bkhd->bhqk", query_heads, key_heads, preferred_element_type=F32)
            * score_scale
        )
        scores = jnp.where(visible, scores, NEGATIVE)
        peak = jnp.max(scores, axis=-1, keepdims=True)
        expo = jnp.exp(scores - peak)
        total = jnp.sum(expo, axis=-1, keepdims=True)
        prob = expo / total
        prob_bf = prob.astype(BF)
        attn_heads = jnp.einsum(
            "bhqk,bkhd->bqhd", prob_bf, value_heads, preferred_element_type=F32
        ).astype(BF)
        attn = attn_heads.reshape(group_tokens, head_width)
        down_w.end_line()
        gate_w.end_high()
        gate_w.start_x(1)
        up_w.start_high()
        up_w.end_x(0)

        def halve(total, axis):
            half = total.shape[0] // 2
            return total[:half], c.start(total[half:].astype(BF), axis)

        def added(pair):
            return pair[0] + c.sync(pair[1]).astype(F32)

        def cross(total):
            rows = own_tokens
            own = stack2(total[:rows], total[2 * rows : 3 * rows])
            sent = stack2(total[rows : 2 * rows], total[3 * rows :])
            return own, c.start(sent.astype(BF), "tensor")

        def scatter_rows(left_of, right_of, first=None, second=None):
            left_sent = c.start(left_of(other).astype(BF), "core")
            right_sent = c.start(right_of(other).astype(BF), "core")
            left = halve(left_of(own) + c.sync(left_sent).astype(F32), "zl")
            right = cross(right_of(own) + c.sync(right_sent).astype(F32))
            if first:
                first()
            left, right = added(left), added(right)
            left, right = halve(left, "tensor"), halve(right, "zl")
            if second:
                second()
            return added(left), added(right)

        def first_down():
            down_w.start_x(0)

        proj = columns(
            scatter_rows(
                lambda rows: dot_nt(attn[rows], wo0), lambda rows: dot_nt(attn[rows], wo1), first_down
            )
        )
        attn_rms = rms_scale(proj)
        resid = tokens_f + proj * attn_rms * attn_scale

        def resid_between():
            gate_w.end_x(1)
            down_w.end_x(0)

        resid_bf = c.sync(resid.astype(BF))
        up_w.end_high()
        up_w.start_x(1)
        down_w.start_high()
        h0, h1 = gather_rows(resid_bf, resid_between)
        wg0, wg1 = gate_w.rows(0), gate_w.rows(1)
        gate = dot(h0, wg0) + dot(h1, wg1)
        gate = c.sync(gate)
        sigma = jax.nn.sigmoid(gate)
        down_w.end_high()
        down_w.start_x(1)
        up_w.end_x(1)
        wu0, wu1 = up_w.rows(0), up_w.rows(1)
        up = dot(h0, wu0) + dot(h1, wu1)
        act = (gate * sigma * up).astype(BF)

        wd0 = down_w.rows(0)
        first_rows = down_w.blocks[1][0]
        left, right = scatter_rows(
            lambda rows: dot_nt(act[rows], wd0), lambda rows: dot_nt(act[rows], first_rows)
        )
        down_w.end_x(1)
        last_rows = down_w.blocks[1][1]
        sent = c.start(dot_nt(act[other], last_rows).astype(BF), "core")
        last = cross(dot_nt(act[own], last_rows) + c.sync(sent).astype(F32))
        last = halve(added(last), "zl")
        ffn = columns([left, right, added(last)])
        wd1 = down_w.rows(1)

        ffn_rms = rms_scale(ffn)
        output = to_natural((resid + ffn * ffn_rms * ffn_scale).astype(BF))
        ffn_gain_term = jnp.sum(d_out * ffn * ffn_rms, axis=0)
        scaled_out = d_out * ffn_scale
        d_ffn = (
            ffn_rms
            * (
                scaled_out
                - ffn * ffn_rms * ffn_rms * jnp.mean(scaled_out * ffn, axis=1, keepdims=True)
            )
        ).astype(BF)
        f0, f1 = gather_rows(d_ffn)

        class Grad:
            def __init__(self, *terms):
                self.terms = terms
                self.x, self.total = [None, None], [None, None]

            def product(self, side, block):
                cols = slice(block * block_width, (block + 1) * block_width)
                return columns([dot_tn(halves[side][:, cols], r) for halves, r in self.terms])

            def start_x(self, block):
                self.x[block] = c.start(self.product(1, block).astype(BF), "x")

            def end_x(self, block):
                moved = c.sync(self.x[block])
                self.total[block] = self.product(0, block) + moved.astype(F32)

            def start_high(self):
                self.high = c.start(self.total[1].astype(BF), high_bits[0])

            def end_high(self):
                total = self.total[0] + c.sync(self.high).astype(F32)
                for name in high_bits[1:]:
                    total = added(halve(total, name))
                self.own, self.sent = split(total, "zl", 0)

            def start_line(self):
                self.line = c.start(self.sent.astype(BF), "zl")

            def joined(self, axis, moved):
                width = moved.shape[1] // len(self.terms)
                cols = [slice(i * width, (i + 1) * width) for i in range(len(self.terms))]
                return [ordered(axis, self.own[:, s], moved[:, s], dim=1) for s in cols]

            def end_line(self):
                moved = c.sync(self.line).astype(F32)
                self.own, sent = split(columns(self.joined("zl", moved)), "core", 0)
                self.core = c.start(sent.astype(BF), "core")

            def end(self):
                self.results = self.joined("core", c.sync(self.core).astype(F32))

        down_grad = Grad(((f0, f1), act))
        down_grad.start_x(1)
        down_grad.start_x(0)
        f0, f1 = c.fence(f0, f1)
        d_act = dot(f0, wd0) + dot(f1, wd1)
        d_gate = (d_act * up * sigma * (1.0 + gate * (1.0 - sigma))).astype(BF)
        d_up = (d_act * gate * sigma).astype(BF)
        gate_grad = Grad(((h0, h1), d_gate))
        up_grad = Grad(((h0, h1), d_up))
        down_grad.end_x(1)
        down_grad.start_high()
        gate_grad.start_x(1)

        def hidden_first():
            down_grad.end_x(0)
            gate_grad.start_x(0)

        d_resid = d_out + columns(
            scatter_rows(
                lambda rows: dot_nt(d_gate[rows], wg0) + dot_nt(d_up[rows], wu0),
                lambda rows: dot_nt(d_gate[rows], wg1) + dot_nt(d_up[rows], wu1),
                hidden_first,
            )
        )
        attn_gain_term = jnp.sum(d_resid * proj * attn_rms, axis=0)
        scaled_resid = d_resid * attn_scale
        d_proj = (
            attn_rms
            * (
                scaled_resid
                - proj * attn_rms * attn_rms * jnp.mean(scaled_resid * proj, axis=1, keepdims=True)
            )
        ).astype(BF)
        gate_grad.end_x(1)
        up_grad.start_x(1)

        d_proj = c.sync(d_proj)
        down_grad.end_high()
        gate_grad.start_high()

        def proj_between():
            down_grad.start_line()

        p0, p1 = gather_rows(d_proj, proj_between)
        gate_grad.end_x(0)
        up_grad.start_x(0)
        p0, p1 = c.fence(p0, p1)
        d_attn = (dot(p0, wo0) + dot(p1, wo1)).astype(BF)

        d_attn_heads = d_attn.reshape(heads)
        d_value = (
            jnp.einsum("bhqk,bqhd->bkhd", prob_bf, d_attn_heads, preferred_element_type=F32)
            .reshape(group_tokens, head_width)
            .astype(BF)
        )
        d_prob = jnp.einsum(
            "bqhd,bkhd->bhqk", d_attn_heads, value_heads, preferred_element_type=F32
        )
        delta = jnp.einsum(
            "bqhd,bqhd->bhq", d_attn_heads, attn.reshape(heads), preferred_element_type=F32
        )[..., None]
        d_score = (prob * (d_prob - delta)).astype(BF)
        d_nq = (
            jnp.einsum("bhqk,bkhd->bqhd", d_score, key_heads, preferred_element_type=F32).reshape(
                group_tokens, head_width
            )
            * score_scale
        )
        d_nk = (
            jnp.einsum("bhqk,bqhd->bkhd", d_score, query_heads, preferred_element_type=F32).reshape(
                group_tokens, head_width
            )
            * score_scale
        )
        query_gain_term = jnp.sum(d_nq * query * q_rms, axis=0)
        key_gain_term = jnp.sum(d_nk * key_proj * k_rms, axis=0)
        scaled_q = d_nq * query_scale
        scaled_k = d_nk * key_scale
        zero = jnp.zeros((2, model_width), F32)
        placed = lax.dynamic_update_slice_in_dim(
            zero, jnp.stack([query_gain_term, key_gain_term]), head_start + c.zero, 1
        )
        gain_parts = jnp.concatenate(
            [to_relative(placed), jnp.stack([attn_gain_term, ffn_gain_term])], axis=0
        )
        gain_steps = Steps(scatter_gains(c, gain_parts))
        up_grad.end_x(1)
        down_grad.end_line()
        inner = pair_sum(
            c, jnp.stack([jnp.sum(scaled_q * query, axis=1), jnp.sum(scaled_k * key_proj, axis=1)])
        )
        gain_steps()
        d_query = (
            q_rms * (scaled_q - query * q_rms * q_rms * (inner[0] / model_width)[:, None])
        ).astype(BF)
        d_key = (
            k_rms * (scaled_k - key_proj * k_rms * k_rms * (inner[1] / model_width)[:, None])
        ).astype(BF)
        d_qk = columns([d_query, d_key])
        ov_grad = Grad(((p0, p1), attn), ((in0, in1), d_value))
        qk_grad = Grad(((in0, in1), d_query), ((in0, in1), d_key))
        gate_grad.end_high()
        gain_steps()
        up_grad.start_high()
        ov_grad.start_x(1)
        down_grad.end()

        def tokens_first():
            up_grad.end_x(0)
            qk_grad.start_x(1)
            gate_grad.start_line()
            ov_grad.end_x(1)
            ov_grad.start_x(0)

        def tokens_second():
            gain_steps()
            qk_grad.end_x(1)
            qk_grad.start_x(0)

        d_tokens = columns(
            scatter_rows(
                lambda rows: dot_nt(d_qk[rows], wqk0) + dot_nt(d_value[rows], wv0),
                lambda rows: dot_nt(d_qk[rows], wqk1) + dot_nt(d_value[rows], wv1),
                tokens_first,
                tokens_second,
            )
        )
        grad_tokens = to_natural(d_resid + d_tokens)
        gate_grad.end_line()
        gain_steps()
        ov_grad.end_x(0)
        up_grad.end_high()
        ov_grad.start_high()
        up_grad.start_line()
        gate_grad.end()
        qk_grad.end_x(0)
        qk_grad.start_high()
        gain_parts = gain_steps.finish()
        up_grad.end_line()
        ov_grad.end_high()
        ov_grad.start_line()
        up_grad.end()
        ov_grad.end_line()
        qk_grad.end_high()
        qk_grad.start_line()
        ov_grad.end()
        qk_grad.end_line()
        qk_grad.end()
        grad_output, grad_value = ov_grad.results
        grad_query, grad_key = qk_grad.results
        return (
            output,
            grad_tokens,
            grad_query,
            grad_key,
            grad_value,
            grad_output,
            gate_grad.results[0],
            up_grad.results[0],
            down_grad.results[0],
            gain_parts[0],
            gain_parts[1],
            gain_parts[2],
            gain_parts[3],
        )

    return shards


def solution(mesh):
    dp = mesh.shape["dp"]
    high = max(dp.bit_length() - 4, 0)
    high_bits = tuple(f"z{i}" for i in range(high))
    names = high_bits + ("zl", "x", "core", "tensor")
    fine = Mesh(mesh.devices.reshape((2,) * len(names)), names)
    rows = names[:-1]
    both = names
    mapped = jax.shard_map(
        build(high_bits),
        mesh=fine,
        in_specs=(
            P(both, None),
            P(rows, None),
            P(rows, "tensor"),
            P(rows, "tensor"),
            P(rows, "tensor"),
            P(rows, "tensor"),
            P(rows, "tensor"),
            P(rows, "tensor"),
            P(rows, "tensor"),
            P(both),
            P(both),
            P(both),
            P(both),
            P(both, None),
        ),
        out_specs=(
            P(both, None),
            P(both, None),
            P(rows, "tensor"),
            P(rows, "tensor"),
            P(rows, "tensor"),
            P(rows, "tensor"),
            P(rows, "tensor"),
            P(rows, "tensor"),
            P(rows, "tensor"),
            P(both),
            P(both),
            P(both),
            P(both),
        ),
        check_vma=False,
    )
    return mapped
```

```python
import math

import jax
import jax.numpy as jnp
from jax import lax
from jax.sharding import Mesh, PartitionSpec as P

HD = 128

EPSILON = 1e-06
NEGATIVE = -1e30
FLIP = [(0, 1), (1, 0)]
BF = jnp.bfloat16
F32 = jnp.float32


def swap(value, axis):
    return lax.ppermute(value, axis, FLIP)


def bit(axis):
    return lax.axis_index(axis)


def pick(axis, low, high):
    return jnp.where(bit(axis) == 0, low, high)


def ordered(axis, own, other, dim=0):
    return jnp.concatenate([pick(axis, own, other), pick(axis, other, own)], axis=dim)


def split(value, axis, dim):
    half = value.shape[dim] // 2
    low = lax.slice_in_dim(value, 0, half, axis=dim)
    high = lax.slice_in_dim(value, half, 2 * half, axis=dim)
    return pick(axis, low, high), pick(axis, high, low)


def dot(a, b):
    return jnp.dot(a, b, preferred_element_type=F32)


def dot_nt(a, b):
    return jnp.einsum("sc,rc->sr", a, b, preferred_element_type=F32)


def dot_tn(a, b):
    return jnp.einsum("sr,sc->rc", a, b, preferred_element_type=F32)


def rms_scale(values):
    return lax.rsqrt(jnp.mean(values * values, axis=1, keepdims=True) + EPSILON)


def build(high_bits):
    def to_relative(value):
        rows, width = value.shape
        count = 2 ** (len(high_bits) + 2)
        run = width // count
        pieces = [value[:, i * run : (i + 1) * run] for i in range(count)]
        names = list(high_bits) + ["zl", "x"]
        for position, name in enumerate(names):
            if name == "zl":
                continue
            mask = 1 << (len(names) - 1 - position)
            pieces = [pick(name, pieces[i], pieces[i ^ mask]) for i in range(count)]
        order = []
        for xr in range(2):
            for rest in range(count // 2):
                order.append(rest * 2 + xr)
        return jnp.concatenate([pieces[i] for i in order], axis=1)

    def to_natural(value):
        rows, width = value.shape
        count = 2 ** (len(high_bits) + 2)
        run = width // count
        moved = [value[:, i * run : (i + 1) * run] for i in range(count)]
        pieces = [None] * count
        place = 0
        for xr in range(2):
            for rest in range(count // 2):
                pieces[rest * 2 + xr] = moved[place]
                place += 1
        names = list(high_bits) + ["zl", "x"]
        for position, name in enumerate(names):
            if name == "zl":
                continue
            mask = 1 << (len(names) - 1 - position)
            pieces = [pick(name, pieces[i], pieces[i ^ mask]) for i in range(count)]
        return jnp.concatenate(pieces, axis=1)

    class Chain:
        def __init__(self, token):
            self.token = token
            self.zero = jnp.int32(0)

        def sync(self, *values):
            out = lax.optimization_barrier((self.token,) + values)
            self.token = out[0]
            return out[1] if len(values) == 1 else out[1:]

        def start(self, value, axis):
            return swap(self.sync(value), axis)

        def fence(self, *values):
            moved = self.sync(self.start(jnp.full((1, HD), bit("core"), jnp.int32), "core"))
            self.zero = self.zero + (moved[0, 0] + bit("core") - 1)
            return self.sync(*values)

    def gather_gains(c, gains):
        for name in ("tensor", "core", "zl"):
            sent = c.start(gains, name)
            yield
            gains = ordered(name, gains, c.sync(sent), dim=1)
        for name in list(high_bits)[::-1] + ["x"]:
            sent = c.start(gains, name)
            yield
            gains = jnp.concatenate([gains, c.sync(sent)], axis=1)
        return gains

    def pair_sum(c, values, between=None):
        count, width = values.shape
        for level, axis in ((1, "zl"), (2, "tensor"), (0, "core")):
            run = width >> (level + 1)
            other = c.sync(c.start(values, axis))
            blocks = [other[:, i * run : (i + 1) * run] for i in range(width // run)]
            values = values + jnp.concatenate([blocks[i ^ 1] for i in range(len(blocks))], axis=1)
            if between and axis == "zl":
                between()
        return values

    def scatter_gains(c, gains):
        for name in ["x"] + list(high_bits):
            half = gains.shape[1] // 2
            sent = c.start(gains[:, half:], name)
            yield
            gains = gains[:, :half] + c.sync(sent)
        for name in ("zl", "core", "tensor"):
            own, sent = split(gains, name, 1)
            sent = c.start(sent, name)
            yield
            gains = own + c.sync(sent)
        return gains

    class Steps:
        def __init__(self, stages):
            self.stages, self.done = stages, False
            self()

        def __call__(self):
            if not self.done:
                try:
                    next(self.stages)
                except StopIteration as end:
                    self.value, self.done = end.value, True

        def finish(self):
            while not self.done:
                self()
            return self.value

    def stack2(low, high):
        return jnp.concatenate([low, high], axis=0)

    def shards(
        tokens,
        segment_ids,
        w_query,
        w_key,
        w_value,
        w_output,
        w_gate,
        w_up,
        w_down,
        query_gain,
        key_gain,
        attn_gain,
        ffn_gain,
        cotangent,
    ):
        own_tokens, model_width = tokens.shape
        half_width = model_width // 2
        block_width = half_width // 2
        seq_length = own_tokens * 2
        core_tokens = seq_length * 2
        group_tokens = core_tokens * 2
        head_width = w_query.shape[1] // 4
        local_heads = head_width // HD
        score_scale = 1.0 / math.sqrt(HD)
        own, other = slice(0, core_tokens), slice(core_tokens, group_tokens)
        c = Chain(jnp.full((1, HD), bit("core"), jnp.int32))

        def columns(parts):
            return parts[0] if len(parts) == 1 else jnp.concatenate(parts, axis=1)

        class Weight:
            def __init__(self, matrices, sent):
                width = sent.shape[1] // len(matrices)
                pairs = [
                    split(ordered("core", m, sent[:, i * width : (i + 1) * width]), "zl", 1)
                    for i, m in enumerate(matrices)
                ]
                self.own = columns([p[0] for p in pairs])
                self.sent = columns([p[1] for p in pairs])
                self.blocks = [[None, None], [None, None]]

            def start_line(self):
                self.line = c.start(self.sent, "zl")

            def end_line(self):
                rows = ordered("zl", self.own, c.sync(self.line))
                for name in high_bits[:0:-1]:
                    rows = stack2(rows, c.sync(c.start(rows, name)))
                self.blocks[0][0] = rows

            def start_high(self):
                self.high = c.start(self.blocks[0][0], high_bits[0])

            def end_high(self):
                self.blocks[0][1] = c.sync(self.high)

            def start_x(self, block):
                self.blocks[1][block] = c.start(self.blocks[0][block], "x")

            def end_x(self, block):
                self.blocks[1][block] = c.sync(self.blocks[1][block])

            def rows(self, side):
                return stack2(*self.blocks[side])

        attn_split = [split(w, "core", 1) for w in (w_query, w_key, w_value, w_output)]
        attn_sent = c.start(columns([s[1] for s in attn_split]), "core")
        gains = jnp.stack([query_gain, key_gain, attn_gain, ffn_gain])
        gain_steps = Steps(gather_gains(c, gains))
        tokens_rel = to_relative(tokens)
        left, right = tokens_rel[:, :half_width], tokens_rel[:, half_width:]
        left_sent = c.start(left, "tensor")
        ffn_split = [split(w, "core", 1) for w in (w_gate, w_up, w_down)]
        ffn_sent = c.start(columns([s[1] for s in ffn_split]), "core")
        gain_steps()

        attn_sent = c.sync(attn_sent)
        pair_width = 4 * head_width
        qk = Weight([s[0] for s in attn_split[:2]], attn_sent[:, :pair_width])
        vo = Weight([s[0] for s in attn_split[2:]], attn_sent[:, pair_width:])
        qk.start_line()
        gain_steps()
        ids = jnp.concatenate(
            [
                pick("tensor", segment_ids[:, :own_tokens], segment_ids[:, own_tokens:]),
                pick("tensor", segment_ids[:, own_tokens:], segment_ids[:, :own_tokens]),
            ],
            axis=1,
        )
        ids_sent = c.start(ids, "zl")
        right_sent = c.start(right, "zl")
        qk.end_line()
        gain_steps()
        qk.start_x(0)
        qk.start_high()
        vo.start_line()
        left = stack2(left, c.sync(left_sent))
        seq_ids = stack2(ids, c.sync(ids_sent))
        ids_sent = c.start(seq_ids, "core")
        right = stack2(right, c.sync(right_sent))

        def rows_second(left, right, between=None, last=None):
            left_sent = c.start(left, "zl")
            right_sent = c.start(right, "tensor")
            if between:
                between()
            left = stack2(left, c.sync(left_sent))
            right_sent = c.sync(right_sent)
            rows = own_tokens
            right = jnp.concatenate(
                [right[:rows], right_sent[:rows], right[rows:], right_sent[rows:]], axis=0
            )
            if last:
                last()
            left_sent = c.start(left, "core")
            right_sent = c.start(right, "core")
            return stack2(left, c.sync(left_sent)), stack2(right, c.sync(right_sent))

        def gather_rows(value, between=None, last=None):
            left, right = value[:, :half_width], value[:, half_width:]
            left_sent = c.start(left, "tensor")
            right_sent = c.start(right, "zl")
            left = stack2(left, c.sync(left_sent))
            right = stack2(right, c.sync(right_sent))
            return rows_second(left, right, between, last)

        ffn_sent = c.sync(ffn_sent)
        width = ffn_sent.shape[1] // 3
        gate_w, up_w, down_w = [
            Weight([s[0]], ffn_sent[:, i * width : (i + 1) * width])
            for i, s in enumerate(ffn_split)
        ]

        def tokens_between():
            vo.end_line()
            gate_w.start_line()
            gain_steps()
            qk.end_x(0)
            vo.start_x(0)

        def tokens_last():
            qk.end_high()
            qk.start_x(1)
            vo.start_high()

        in0, in1 = rows_second(left, right, tokens_between, tokens_last)
        seq_ids = stack2(seq_ids, c.sync(ids_sent))
        gate_w.end_line()
        gains = gain_steps.finish()
        qk.end_x(1)

        attn_scale = gains[2]
        ffn_scale = gains[3]
        head_gains = to_natural(gains[:2])
        head_start = (bit("tensor") * 4 + bit("core") * 2 + bit("zl")) * head_width
        head_gains = lax.dynamic_slice_in_dim(head_gains, head_start, head_width, axis=1)
        query_scale, key_scale = head_gains[0], head_gains[1]
        tokens_f = tokens_rel.astype(F32)
        d_out = to_relative(cotangent).astype(F32)
        places = jnp.arange(own_tokens)
        positions = jnp.concatenate(
            [places + bit("tensor") * own_tokens, places + (1 - bit("tensor")) * own_tokens]
        )
        visible = (positions[:, None] >= positions[None, :])[None] & (
            seq_ids[:, :, None] == seq_ids[:, None, :]
        )
        visible = visible[:, None]

        wqk0, wqk1 = qk.rows(0), qk.rows(1)
        projected = dot(in0, wqk0) + dot(in1, wqk1)
        query, key_proj = projected[:, :head_width], projected[:, head_width:]

        def squares_between():
            vo.end_high()
            vo.end_x(0)
            vo.start_x(1)
            gate_w.start_high()
            up_w.start_line()

        squares = pair_sum(
            c,
            jnp.stack([jnp.sum(query * query, axis=1), jnp.sum(key_proj * key_proj, axis=1)]),
            squares_between,
        )
        q_rms = lax.rsqrt(squares[0] / model_width + EPSILON)[:, None]
        k_rms = lax.rsqrt(squares[1] / model_width + EPSILON)[:, None]
        normed_query = (query * q_rms * query_scale).astype(BF)
        normed_key = (key_proj * k_rms * key_scale).astype(BF)
        gate_w.start_x(0)
        down_w.start_line()
        vo.end_x(1)
        normed_query, normed_key = c.sync(normed_query, normed_key)
        wvo0, wvo1 = vo.rows(0), vo.rows(1)
        wv0, wo0 = wvo0[:, :head_width], wvo0[:, head_width:]
        wv1, wo1 = wvo1[:, :head_width], wvo1[:, head_width:]
        value_bf = (dot(in0, wv0) + dot(in1, wv1)).astype(BF)
        heads = (4, seq_length, local_heads, HD)
        query_heads = normed_query.reshape(heads)
        key_heads = normed_key.reshape(heads)
        value_heads = value_bf.reshape(heads)
        scores = (
            jnp.einsum("bqhd,bkhd->bhqk", query_heads, key_heads, preferred_element_type=F32)
            * score_scale
        )
        scores = jnp.where(visible, scores, NEGATIVE)
        peak = jnp.max(scores, axis=-1, keepdims=True)
        expo = jnp.exp(scores - peak)
        total = jnp.sum(expo, axis=-1, keepdims=True)
        prob = expo / total
        prob_bf = prob.astype(BF)
        attn_heads = jnp.einsum(
            "bhqk,bkhd->bqhd", prob_bf, value_heads, preferred_element_type=F32
        ).astype(BF)
        attn = attn_heads.reshape(group_tokens, head_width)
        up_w.end_line()
        gate_w.end_x(0)
        up_w.start_x(0)
        down_w.end_line()
        gate_w.end_high()
        gate_w.start_x(1)
        up_w.start_high()

        def halve(total, axis):
            half = total.shape[0] // 2
            return total[:half], c.start(total[half:].astype(BF), axis)

        def added(pair):
            return pair[0] + c.sync(pair[1]).astype(F32)

        def cross(total):
            rows = own_tokens
            own = stack2(total[:rows], total[2 * rows : 3 * rows])
            sent = stack2(total[rows : 2 * rows], total[3 * rows :])
            return own, c.start(sent.astype(BF), "tensor")

        def scatter_rows(left_of, right_of, first=None, second=None):
            left_sent = c.start(left_of(other).astype(BF), "core")
            right_sent = c.start(right_of(other).astype(BF), "core")
            left = halve(left_of(own) + c.sync(left_sent).astype(F32), "zl")
            right = cross(right_of(own) + c.sync(right_sent).astype(F32))
            if first:
                first()
            left, right = added(left), added(right)
            left, right = halve(left, "tensor"), halve(right, "zl")
            if second:
                second()
            return added(left), added(right)

        def proj_second():
            up_w.end_x(0)
            up_w.end_high()
            gate_w.end_x(1)
            up_w.start_x(1)
            down_w.start_high()
            down_w.start_x(0)

        proj = columns(
            scatter_rows(
                lambda rows: dot_nt(attn[rows], wo0), lambda rows: dot_nt(attn[rows], wo1), None, proj_second
            )
        )
        attn_rms = rms_scale(proj)
        resid = tokens_f + proj * attn_rms * attn_scale

        def resid_last():
            up_w.end_x(1)
            down_w.end_high()
            down_w.end_x(0)
            down_w.start_x(1)

        h0, h1 = gather_rows(resid.astype(BF), None, resid_last)
        wg0, wg1 = gate_w.rows(0), gate_w.rows(1)
        gate = dot(h0, wg0) + dot(h1, wg1)
        sigma = jax.nn.sigmoid(gate)
        wu0, wu1 = up_w.rows(0), up_w.rows(1)
        up = dot(h0, wu0) + dot(h1, wu1)
        act = (gate * sigma * up).astype(BF)

        wd0 = down_w.rows(0)
        first_rows = down_w.blocks[1][0]
        left, right = scatter_rows(
            lambda rows: dot_nt(act[rows], wd0), lambda rows: dot_nt(act[rows], first_rows)
        )
        down_w.end_x(1)
        last_rows = down_w.blocks[1][1]
        sent = c.start(dot_nt(act[other], last_rows).astype(BF), "core")
        last = cross(dot_nt(act[own], last_rows) + c.sync(sent).astype(F32))
        last = halve(added(last), "zl")
        ffn = columns([left, right, added(last)])
        wd1 = down_w.rows(1)

        ffn_rms = rms_scale(ffn)
        output = to_natural((resid + ffn * ffn_rms * ffn_scale).astype(BF))
        ffn_gain_term = jnp.sum(d_out * ffn * ffn_rms, axis=0)
        scaled_out = d_out * ffn_scale
        d_ffn = (
            ffn_rms
            * (
                scaled_out
                - ffn * ffn_rms * ffn_rms * jnp.mean(scaled_out * ffn, axis=1, keepdims=True)
            )
        ).astype(BF)
        f0, f1 = gather_rows(d_ffn)

        class Grad:
            def __init__(self, *terms):
                self.terms = terms
                self.x, self.total = [None, None], [None, None]

            def product(self, side, block):
                cols = slice(block * block_width, (block + 1) * block_width)
                return columns([dot_tn(halves[side][:, cols], r) for halves, r in self.terms])

            def start_x(self, block):
                self.x[block] = c.start(self.product(1, block).astype(BF), "x")

            def end_x(self, block):
                moved = c.sync(self.x[block])
                self.total[block] = self.product(0, block) + moved.astype(F32)

            def start_high(self):
                self.high = c.start(self.total[1].astype(BF), high_bits[0])

            def end_high(self):
                total = self.total[0] + c.sync(self.high).astype(F32)
                for name in high_bits[1:]:
                    total = added(halve(total, name))
                self.own, self.sent = split(total, "zl", 0)

            def start_line(self):
                self.line = c.start(self.sent.astype(BF), "zl")

            def joined(self, axis, moved, low=None):
                width = moved.shape[1] // len(self.terms)
                cols = [slice(i * width, (i + 1) * width) for i in range(len(self.terms))]
                if low is None:
                    return [ordered(axis, self.own[:, s], moved[:, s], dim=1) for s in cols]
                pairs = [(self.own[:, s], moved[:, s]) for s in cols]
                return [columns([jnp.where(low, a, b), jnp.where(low, b, a)]) for a, b in pairs]

            def end_line(self):
                moved = c.sync(self.line).astype(F32)
                self.own, sent = split(columns(self.joined("zl", moved)), "core", 0)
                self.core = c.start(sent.astype(BF), "core")

            def end(self):
                moved = c.sync(self.core).astype(F32)
                self.results = self.joined("core", moved, c.token[0, 0] == 0)

        down_grad = Grad(((f0, f1), act))
        down_grad.start_x(1)
        down_grad.start_x(0)
        f0, f1 = c.fence(f0, f1)
        d_act = dot(f0, wd0) + dot(f1, wd1)
        d_gate = (d_act * up * sigma * (1.0 + gate * (1.0 - sigma))).astype(BF)
        d_up = (d_act * gate * sigma).astype(BF)
        gate_grad = Grad(((h0, h1), d_gate))
        up_grad = Grad(((h0, h1), d_up))
        down_grad.end_x(1)
        down_grad.start_high()
        gate_grad.start_x(1)
        d_gate, d_up = c.fence(d_gate, d_up)

        def hidden_first():
            down_grad.end_x(0)
            gate_grad.start_x(0)

        def hidden_second():
            gate_grad.end_x(1)
            up_grad.start_x(1)
            down_grad.end_high()
            gate_grad.start_high()

        d_resid = d_out + columns(
            scatter_rows(
                lambda rows: dot_nt(d_gate[rows], wg0) + dot_nt(d_up[rows], wu0),
                lambda rows: dot_nt(d_gate[rows], wg1) + dot_nt(d_up[rows], wu1),
                hidden_first,
                hidden_second,
            )
        )
        attn_gain_term = jnp.sum(d_resid * proj * attn_rms, axis=0)
        scaled_resid = d_resid * attn_scale
        d_proj = (
            attn_rms
            * (
                scaled_resid
                - proj * attn_rms * attn_rms * jnp.mean(scaled_resid * proj, axis=1, keepdims=True)
            )
        ).astype(BF)

        def proj_between():
            down_grad.start_line()
            gate_grad.end_x(0)
            up_grad.start_x(0)

        def proj_last():
            up_grad.end_x(1)
            gate_grad.end_high()
            up_grad.start_high()
            gate_grad.start_line()

        p0, p1 = gather_rows(d_proj, proj_between, proj_last)
        up_grad.end_x(0)
        down_grad.end_line()
        p0, p1 = c.fence(p0, p1)
        d_attn = (dot(p0, wo0) + dot(p1, wo1)).astype(BF)

        d_attn_heads = d_attn.reshape(heads)
        d_value = (
            jnp.einsum("bhqk,bqhd->bkhd", prob_bf, d_attn_heads, preferred_element_type=F32)
            .reshape(group_tokens, head_width)
            .astype(BF)
        )
        d_prob = jnp.einsum(
            "bqhd,bkhd->bhqk", d_attn_heads, value_heads, preferred_element_type=F32
        )
        delta = jnp.einsum(
            "bqhd,bqhd->bhq", d_attn_heads, attn.reshape(heads), preferred_element_type=F32
        )[..., None]
        d_score = (prob * (d_prob - delta)).astype(BF)
        d_nq = (
            jnp.einsum("bhqk,bkhd->bqhd", d_score, key_heads, preferred_element_type=F32).reshape(
                group_tokens, head_width
            )
            * score_scale
        )
        d_nk = (
            jnp.einsum("bhqk,bqhd->bkhd", d_score, query_heads, preferred_element_type=F32).reshape(
                group_tokens, head_width
            )
            * score_scale
        )
        query_gain_term = jnp.sum(d_nq * query * q_rms, axis=0)
        key_gain_term = jnp.sum(d_nk * key_proj * k_rms, axis=0)
        scaled_q = d_nq * query_scale
        scaled_k = d_nk * key_scale
        zero = jnp.zeros((2, model_width), F32)
        placed = lax.dynamic_update_slice_in_dim(
            zero, jnp.stack([query_gain_term, key_gain_term]), head_start + c.zero, 1
        )
        gain_parts = jnp.concatenate(
            [to_relative(placed), jnp.stack([attn_gain_term, ffn_gain_term])], axis=0
        )
        gain_steps = Steps(scatter_gains(c, gain_parts))
        gate_grad.end_line()
        ov_grad = Grad(((p0, p1), attn), ((in0, in1), d_value))
        ov_grad.start_x(1)
        up_grad.end_high()
        down_grad.end()
        inner = pair_sum(
            c, jnp.stack([jnp.sum(scaled_q * query, axis=1), jnp.sum(scaled_k * key_proj, axis=1)])
        )
        gain_steps()
        d_query = (
            q_rms * (scaled_q - query * q_rms * q_rms * (inner[0] / model_width)[:, None])
        ).astype(BF)
        d_key = (
            k_rms * (scaled_k - key_proj * k_rms * k_rms * (inner[1] / model_width)[:, None])
        ).astype(BF)
        d_qk = columns([d_query, d_key])
        qk_grad = Grad(((in0, in1), d_query), ((in0, in1), d_key))
        ov_grad.end_x(1)
        ov_grad.start_high()
        qk_grad.start_x(1)
        ov_grad.start_x(0)
        gate_grad.end()

        def tokens_first():
            up_grad.start_line()
            qk_grad.end_x(1)
            qk_grad.start_x(0)

        def tokens_second():
            gain_steps()
            ov_grad.end_x(0)
            ov_grad.end_high()
            qk_grad.start_high()

        d_tokens = columns(
            scatter_rows(
                lambda rows: dot_nt(d_qk[rows], wqk0) + dot_nt(d_value[rows], wv0),
                lambda rows: dot_nt(d_qk[rows], wqk1) + dot_nt(d_value[rows], wv1),
                tokens_first,
                tokens_second,
            )
        )
        grad_tokens = to_natural(d_resid + d_tokens)
        gain_steps()
        up_grad.end_line()
        ov_grad.start_line()
        qk_grad.end_x(0)
        gain_steps()
        up_grad.end()
        gain_parts = gain_steps.finish()
        ov_grad.end_line()
        qk_grad.end_high()
        qk_grad.start_line()
        ov_grad.end()
        qk_grad.end_line()
        qk_grad.end()
        grad_output, grad_value = ov_grad.results
        grad_query, grad_key = qk_grad.results
        return (
            output,
            grad_tokens,
            grad_query,
            grad_key,
            grad_value,
            grad_output,
            gate_grad.results[0],
            up_grad.results[0],
            down_grad.results[0],
            gain_parts[0],
            gain_parts[1],
            gain_parts[2],
            gain_parts[3],
        )

    return shards


def solution(mesh):
    dp = mesh.shape["dp"]
    high = max(dp.bit_length() - 4, 0)
    high_bits = tuple(f"z{i}" for i in range(high))
    names = high_bits + ("zl", "x", "core", "tensor")
    fine = Mesh(mesh.devices.reshape((2,) * len(names)), names)
    rows = names[:-1]
    both = names
    mapped = jax.shard_map(
        build(high_bits),
        mesh=fine,
        in_specs=(
            P(both, None),
            P(rows, None),
            P(rows, "tensor"),
            P(rows, "tensor"),
            P(rows, "tensor"),
            P(rows, "tensor"),
            P(rows, "tensor"),
            P(rows, "tensor"),
            P(rows, "tensor"),
            P(both),
            P(both),
            P(both),
            P(both),
            P(both, None),
        ),
        out_specs=(
            P(both, None),
            P(both, None),
            P(rows, "tensor"),
            P(rows, "tensor"),
            P(rows, "tensor"),
            P(rows, "tensor"),
            P(rows, "tensor"),
            P(rows, "tensor"),
            P(rows, "tensor"),
            P(both),
            P(both),
            P(both),
            P(both),
        ),
        check_vma=False,
    )
    return mapped
```

```python
import math

import jax
import jax.numpy as jnp
from jax import lax
from jax.sharding import Mesh, PartitionSpec as P

HD = 128

EPSILON = 1e-06
NEGATIVE = -1e30
FLIP = [(0, 1), (1, 0)]
BF = jnp.bfloat16
F32 = jnp.float32


def swap(value, axis):
    return lax.ppermute(value, axis, FLIP)


def bit(axis):
    return lax.axis_index(axis)


def pick(axis, low, high):
    return jnp.where(bit(axis) == 0, low, high)


def ordered(axis, own, other, dim=0):
    return jnp.concatenate([pick(axis, own, other), pick(axis, other, own)], axis=dim)


def split(value, axis, dim):
    half = value.shape[dim] // 2
    low = lax.slice_in_dim(value, 0, half, axis=dim)
    high = lax.slice_in_dim(value, half, 2 * half, axis=dim)
    return pick(axis, low, high), pick(axis, high, low)


def dot(a, b):
    return jnp.dot(a, b, preferred_element_type=F32)


def dot_nt(a, b):
    return jnp.einsum("sc,rc->sr", a, b, preferred_element_type=F32)


def dot_tn(a, b):
    return jnp.einsum("sr,sc->rc", a, b, preferred_element_type=F32)


def rms_scale(values):
    return lax.rsqrt(jnp.mean(values * values, axis=1, keepdims=True) + EPSILON)


def build(high_bits):
    def to_relative(value):
        rows, width = value.shape
        count = 2 ** (len(high_bits) + 2)
        run = width // count
        pieces = [value[:, i * run : (i + 1) * run] for i in range(count)]
        names = list(high_bits) + ["zl", "x"]
        for position, name in enumerate(names):
            if name == "zl":
                continue
            mask = 1 << (len(names) - 1 - position)
            pieces = [pick(name, pieces[i], pieces[i ^ mask]) for i in range(count)]
        order = []
        for xr in range(2):
            for rest in range(count // 2):
                order.append(rest * 2 + xr)
        return jnp.concatenate([pieces[i] for i in order], axis=1)

    def to_natural(value):
        rows, width = value.shape
        count = 2 ** (len(high_bits) + 2)
        run = width // count
        moved = [value[:, i * run : (i + 1) * run] for i in range(count)]
        pieces = [None] * count
        place = 0
        for xr in range(2):
            for rest in range(count // 2):
                pieces[rest * 2 + xr] = moved[place]
                place += 1
        names = list(high_bits) + ["zl", "x"]
        for position, name in enumerate(names):
            if name == "zl":
                continue
            mask = 1 << (len(names) - 1 - position)
            pieces = [pick(name, pieces[i], pieces[i ^ mask]) for i in range(count)]
        return jnp.concatenate(pieces, axis=1)

    class Chain:
        def __init__(self, token):
            self.token = token
            self.zero = jnp.int32(0)

        def sync(self, *values):
            out = lax.optimization_barrier((self.token,) + values)
            self.token = out[0]
            return out[1] if len(values) == 1 else out[1:]

        def start(self, value, axis):
            return swap(self.sync(value), axis)

        def fence(self, *values):
            moved = self.sync(self.start(jnp.full((1, HD), bit("core"), jnp.int32), "core"))
            self.zero = self.zero + (moved[0, 0] + bit("core") - 1)
            return self.sync(*values)

    def gather_gains(c, gains):
        for name in ("tensor", "core", "zl"):
            sent = c.start(gains, name)
            yield
            gains = ordered(name, gains, c.sync(sent), dim=1)
        for name in list(high_bits)[::-1] + ["x"]:
            sent = c.start(gains, name)
            yield
            gains = jnp.concatenate([gains, c.sync(sent)], axis=1)
        return gains

    def pair_sum(c, values, between=None):
        count, width = values.shape
        for level, axis in ((1, "zl"), (2, "tensor"), (0, "core")):
            run = width >> (level + 1)
            other = c.sync(c.start(values, axis))
            blocks = [other[:, i * run : (i + 1) * run] for i in range(width // run)]
            values = values + jnp.concatenate([blocks[i ^ 1] for i in range(len(blocks))], axis=1)
            if between and axis == "zl":
                between()
        return values

    def scatter_gains(c, gains):
        for name in ["x"] + list(high_bits):
            half = gains.shape[1] // 2
            sent = c.start(gains[:, half:], name)
            yield
            gains = gains[:, :half] + c.sync(sent)
        for name in ("zl", "core", "tensor"):
            own, sent = split(gains, name, 1)
            sent = c.start(sent, name)
            yield
            gains = own + c.sync(sent)
        return gains

    class Steps:
        def __init__(self, stages):
            self.stages, self.done = stages, False
            self()

        def __call__(self):
            if not self.done:
                try:
                    next(self.stages)
                except StopIteration as end:
                    self.value, self.done = end.value, True

        def finish(self):
            while not self.done:
                self()
            return self.value

    def stack2(low, high):
        return jnp.concatenate([low, high], axis=0)

    def shards(
        tokens,
        segment_ids,
        w_query,
        w_key,
        w_value,
        w_output,
        w_gate,
        w_up,
        w_down,
        query_gain,
        key_gain,
        attn_gain,
        ffn_gain,
        cotangent,
    ):
        own_tokens, model_width = tokens.shape
        half_width = model_width // 2
        block_width = half_width // 2
        seq_length = own_tokens * 2
        core_tokens = seq_length * 2
        group_tokens = core_tokens * 2
        head_width = w_query.shape[1] // 4
        local_heads = head_width // HD
        score_scale = 1.0 / math.sqrt(HD)
        own, other = slice(0, core_tokens), slice(core_tokens, group_tokens)
        c = Chain(jnp.full((1, HD), bit("core"), jnp.int32))

        def columns(parts):
            return parts[0] if len(parts) == 1 else jnp.concatenate(parts, axis=1)

        class Weight:
            def __init__(self, matrices, sent):
                width = sent.shape[1] // len(matrices)
                pairs = [
                    split(ordered("core", m, sent[:, i * width : (i + 1) * width]), "zl", 1)
                    for i, m in enumerate(matrices)
                ]
                self.own = columns([p[0] for p in pairs])
                self.sent = columns([p[1] for p in pairs])
                self.blocks = [[None, None], [None, None]]

            def start_line(self):
                self.line = c.start(self.sent, "zl")

            def end_line(self):
                rows = ordered("zl", self.own, c.sync(self.line))
                for name in high_bits[:0:-1]:
                    rows = stack2(rows, c.sync(c.start(rows, name)))
                self.blocks[0][0] = rows

            def start_high(self):
                self.high = c.start(self.blocks[0][0], high_bits[0])

            def end_high(self):
                self.blocks[0][1] = c.sync(self.high)

            def start_x(self, block):
                self.blocks[1][block] = c.start(self.blocks[0][block], "x")

            def end_x(self, block):
                self.blocks[1][block] = c.sync(self.blocks[1][block])

            def rows(self, side):
                return stack2(*self.blocks[side])

        attn_split = [split(w, "core", 1) for w in (w_query, w_key, w_value, w_output)]
        attn_sent = c.start(columns([s[1] for s in attn_split]), "core")
        gains = jnp.stack([query_gain, key_gain, attn_gain, ffn_gain])
        gain_steps = Steps(gather_gains(c, gains))
        tokens_rel = to_relative(tokens)
        left, right = tokens_rel[:, :half_width], tokens_rel[:, half_width:]
        left_sent = c.start(left, "tensor")
        ffn_split = [split(w, "core", 1) for w in (w_gate, w_up, w_down)]
        ffn_sent = c.start(columns([s[1] for s in ffn_split]), "core")
        gain_steps()

        attn_sent = c.sync(attn_sent)
        pair_width = 4 * head_width
        qk = Weight([s[0] for s in attn_split[:2]], attn_sent[:, :pair_width])
        vo = Weight([s[0] for s in attn_split[2:]], attn_sent[:, pair_width:])
        qk.start_line()
        gain_steps()
        ids = jnp.concatenate(
            [
                pick("tensor", segment_ids[:, :own_tokens], segment_ids[:, own_tokens:]),
                pick("tensor", segment_ids[:, own_tokens:], segment_ids[:, :own_tokens]),
            ],
            axis=1,
        )
        ids_sent = c.start(ids, "zl")
        qk.end_line()
        gain_steps()
        qk.start_x(0)
        qk.start_high()
        right_sent = c.start(right, "zl")
        vo.start_line()
        left = stack2(left, c.sync(left_sent))
        seq_ids = stack2(ids, c.sync(ids_sent))
        ids_sent = c.start(seq_ids, "core")
        right = stack2(right, c.sync(right_sent))

        def rows_second(left, right, between=None, last=None):
            left_sent = c.start(left, "zl")
            right_sent = c.start(right, "tensor")
            if between:
                between()
            left = stack2(left, c.sync(left_sent))
            right_sent = c.sync(right_sent)
            rows = own_tokens
            right = jnp.concatenate(
                [right[:rows], right_sent[:rows], right[rows:], right_sent[rows:]], axis=0
            )
            if last:
                last()
            left_sent = c.start(left, "core")
            right_sent = c.start(right, "core")
            return stack2(left, c.sync(left_sent)), stack2(right, c.sync(right_sent))

        def gather_rows(value, between=None, last=None):
            left, right = value[:, :half_width], value[:, half_width:]
            left_sent = c.start(left, "tensor")
            right_sent = c.start(right, "zl")
            left = stack2(left, c.sync(left_sent))
            right = stack2(right, c.sync(right_sent))
            return rows_second(left, right, between, last)

        ffn_sent = c.sync(ffn_sent)
        width = ffn_sent.shape[1] // 3
        gate_w, up_w, down_w = [
            Weight([s[0]], ffn_sent[:, i * width : (i + 1) * width])
            for i, s in enumerate(ffn_split)
        ]

        def tokens_between():
            vo.end_line()
            gate_w.start_line()
            gain_steps()
            qk.end_x(0)
            vo.start_x(0)
            qk.end_high()
            qk.start_x(1)
            vo.start_high()

        in0, in1 = rows_second(left, right, tokens_between)
        seq_ids = stack2(seq_ids, c.sync(ids_sent))
        gate_w.end_line()
        gains = gain_steps.finish()
        qk.end_x(1)

        attn_scale = gains[2]
        ffn_scale = gains[3]
        head_gains = to_natural(gains[:2])
        head_start = (bit("tensor") * 4 + bit("core") * 2 + bit("zl")) * head_width
        head_gains = lax.dynamic_slice_in_dim(head_gains, head_start, head_width, axis=1)
        query_scale, key_scale = head_gains[0], head_gains[1]
        tokens_f = tokens_rel.astype(F32)
        d_out = to_relative(cotangent).astype(F32)
        places = jnp.arange(own_tokens)
        positions = jnp.concatenate(
            [places + bit("tensor") * own_tokens, places + (1 - bit("tensor")) * own_tokens]
        )
        visible = (positions[:, None] >= positions[None, :])[None] & (
            seq_ids[:, :, None] == seq_ids[:, None, :]
        )
        visible = visible[:, None]

        wqk0, wqk1 = qk.rows(0), qk.rows(1)
        projected = dot(in0, wqk0) + dot(in1, wqk1)
        query, key_proj = projected[:, :head_width], projected[:, head_width:]

        def squares_between():
            vo.end_high()
            vo.end_x(0)
            vo.start_x(1)
            gate_w.start_high()
            up_w.start_line()

        squares = pair_sum(
            c,
            jnp.stack([jnp.sum(query * query, axis=1), jnp.sum(key_proj * key_proj, axis=1)]),
            squares_between,
        )
        q_rms = lax.rsqrt(squares[0] / model_width + EPSILON)[:, None]
        k_rms = lax.rsqrt(squares[1] / model_width + EPSILON)[:, None]
        normed_query = (query * q_rms * query_scale).astype(BF)
        normed_key = (key_proj * k_rms * key_scale).astype(BF)
        gate_w.start_x(0)
        down_w.start_line()
        vo.end_x(1)
        normed_query, normed_key = c.sync(normed_query, normed_key)
        wvo0, wvo1 = vo.rows(0), vo.rows(1)
        wv0, wo0 = wvo0[:, :head_width], wvo0[:, head_width:]
        wv1, wo1 = wvo1[:, :head_width], wvo1[:, head_width:]
        value_bf = (dot(in0, wv0) + dot(in1, wv1)).astype(BF)
        heads = (4, seq_length, local_heads, HD)
        query_heads = normed_query.reshape(heads)
        key_heads = normed_key.reshape(heads)
        value_heads = value_bf.reshape(heads)
        scores = (
            jnp.einsum("bqhd,bkhd->bhqk", query_heads, key_heads, preferred_element_type=F32)
            * score_scale
        )
        scores = jnp.where(visible, scores, NEGATIVE)
        peak = jnp.max(scores, axis=-1, keepdims=True)
        expo = jnp.exp(scores - peak)
        total = jnp.sum(expo, axis=-1, keepdims=True)
        prob = expo / total
        prob_bf = prob.astype(BF)
        attn_heads = jnp.einsum(
            "bhqk,bkhd->bqhd", prob_bf, value_heads, preferred_element_type=F32
        ).astype(BF)
        attn = attn_heads.reshape(group_tokens, head_width)
        attn = c.sync(attn)
        up_w.end_line()
        gate_w.end_x(0)
        up_w.start_x(0)
        down_w.end_line()
        gate_w.end_high()
        gate_w.start_x(1)
        up_w.start_high()

        def halve(total, axis):
            half = total.shape[0] // 2
            return total[:half], c.start(total[half:].astype(BF), axis)

        def added(pair):
            return pair[0] + c.sync(pair[1]).astype(F32)

        def cross(total):
            rows = own_tokens
            own = stack2(total[:rows], total[2 * rows : 3 * rows])
            sent = stack2(total[rows : 2 * rows], total[3 * rows :])
            return own, c.start(sent.astype(BF), "tensor")

        def scatter_rows(left_of, right_of, first=None, second=None):
            left_sent = c.start(left_of(other).astype(BF), "core")
            right_sent = c.start(right_of(other).astype(BF), "core")
            left = halve(left_of(own) + c.sync(left_sent).astype(F32), "zl")
            right = cross(right_of(own) + c.sync(right_sent).astype(F32))
            if first:
                first()
            left, right = added(left), added(right)
            left, right = halve(left, "tensor"), halve(right, "zl")
            if second:
                second()
            return added(left), added(right)

        def proj_second():
            up_w.end_x(0)
            up_w.end_high()
            gate_w.end_x(1)
            up_w.start_x(1)
            down_w.start_high()
            down_w.start_x(0)

        proj = columns(
            scatter_rows(
                lambda rows: dot_nt(attn[rows], wo0), lambda rows: dot_nt(attn[rows], wo1), None, proj_second
            )
        )
        attn_rms = rms_scale(proj)
        resid = tokens_f + proj * attn_rms * attn_scale

        def resid_last():
            up_w.end_x(1)
            down_w.end_high()
            down_w.end_x(0)
            down_w.start_x(1)

        h0, h1 = gather_rows(resid.astype(BF), None, resid_last)
        wg0, wg1 = gate_w.rows(0), gate_w.rows(1)
        gate = dot(h0, wg0) + dot(h1, wg1)
        sigma = jax.nn.sigmoid(gate)
        wu0, wu1 = up_w.rows(0), up_w.rows(1)
        up = dot(h0, wu0) + dot(h1, wu1)
        act = (gate * sigma * up).astype(BF)

        wd0 = down_w.rows(0)
        first_rows = down_w.blocks[1][0]
        left, right = scatter_rows(
            lambda rows: dot_nt(act[rows], wd0), lambda rows: dot_nt(act[rows], first_rows)
        )
        down_w.end_x(1)
        last_rows = down_w.blocks[1][1]
        sent = c.start(dot_nt(act[other], last_rows).astype(BF), "core")
        last = cross(dot_nt(act[own], last_rows) + c.sync(sent).astype(F32))
        last = halve(added(last), "zl")
        ffn = columns([left, right, added(last)])
        wd1 = down_w.rows(1)

        ffn_rms = rms_scale(ffn)
        output = to_natural((resid + ffn * ffn_rms * ffn_scale).astype(BF))
        ffn_gain_term = jnp.sum(d_out * ffn * ffn_rms, axis=0)
        scaled_out = d_out * ffn_scale
        d_ffn = (
            ffn_rms
            * (
                scaled_out
                - ffn * ffn_rms * ffn_rms * jnp.mean(scaled_out * ffn, axis=1, keepdims=True)
            )
        ).astype(BF)
        f0, f1 = gather_rows(d_ffn)

        class Grad:
            def __init__(self, *terms):
                self.terms = terms
                self.x, self.total = [None, None], [None, None]

            def product(self, side, block):
                cols = slice(block * block_width, (block + 1) * block_width)
                return columns([dot_tn(halves[side][:, cols], r) for halves, r in self.terms])

            def start_x(self, block):
                self.x[block] = c.start(self.product(1, block).astype(BF), "x")

            def end_x(self, block):
                moved = c.sync(self.x[block])
                self.total[block] = self.product(0, block) + moved.astype(F32)

            def start_high(self):
                self.high = c.start(self.total[1].astype(BF), high_bits[0])

            def end_high(self):
                total = self.total[0] + c.sync(self.high).astype(F32)
                for name in high_bits[1:]:
                    total = added(halve(total, name))
                self.own, self.sent = split(total, "zl", 0)

            def start_line(self):
                self.line = c.start(self.sent.astype(BF), "zl")

            def joined(self, axis, moved, low=None):
                width = moved.shape[1] // len(self.terms)
                cols = [slice(i * width, (i + 1) * width) for i in range(len(self.terms))]
                if low is None:
                    return [ordered(axis, self.own[:, s], moved[:, s], dim=1) for s in cols]
                pairs = [(self.own[:, s], moved[:, s]) for s in cols]
                return [columns([jnp.where(low, a, b), jnp.where(low, b, a)]) for a, b in pairs]

            def end_line(self):
                moved = c.sync(self.line).astype(F32)
                self.own, sent = split(columns(self.joined("zl", moved)), "core", 0)
                self.core = c.start(sent.astype(BF), "core")

            def end(self):
                moved = c.sync(self.core).astype(F32)
                self.results = self.joined("core", moved, c.token[0, 0] == 0)

        down_grad = Grad(((f0, f1), act))
        down_grad.start_x(1)
        down_grad.start_x(0)
        f0, f1 = c.fence(f0, f1)
        d_act = dot(f0, wd0) + dot(f1, wd1)
        d_gate = (d_act * up * sigma * (1.0 + gate * (1.0 - sigma))).astype(BF)
        d_up = (d_act * gate * sigma).astype(BF)
        gate_grad = Grad(((h0, h1), d_gate))
        up_grad = Grad(((h0, h1), d_up))
        down_grad.end_x(1)
        down_grad.start_high()
        gate_grad.start_x(1)
        d_gate, d_up = c.fence(d_gate, d_up)

        def hidden_first():
            down_grad.end_x(0)
            gate_grad.start_x(0)

        def hidden_second():
            gate_grad.end_x(1)
            up_grad.start_x(1)
            down_grad.end_high()
            gate_grad.start_high()

        d_resid = d_out + columns(
            scatter_rows(
                lambda rows: dot_nt(d_gate[rows], wg0) + dot_nt(d_up[rows], wu0),
                lambda rows: dot_nt(d_gate[rows], wg1) + dot_nt(d_up[rows], wu1),
                hidden_first,
                hidden_second,
            )
        )
        attn_gain_term = jnp.sum(d_resid * proj * attn_rms, axis=0)
        scaled_resid = d_resid * attn_scale
        d_proj = (
            attn_rms
            * (
                scaled_resid
                - proj * attn_rms * attn_rms * jnp.mean(scaled_resid * proj, axis=1, keepdims=True)
            )
        ).astype(BF)

        def proj_between():
            down_grad.start_line()
            gate_grad.end_x(0)
            up_grad.start_x(0)

        def proj_last():
            up_grad.end_x(1)
            gate_grad.end_high()
            up_grad.start_high()
            gate_grad.start_line()

        p0, p1 = gather_rows(d_proj, proj_between, proj_last)
        up_grad.end_x(0)
        d_attn = (dot(p0, wo0) + dot(p1, wo1)).astype(BF)

        d_attn_heads = d_attn.reshape(heads)
        d_value = (
            jnp.einsum("bhqk,bqhd->bkhd", prob_bf, d_attn_heads, preferred_element_type=F32)
            .reshape(group_tokens, head_width)
            .astype(BF)
        )
        ov_grad = Grad(((p0, p1), attn), ((in0, in1), d_value))
        ov_grad.start_x(1)
        d_attn = c.fence(d_attn)
        d_attn_heads = d_attn.reshape(heads)
        d_prob = jnp.einsum(
            "bqhd,bkhd->bhqk", d_attn_heads, value_heads, preferred_element_type=F32
        )
        delta = jnp.einsum(
            "bqhd,bqhd->bhq", d_attn_heads, attn.reshape(heads), preferred_element_type=F32
        )[..., None]
        d_score = (prob * (d_prob - delta)).astype(BF)
        d_nq = (
            jnp.einsum("bhqk,bkhd->bqhd", d_score, key_heads, preferred_element_type=F32).reshape(
                group_tokens, head_width
            )
            * score_scale
        )
        d_nk = (
            jnp.einsum("bhqk,bqhd->bkhd", d_score, query_heads, preferred_element_type=F32).reshape(
                group_tokens, head_width
            )
            * score_scale
        )
        query_gain_term = jnp.sum(d_nq * query * q_rms, axis=0)
        key_gain_term = jnp.sum(d_nk * key_proj * k_rms, axis=0)
        scaled_q = d_nq * query_scale
        scaled_k = d_nk * key_scale
        zero = jnp.zeros((2, model_width), F32)
        placed = lax.dynamic_update_slice_in_dim(
            zero, jnp.stack([query_gain_term, key_gain_term]), head_start + c.zero, 1
        )
        gain_parts = jnp.concatenate(
            [to_relative(placed), jnp.stack([attn_gain_term, ffn_gain_term])], axis=0
        )
        gain_steps = Steps(scatter_gains(c, gain_parts))
        inner = c.sync(
            jnp.stack([jnp.sum(scaled_q * query, axis=1), jnp.sum(scaled_k * key_proj, axis=1)])
        )
        up_grad.end_high()
        ov_grad.end_x(1)
        ov_grad.start_high()
        down_grad.end_line()
        inner = pair_sum(c, inner)
        gain_steps()
        d_query = (
            q_rms * (scaled_q - query * q_rms * q_rms * (inner[0] / model_width)[:, None])
        ).astype(BF)
        d_key = (
            k_rms * (scaled_k - key_proj * k_rms * k_rms * (inner[1] / model_width)[:, None])
        ).astype(BF)
        d_qk = columns([d_query, d_key])
        qk_grad = Grad(((in0, in1), d_query), ((in0, in1), d_key))
        qk_grad.start_x(1)
        gate_grad.end_line()
        down_grad.end()
        ov_grad.start_x(0)

        def tokens_first():
            ov_grad.end_x(0)
            ov_grad.end_high()
            qk_grad.end_x(1)
            qk_grad.start_high()
            qk_grad.start_x(0)

        def tokens_second():
            gain_steps()
            up_grad.start_line()
            gate_grad.end()

        d_tokens = columns(
            scatter_rows(
                lambda rows: dot_nt(d_qk[rows], wqk0) + dot_nt(d_value[rows], wv0),
                lambda rows: dot_nt(d_qk[rows], wqk1) + dot_nt(d_value[rows], wv1),
                tokens_first,
                tokens_second,
            )
        )
        grad_tokens = to_natural(d_resid + d_tokens)
        gain_steps()
        ov_grad.start_line()
        up_grad.end_line()
        gain_steps()
        qk_grad.end_x(0)
        ov_grad.end_line()
        gain_parts = gain_steps.finish()
        qk_grad.end_high()
        qk_grad.start_line()
        up_grad.end()
        ov_grad.end()
        qk_grad.end_line()
        qk_grad.end()
        grad_output, grad_value = ov_grad.results
        grad_query, grad_key = qk_grad.results
        return (
            output,
            grad_tokens,
            grad_query,
            grad_key,
            grad_value,
            grad_output,
            gate_grad.results[0],
            up_grad.results[0],
            down_grad.results[0],
            gain_parts[0],
            gain_parts[1],
            gain_parts[2],
            gain_parts[3],
        )

    return shards


def solution(mesh):
    dp = mesh.shape["dp"]
    high = max(dp.bit_length() - 4, 0)
    high_bits = tuple(f"z{i}" for i in range(high))
    names = high_bits + ("zl", "x", "core", "tensor")
    fine = Mesh(mesh.devices.reshape((2,) * len(names)), names)
    rows = names[:-1]
    both = names
    mapped = jax.shard_map(
        build(high_bits),
        mesh=fine,
        in_specs=(
            P(both, None),
            P(rows, None),
            P(rows, "tensor"),
            P(rows, "tensor"),
            P(rows, "tensor"),
            P(rows, "tensor"),
            P(rows, "tensor"),
            P(rows, "tensor"),
            P(rows, "tensor"),
            P(both),
            P(both),
            P(both),
            P(both),
            P(both, None),
        ),
        out_specs=(
            P(both, None),
            P(both, None),
            P(rows, "tensor"),
            P(rows, "tensor"),
            P(rows, "tensor"),
            P(rows, "tensor"),
            P(rows, "tensor"),
            P(rows, "tensor"),
            P(rows, "tensor"),
            P(both),
            P(both),
            P(both),
            P(both),
        ),
        check_vma=False,
    )
    return mapped
```

```python
import math

import jax
import jax.numpy as jnp
from jax import lax
from jax.sharding import Mesh, PartitionSpec as P

HD = 128

EPSILON = 1e-06
NEGATIVE = -1e30
FLIP = [(0, 1), (1, 0)]
BF = jnp.bfloat16
F32 = jnp.float32


def swap(value, axis):
    return lax.ppermute(value, axis, FLIP)


def bit(axis):
    return lax.axis_index(axis)


def pick(axis, low, high):
    return jnp.where(bit(axis) == 0, low, high)


def ordered(axis, own, other, dim=0):
    return jnp.concatenate([pick(axis, own, other), pick(axis, other, own)], axis=dim)


def split(value, axis, dim):
    half = value.shape[dim] // 2
    low = lax.slice_in_dim(value, 0, half, axis=dim)
    high = lax.slice_in_dim(value, half, 2 * half, axis=dim)
    return pick(axis, low, high), pick(axis, high, low)


def dot(a, b):
    return jnp.dot(a, b, preferred_element_type=F32)


def dot_nt(a, b):
    return jnp.einsum("sc,rc->sr", a, b, preferred_element_type=F32)


def dot_tn(a, b):
    return jnp.einsum("sr,sc->rc", a, b, preferred_element_type=F32)


def rms_scale(values):
    return lax.rsqrt(jnp.mean(values * values, axis=1, keepdims=True) + EPSILON)


def build(high_bits):
    def to_relative(value):
        rows, width = value.shape
        count = 2 ** (len(high_bits) + 2)
        run = width // count
        pieces = [value[:, i * run : (i + 1) * run] for i in range(count)]
        names = list(high_bits) + ["zl", "x"]
        for position, name in enumerate(names):
            if name == "zl":
                continue
            mask = 1 << (len(names) - 1 - position)
            pieces = [pick(name, pieces[i], pieces[i ^ mask]) for i in range(count)]
        order = []
        for xr in range(2):
            for rest in range(count // 2):
                order.append(rest * 2 + xr)
        return jnp.concatenate([pieces[i] for i in order], axis=1)

    def to_natural(value):
        rows, width = value.shape
        count = 2 ** (len(high_bits) + 2)
        run = width // count
        moved = [value[:, i * run : (i + 1) * run] for i in range(count)]
        pieces = [None] * count
        place = 0
        for xr in range(2):
            for rest in range(count // 2):
                pieces[rest * 2 + xr] = moved[place]
                place += 1
        names = list(high_bits) + ["zl", "x"]
        for position, name in enumerate(names):
            if name == "zl":
                continue
            mask = 1 << (len(names) - 1 - position)
            pieces = [pick(name, pieces[i], pieces[i ^ mask]) for i in range(count)]
        return jnp.concatenate(pieces, axis=1)

    class Chain:
        def __init__(self, token):
            self.token = token
            self.zero = jnp.int32(0)

        def sync(self, *values):
            out = lax.optimization_barrier((self.token,) + values)
            self.token = out[0]
            return out[1] if len(values) == 1 else out[1:]

        def start(self, value, axis):
            return swap(self.sync(value), axis)

        def fence(self, *values):
            moved = self.sync(self.start(jnp.full((1, HD), bit("core"), jnp.int32), "core"))
            self.zero = self.zero + (moved[0, 0] + bit("core") - 1)
            return self.sync(*values)

    def gather_gains(c, gains):
        for name in ("tensor", "core", "zl"):
            sent = c.start(gains, name)
            yield
            gains = ordered(name, gains, c.sync(sent), dim=1)
        for name in list(high_bits)[::-1] + ["x"]:
            sent = c.start(gains, name)
            yield
            gains = jnp.concatenate([gains, c.sync(sent)], axis=1)
        return gains

    def pair_sum(c, values, between=None):
        count, width = values.shape
        for level, axis in ((1, "zl"), (2, "tensor"), (0, "core")):
            run = width >> (level + 1)
            other = c.sync(c.start(values, axis))
            blocks = [other[:, i * run : (i + 1) * run] for i in range(width // run)]
            values = values + jnp.concatenate([blocks[i ^ 1] for i in range(len(blocks))], axis=1)
            if between and axis == "zl":
                between()
        return values

    def scatter_gains(c, gains):
        for name in ["x"] + list(high_bits):
            half = gains.shape[1] // 2
            sent = c.start(gains[:, half:], name)
            yield
            gains = gains[:, :half] + c.sync(sent)
        for name in ("zl", "core", "tensor"):
            own, sent = split(gains, name, 1)
            sent = c.start(sent, name)
            yield
            gains = own + c.sync(sent)
        return gains

    class Steps:
        def __init__(self, stages):
            self.stages, self.done = stages, False
            self()

        def __call__(self):
            if not self.done:
                try:
                    next(self.stages)
                except StopIteration as end:
                    self.value, self.done = end.value, True

        def finish(self):
            while not self.done:
                self()
            return self.value

    def stack2(low, high):
        return jnp.concatenate([low, high], axis=0)

    def shards(
        tokens,
        segment_ids,
        w_query,
        w_key,
        w_value,
        w_output,
        w_gate,
        w_up,
        w_down,
        query_gain,
        key_gain,
        attn_gain,
        ffn_gain,
        cotangent,
    ):
        own_tokens, model_width = tokens.shape
        half_width = model_width // 2
        block_width = half_width // 2
        seq_length = own_tokens * 2
        core_tokens = seq_length * 2
        group_tokens = core_tokens * 2
        head_width = w_query.shape[1] // 4
        local_heads = head_width // HD
        score_scale = 1.0 / math.sqrt(HD)
        own, other = slice(0, core_tokens), slice(core_tokens, group_tokens)
        c = Chain(jnp.full((1, HD), bit("core"), jnp.int32))

        def columns(parts):
            return parts[0] if len(parts) == 1 else jnp.concatenate(parts, axis=1)

        class Weight:
            def __init__(self, matrices, sent):
                width = sent.shape[1] // len(matrices)
                pairs = [
                    split(ordered("core", m, sent[:, i * width : (i + 1) * width]), "zl", 1)
                    for i, m in enumerate(matrices)
                ]
                self.own = columns([p[0] for p in pairs])
                self.sent = columns([p[1] for p in pairs])
                self.blocks = [[None, None], [None, None]]

            def start_line(self):
                self.line = c.start(self.sent, "zl")

            def end_line(self):
                rows = ordered("zl", self.own, c.sync(self.line))
                for name in high_bits[:0:-1]:
                    rows = stack2(rows, c.sync(c.start(rows, name)))
                self.blocks[0][0] = rows

            def start_high(self):
                self.high = c.start(self.blocks[0][0], high_bits[0])

            def end_high(self):
                self.blocks[0][1] = c.sync(self.high)

            def start_x(self, block):
                self.blocks[1][block] = c.start(self.blocks[0][block], "x")

            def end_x(self, block):
                self.blocks[1][block] = c.sync(self.blocks[1][block])

            def rows(self, side):
                return stack2(*self.blocks[side])

        attn_split = [split(w, "core", 1) for w in (w_query, w_key, w_value, w_output)]
        attn_sent = c.start(columns([s[1] for s in attn_split]), "core")
        gains = jnp.stack([query_gain, key_gain, attn_gain, ffn_gain])
        gain_steps = Steps(gather_gains(c, gains))
        tokens_rel = to_relative(tokens)
        left, right = tokens_rel[:, :half_width], tokens_rel[:, half_width:]
        left_sent = c.start(left, "tensor")
        gain_steps()

        attn_sent = c.sync(attn_sent)
        pair_width = 4 * head_width
        qk = Weight([s[0] for s in attn_split[:2]], attn_sent[:, :pair_width])
        vo = Weight([s[0] for s in attn_split[2:]], attn_sent[:, pair_width:])
        qk.start_line()
        gain_steps()
        ids = jnp.concatenate(
            [
                pick("tensor", segment_ids[:, :own_tokens], segment_ids[:, own_tokens:]),
                pick("tensor", segment_ids[:, own_tokens:], segment_ids[:, :own_tokens]),
            ],
            axis=1,
        )
        ids_sent = c.start(ids, "zl")
        ffn_split = [split(w, "core", 1) for w in (w_gate, w_up, w_down)]
        ffn_sent = c.start(columns([s[1] for s in ffn_split]), "core")
        qk.end_line()
        gain_steps()
        qk.start_x(0)
        qk.start_high()
        right_sent = c.start(right, "zl")
        vo.start_line()
        left = stack2(left, c.sync(left_sent))
        seq_ids = stack2(ids, c.sync(ids_sent))
        ids_sent = c.start(seq_ids, "core")
        right = stack2(right, c.sync(right_sent))

        def rows_second(left, right, between=None, last=None, busy=False):
            left_sent = c.start(left, "tensor" if busy else "zl")
            right_sent = c.start(right, "tensor")
            if between:
                between()

            def woven(rows, sent):
                half = own_tokens
                return jnp.concatenate([rows[:half], sent[:half], rows[half:], sent[half:]], axis=0)

            left_sent = c.sync(left_sent)
            left = woven(left, left_sent) if busy else stack2(left, left_sent)
            right = woven(right, c.sync(right_sent))
            if last:
                last()
            left_sent = c.start(left, "core")
            right_sent = c.start(right, "core")
            return stack2(left, c.sync(left_sent)), stack2(right, c.sync(right_sent))

        def gather_rows(value, between=None, last=None, busy=False):
            left, right = value[:, :half_width], value[:, half_width:]
            left_sent = c.start(left, "zl" if busy else "tensor")
            right_sent = c.start(right, "zl")
            left = stack2(left, c.sync(left_sent))
            right = stack2(right, c.sync(right_sent))
            return rows_second(left, right, between, last, busy)

        ffn_sent = c.sync(ffn_sent)
        width = ffn_sent.shape[1] // 3
        gate_w, up_w, down_w = [
            Weight([s[0]], ffn_sent[:, i * width : (i + 1) * width])
            for i, s in enumerate(ffn_split)
        ]

        def tokens_between():
            vo.end_line()
            gate_w.start_line()
            gain_steps()
            qk.end_x(0)
            vo.start_x(0)
            qk.end_high()
            qk.start_x(1)
            vo.start_high()

        in0, in1 = rows_second(left, right, tokens_between)
        seq_ids = stack2(seq_ids, c.sync(ids_sent))
        gate_w.end_line()
        gains = gain_steps.finish()
        qk.end_x(1)

        attn_scale = gains[2]
        ffn_scale = gains[3]
        head_gains = to_natural(gains[:2])
        head_start = (bit("tensor") * 4 + bit("core") * 2 + bit("zl")) * head_width
        head_gains = lax.dynamic_slice_in_dim(head_gains, head_start, head_width, axis=1)
        query_scale, key_scale = head_gains[0], head_gains[1]
        tokens_f = tokens_rel.astype(F32)
        d_out = to_relative(cotangent).astype(F32)
        places = jnp.arange(own_tokens)
        positions = jnp.concatenate(
            [places + bit("tensor") * own_tokens, places + (1 - bit("tensor")) * own_tokens]
        )
        visible = (positions[:, None] >= positions[None, :])[None] & (
            seq_ids[:, :, None] == seq_ids[:, None, :]
        )
        visible = visible[:, None]

        wqk0, wqk1 = qk.rows(0), qk.rows(1)
        projected = dot(in0, wqk0) + dot(in1, wqk1)
        query, key_proj = projected[:, :head_width], projected[:, head_width:]

        def squares_between():
            vo.end_high()
            vo.end_x(0)
            vo.start_x(1)
            gate_w.start_high()
            up_w.start_line()

        squares = pair_sum(
            c,
            jnp.stack([jnp.sum(query * query, axis=1), jnp.sum(key_proj * key_proj, axis=1)]),
            squares_between,
        )
        q_rms = lax.rsqrt(squares[0] / model_width + EPSILON)[:, None]
        k_rms = lax.rsqrt(squares[1] / model_width + EPSILON)[:, None]
        normed_query = (query * q_rms * query_scale).astype(BF)
        normed_key = (key_proj * k_rms * key_scale).astype(BF)
        gate_w.start_x(0)
        down_w.start_line()
        vo.end_x(1)
        normed_query, normed_key = c.sync(normed_query, normed_key)
        wvo0, wvo1 = vo.rows(0), vo.rows(1)
        wv0, wo0 = wvo0[:, :head_width], wvo0[:, head_width:]
        wv1, wo1 = wvo1[:, :head_width], wvo1[:, head_width:]
        value_bf = (dot(in0, wv0) + dot(in1, wv1)).astype(BF)
        heads = (4, seq_length, local_heads, HD)
        query_heads = normed_query.reshape(heads)
        key_heads = normed_key.reshape(heads)
        value_heads = value_bf.reshape(heads)
        scores = (
            jnp.einsum("bqhd,bkhd->bhqk", query_heads, key_heads, preferred_element_type=F32)
            * score_scale
        )
        scores = jnp.where(visible, scores, NEGATIVE)
        peak = jnp.max(scores, axis=-1, keepdims=True)
        expo = jnp.exp(scores - peak)
        total = jnp.sum(expo, axis=-1, keepdims=True)
        prob = expo / total
        prob_bf = prob.astype(BF)
        attn_heads = jnp.einsum(
            "bhqk,bkhd->bqhd", prob_bf, value_heads, preferred_element_type=F32
        ).astype(BF)
        attn = attn_heads.reshape(group_tokens, head_width)
        attn = c.sync(attn)
        up_w.end_line()
        gate_w.end_x(0)
        up_w.start_x(0)
        down_w.end_line()
        gate_w.end_high()
        gate_w.start_x(1)
        up_w.start_high()

        def halve(total, axis):
            half = total.shape[0] // 2
            return total[:half], c.start(total[half:].astype(BF), axis)

        def added(pair):
            return pair[0] + c.sync(pair[1]).astype(F32)

        def cross(total):
            rows = own_tokens
            own = stack2(total[:rows], total[2 * rows : 3 * rows])
            sent = stack2(total[rows : 2 * rows], total[3 * rows :])
            return own, c.start(sent.astype(BF), "tensor")

        def scatter_rows(left_of, right_of, first=None, second=None, busy=False):
            left_sent = c.start(left_of(other).astype(BF), "core")
            right_sent = c.start(right_of(other).astype(BF), "core")
            left = left_of(own) + c.sync(left_sent).astype(F32)
            left = cross(left) if busy else halve(left, "zl")
            right = cross(right_of(own) + c.sync(right_sent).astype(F32))
            if first:
                first()
            left, right = added(left), added(right)
            left, right = halve(left, "zl" if busy else "tensor"), halve(right, "zl")
            if second:
                second()
            return added(left), added(right)

        def proj_second():
            up_w.end_x(0)
            up_w.end_high()
            gate_w.end_x(1)
            up_w.start_x(1)
            down_w.start_high()
            down_w.start_x(0)

        proj = columns(
            scatter_rows(
                lambda rows: dot_nt(attn[rows], wo0), lambda rows: dot_nt(attn[rows], wo1), None, proj_second, True
            )
        )
        attn_rms = rms_scale(proj)
        resid = tokens_f + proj * attn_rms * attn_scale

        def resid_last():
            up_w.end_x(1)
            down_w.end_high()
            down_w.end_x(0)
            down_w.start_x(1)

        h0, h1 = gather_rows(resid.astype(BF), None, resid_last, True)
        wg0, wg1 = gate_w.rows(0), gate_w.rows(1)
        gate = dot(h0, wg0) + dot(h1, wg1)
        sigma = jax.nn.sigmoid(gate)
        wu0, wu1 = up_w.rows(0), up_w.rows(1)
        up = dot(h0, wu0) + dot(h1, wu1)
        act = (gate * sigma * up).astype(BF)

        wd0 = down_w.rows(0)
        first_rows = down_w.blocks[1][0]
        left, right = scatter_rows(
            lambda rows: dot_nt(act[rows], wd0), lambda rows: dot_nt(act[rows], first_rows)
        )
        down_w.end_x(1)
        last_rows = down_w.blocks[1][1]
        sent = c.start(dot_nt(act[other], last_rows).astype(BF), "core")
        last = cross(dot_nt(act[own], last_rows) + c.sync(sent).astype(F32))
        last = halve(added(last), "zl")
        ffn = columns([left, right, added(last)])
        wd1 = down_w.rows(1)

        ffn_rms = rms_scale(ffn)
        output = to_natural((resid + ffn * ffn_rms * ffn_scale).astype(BF))
        ffn_gain_term = jnp.sum(d_out * ffn * ffn_rms, axis=0)
        scaled_out = d_out * ffn_scale
        d_ffn = (
            ffn_rms
            * (
                scaled_out
                - ffn * ffn_rms * ffn_rms * jnp.mean(scaled_out * ffn, axis=1, keepdims=True)
            )
        ).astype(BF)
        f0, f1 = gather_rows(d_ffn)

        class Grad:
            def __init__(self, *terms):
                self.terms = terms
                self.x, self.total = [None, None], [None, None]

            def product(self, side, block):
                cols = slice(block * block_width, (block + 1) * block_width)
                return columns([dot_tn(halves[side][:, cols], r) for halves, r in self.terms])

            def start_x(self, block):
                self.x[block] = c.start(self.product(1, block).astype(BF), "x")

            def end_x(self, block):
                moved = c.sync(self.x[block])
                self.total[block] = self.product(0, block) + moved.astype(F32)

            def start_high(self):
                self.high = c.start(self.total[1].astype(BF), high_bits[0])

            def end_high(self):
                total = self.total[0] + c.sync(self.high).astype(F32)
                for name in high_bits[1:]:
                    total = added(halve(total, name))
                self.own, self.sent = split(total, "zl", 0)

            def start_line(self):
                self.line = c.start(self.sent.astype(BF), "zl")

            def joined(self, axis, moved, low=None):
                width = moved.shape[1] // len(self.terms)
                cols = [slice(i * width, (i + 1) * width) for i in range(len(self.terms))]
                if low is None:
                    return [ordered(axis, self.own[:, s], moved[:, s], dim=1) for s in cols]
                pairs = [(self.own[:, s], moved[:, s]) for s in cols]
                return [columns([jnp.where(low, a, b), jnp.where(low, b, a)]) for a, b in pairs]

            def end_line(self):
                moved = c.sync(self.line).astype(F32)
                self.own, sent = split(columns(self.joined("zl", moved)), "core", 0)
                self.core = c.start(sent.astype(BF), "core")

            def end(self):
                moved = c.sync(self.core).astype(F32)
                self.results = self.joined("core", moved, c.token[0, 0] == 0)

        down_grad = Grad(((f0, f1), act))
        down_grad.start_x(1)
        f0, f1 = c.fence(f0, f1)
        down_grad.terms = (((f0, f1), act),)
        down_grad.start_x(0)
        d_act = dot(f0, wd0) + dot(f1, wd1)
        d_gate = (d_act * up * sigma * (1.0 + gate * (1.0 - sigma))).astype(BF)
        d_up = (d_act * gate * sigma).astype(BF)
        gate_grad = Grad(((h0, h1), d_gate))
        up_grad = Grad(((h0, h1), d_up))
        down_grad.end_x(1)
        down_grad.start_high()
        gate_grad.start_x(1)
        d_gate, d_up = c.fence(d_gate, d_up)

        def hidden_first():
            down_grad.end_x(0)
            gate_grad.start_x(0)

        def hidden_second():
            gate_grad.end_x(1)
            up_grad.start_x(1)
            down_grad.end_high()
            gate_grad.start_high()

        d_resid = d_out + columns(
            scatter_rows(
                lambda rows: dot_nt(d_gate[rows], wg0) + dot_nt(d_up[rows], wu0),
                lambda rows: dot_nt(d_gate[rows], wg1) + dot_nt(d_up[rows], wu1),
                hidden_first,
                hidden_second,
                True,
            )
        )
        attn_gain_term = jnp.sum(d_resid * proj * attn_rms, axis=0)
        scaled_resid = d_resid * attn_scale
        d_proj = (
            attn_rms
            * (
                scaled_resid
                - proj * attn_rms * attn_rms * jnp.mean(scaled_resid * proj, axis=1, keepdims=True)
            )
        ).astype(BF)

        def proj_between():
            down_grad.start_line()
            gate_grad.end_x(0)
            up_grad.start_x(0)

        def proj_last():
            up_grad.end_x(1)
            gate_grad.end_high()
            up_grad.start_high()
            gate_grad.start_line()

        p0, p1 = gather_rows(d_proj, proj_between, proj_last, True)
        up_grad.end_x(0)
        d_attn = (dot(p0, wo0) + dot(p1, wo1)).astype(BF)

        d_attn_heads = d_attn.reshape(heads)
        d_value = (
            jnp.einsum("bhqk,bqhd->bkhd", prob_bf, d_attn_heads, preferred_element_type=F32)
            .reshape(group_tokens, head_width)
            .astype(BF)
        )
        ov_grad = Grad(((p0, p1), attn), ((in0, in1), d_value))
        ov_grad.start_x(1)
        d_attn = c.fence(d_attn)
        d_attn_heads = d_attn.reshape(heads)
        d_prob = jnp.einsum(
            "bqhd,bkhd->bhqk", d_attn_heads, value_heads, preferred_element_type=F32
        )
        delta = jnp.einsum(
            "bqhd,bqhd->bhq", d_attn_heads, attn.reshape(heads), preferred_element_type=F32
        )[..., None]
        d_score = (prob * (d_prob - delta)).astype(BF)
        d_nq = (
            jnp.einsum("bhqk,bkhd->bqhd", d_score, key_heads, preferred_element_type=F32).reshape(
                group_tokens, head_width
            )
            * score_scale
        )
        d_nk = (
            jnp.einsum("bhqk,bqhd->bkhd", d_score, query_heads, preferred_element_type=F32).reshape(
                group_tokens, head_width
            )
            * score_scale
        )
        query_gain_term = jnp.sum(d_nq * query * q_rms, axis=0)
        key_gain_term = jnp.sum(d_nk * key_proj * k_rms, axis=0)
        scaled_q = d_nq * query_scale
        scaled_k = d_nk * key_scale
        zero = jnp.zeros((2, model_width), F32)
        placed = lax.dynamic_update_slice_in_dim(
            zero, jnp.stack([query_gain_term, key_gain_term]), head_start + c.zero, 1
        )
        gain_parts = jnp.concatenate(
            [to_relative(placed), jnp.stack([attn_gain_term, ffn_gain_term])], axis=0
        )
        gain_steps = Steps(scatter_gains(c, gain_parts))
        inner = c.sync(
            jnp.stack([jnp.sum(scaled_q * query, axis=1), jnp.sum(scaled_k * key_proj, axis=1)])
        )
        up_grad.end_high()
        ov_grad.end_x(1)
        ov_grad.start_high()
        down_grad.end_line()
        inner = pair_sum(c, inner, up_grad.start_line)
        gain_steps()
        d_query = (
            q_rms * (scaled_q - query * q_rms * q_rms * (inner[0] / model_width)[:, None])
        ).astype(BF)
        d_key = (
            k_rms * (scaled_k - key_proj * k_rms * k_rms * (inner[1] / model_width)[:, None])
        ).astype(BF)
        d_qk = columns([d_query, d_key])
        qk_grad = Grad(((in0, in1), d_query), ((in0, in1), d_key))
        qk_grad.start_x(1)
        gate_grad.end_line()
        down_grad.end()

        def tokens_first():
            ov_grad.high = c.sync(ov_grad.high)
            qk_grad.end_x(1)
            qk_grad.start_high()
            ov_grad.start_x(0)
            qk_grad.start_x(0)

        def tokens_second():
            gain_steps()
            up_grad.end_line()
            gate_grad.end()

        d_tokens = columns(
            scatter_rows(
                lambda rows: dot_nt(d_qk[rows], wqk0) + dot_nt(d_value[rows], wv0),
                lambda rows: dot_nt(d_qk[rows], wqk1) + dot_nt(d_value[rows], wv1),
                tokens_first,
                tokens_second,
                True,
            )
        )
        grad_tokens = to_natural(d_resid + d_tokens)
        gain_steps()
        ov_grad.end_x(0)
        ov_grad.end_high()
        ov_grad.start_line()
        gain_steps()
        qk_grad.end_x(0)
        ov_grad.end_line()
        gain_parts = gain_steps.finish()
        qk_grad.end_high()
        qk_grad.start_line()
        up_grad.end()
        ov_grad.end()
        qk_grad.end_line()
        qk_grad.end()
        grad_output, grad_value = ov_grad.results
        grad_query, grad_key = qk_grad.results
        return (
            output,
            grad_tokens,
            grad_query,
            grad_key,
            grad_value,
            grad_output,
            gate_grad.results[0],
            up_grad.results[0],
            down_grad.results[0],
            gain_parts[0],
            gain_parts[1],
            gain_parts[2],
            gain_parts[3],
        )

    return shards


def solution(mesh):
    dp = mesh.shape["dp"]
    high = max(dp.bit_length() - 4, 0)
    high_bits = tuple(f"z{i}" for i in range(high))
    names = high_bits + ("zl", "x", "core", "tensor")
    fine = Mesh(mesh.devices.reshape((2,) * len(names)), names)
    rows = names[:-1]
    both = names
    mapped = jax.shard_map(
        build(high_bits),
        mesh=fine,
        in_specs=(
            P(both, None),
            P(rows, None),
            P(rows, "tensor"),
            P(rows, "tensor"),
            P(rows, "tensor"),
            P(rows, "tensor"),
            P(rows, "tensor"),
            P(rows, "tensor"),
            P(rows, "tensor"),
            P(both),
            P(both),
            P(both),
            P(both),
            P(both, None),
        ),
        out_specs=(
            P(both, None),
            P(both, None),
            P(rows, "tensor"),
            P(rows, "tensor"),
            P(rows, "tensor"),
            P(rows, "tensor"),
            P(rows, "tensor"),
            P(rows, "tensor"),
            P(rows, "tensor"),
            P(both),
            P(both),
            P(both),
            P(both),
        ),
        check_vma=False,
    )
    return mapped
```

```python
import math

import jax
import jax.numpy as jnp
from jax import lax
from jax.sharding import Mesh, PartitionSpec as P

HD = 128

EPSILON = 1e-06
NEGATIVE = -1e30
FLIP = [(0, 1), (1, 0)]
BF = jnp.bfloat16
F32 = jnp.float32


def swap(value, axis):
    return lax.ppermute(value, axis, FLIP)


def bit(axis):
    return lax.axis_index(axis)


def pick(axis, low, high):
    return jnp.where(bit(axis) == 0, low, high)


def ordered(axis, own, other, dim=0):
    return jnp.concatenate([pick(axis, own, other), pick(axis, other, own)], axis=dim)


def split(value, axis, dim):
    half = value.shape[dim] // 2
    low = lax.slice_in_dim(value, 0, half, axis=dim)
    high = lax.slice_in_dim(value, half, 2 * half, axis=dim)
    return pick(axis, low, high), pick(axis, high, low)


def dot(a, b):
    return jnp.dot(a, b, preferred_element_type=F32)


def dot_nt(a, b):
    return jnp.einsum("sc,rc->sr", a, b, preferred_element_type=F32)


def dot_tn(a, b):
    return jnp.einsum("sr,sc->rc", a, b, preferred_element_type=F32)


def rms_scale(values):
    return lax.rsqrt(jnp.mean(values * values, axis=1, keepdims=True) + EPSILON)


def build(high_bits):
    def to_relative(value):
        rows, width = value.shape
        count = 2 ** (len(high_bits) + 2)
        run = width // count
        pieces = [value[:, i * run : (i + 1) * run] for i in range(count)]
        names = list(high_bits) + ["zl", "x"]
        for position, name in enumerate(names):
            if name == "zl":
                continue
            mask = 1 << (len(names) - 1 - position)
            pieces = [pick(name, pieces[i], pieces[i ^ mask]) for i in range(count)]
        order = []
        for xr in range(2):
            for rest in range(count // 2):
                order.append(rest * 2 + xr)
        return jnp.concatenate([pieces[i] for i in order], axis=1)

    def to_natural(value):
        rows, width = value.shape
        count = 2 ** (len(high_bits) + 2)
        run = width // count
        moved = [value[:, i * run : (i + 1) * run] for i in range(count)]
        pieces = [None] * count
        place = 0
        for xr in range(2):
            for rest in range(count // 2):
                pieces[rest * 2 + xr] = moved[place]
                place += 1
        names = list(high_bits) + ["zl", "x"]
        for position, name in enumerate(names):
            if name == "zl":
                continue
            mask = 1 << (len(names) - 1 - position)
            pieces = [pick(name, pieces[i], pieces[i ^ mask]) for i in range(count)]
        return jnp.concatenate(pieces, axis=1)

    class Chain:
        def __init__(self, token):
            self.token = token
            self.zero = jnp.int32(0)

        def sync(self, *values):
            out = lax.optimization_barrier((self.token,) + values)
            self.token = out[0]
            return out[1] if len(values) == 1 else out[1:]

        def start(self, value, axis):
            return swap(self.sync(value), axis)

        def fence(self, *values):
            moved = self.sync(self.start(jnp.full((1, HD), bit("core"), jnp.int32), "core"))
            self.zero = self.zero + (moved[0, 0] + bit("core") - 1)
            return self.sync(*values)

    def gather_gains(c, gains):
        for name in ("tensor", "core", "zl"):
            sent = c.start(gains, name)
            yield
            gains = ordered(name, gains, c.sync(sent), dim=1)
        for name in list(high_bits)[::-1] + ["x"]:
            sent = c.start(gains, name)
            yield
            gains = jnp.concatenate([gains, c.sync(sent)], axis=1)
        return gains

    def pair_sum(c, values, between=None):
        count, width = values.shape
        for level, axis in ((1, "zl"), (2, "tensor"), (0, "core")):
            run = width >> (level + 1)
            other = c.sync(c.start(values, axis))
            blocks = [other[:, i * run : (i + 1) * run] for i in range(width // run)]
            values = values + jnp.concatenate([blocks[i ^ 1] for i in range(len(blocks))], axis=1)
            if between and axis == "zl":
                between()
        return values

    def scatter_gains(c, gains):
        for name in ["x"] + list(high_bits):
            half = gains.shape[1] // 2
            sent = c.start(gains[:, half:], name)
            yield
            gains = gains[:, :half] + c.sync(sent)
        for name in ("zl", "core", "tensor"):
            own, sent = split(gains, name, 1)
            sent = c.start(sent, name)
            yield
            gains = own + c.sync(sent)
        return gains

    class Steps:
        def __init__(self, stages):
            self.stages, self.done = stages, False
            self()

        def __call__(self):
            if not self.done:
                try:
                    next(self.stages)
                except StopIteration as end:
                    self.value, self.done = end.value, True

        def finish(self):
            while not self.done:
                self()
            return self.value

    def stack2(low, high):
        return jnp.concatenate([low, high], axis=0)

    def shards(
        tokens,
        segment_ids,
        w_query,
        w_key,
        w_value,
        w_output,
        w_gate,
        w_up,
        w_down,
        query_gain,
        key_gain,
        attn_gain,
        ffn_gain,
        cotangent,
    ):
        own_tokens, model_width = tokens.shape
        half_width = model_width // 2
        block_width = half_width // 2
        seq_length = own_tokens * 2
        core_tokens = seq_length * 2
        group_tokens = core_tokens * 2
        head_width = w_query.shape[1] // 4
        local_heads = head_width // HD
        score_scale = 1.0 / math.sqrt(HD)
        own, other = slice(0, core_tokens), slice(core_tokens, group_tokens)
        c = Chain(jnp.full((1, HD), bit("core"), jnp.int32))

        def columns(parts):
            return parts[0] if len(parts) == 1 else jnp.concatenate(parts, axis=1)

        class Weight:
            def __init__(self, matrices, sent):
                width = sent.shape[1] // len(matrices)
                pairs = [
                    split(ordered("core", m, sent[:, i * width : (i + 1) * width]), "zl", 1)
                    for i, m in enumerate(matrices)
                ]
                self.own = columns([p[0] for p in pairs])
                self.sent = columns([p[1] for p in pairs])
                self.blocks = [[None, None], [None, None]]

            def start_line(self):
                self.line = c.start(self.sent, "zl")

            def end_line(self):
                rows = ordered("zl", self.own, c.sync(self.line))
                for name in high_bits[:0:-1]:
                    rows = stack2(rows, c.sync(c.start(rows, name)))
                self.blocks[0][0] = rows

            def start_high(self):
                self.high = c.start(self.blocks[0][0], high_bits[0])

            def end_high(self):
                self.blocks[0][1] = c.sync(self.high)

            def start_x(self, block):
                self.blocks[1][block] = c.start(self.blocks[0][block], "x")

            def end_x(self, block):
                self.blocks[1][block] = c.sync(self.blocks[1][block])

            def rows(self, side):
                return stack2(*self.blocks[side])

        attn_split = [split(w, "core", 1) for w in (w_query, w_key, w_value, w_output)]
        attn_sent = c.start(columns([s[1] for s in attn_split]), "core")
        gains = jnp.stack([query_gain, key_gain, attn_gain, ffn_gain])
        gain_steps = Steps(gather_gains(c, gains))
        tokens_rel = to_relative(tokens)
        left, right = tokens_rel[:, :half_width], tokens_rel[:, half_width:]
        left_sent = c.start(left, "tensor")
        gain_steps()

        attn_sent = c.sync(attn_sent)
        pair_width = 4 * head_width
        qk = Weight([s[0] for s in attn_split[:2]], attn_sent[:, :pair_width])
        vo = Weight([s[0] for s in attn_split[2:]], attn_sent[:, pair_width:])
        qk.start_line()
        gain_steps()
        ids = jnp.concatenate(
            [
                pick("tensor", segment_ids[:, :own_tokens], segment_ids[:, own_tokens:]),
                pick("tensor", segment_ids[:, own_tokens:], segment_ids[:, :own_tokens]),
            ],
            axis=1,
        )
        ids_sent = c.start(ids, "zl")
        ffn_split = [split(w, "core", 1) for w in (w_gate, w_up, w_down)]
        ffn_sent = c.start(columns([s[1] for s in ffn_split]), "core")
        qk.end_line()
        gain_steps()
        qk.start_x(0)
        qk.start_high()
        right_sent = c.start(right, "zl")
        vo.start_line()
        left = stack2(left, c.sync(left_sent))
        seq_ids = stack2(ids, c.sync(ids_sent))
        ids_sent = c.start(seq_ids, "core")
        right = stack2(right, c.sync(right_sent))

        def rows_second(left, right, between=None, last=None):
            left_sent = c.start(left, "zl")
            right_sent = c.start(right, "tensor")
            if between:
                between()
            left = stack2(left, c.sync(left_sent))
            right_sent = c.sync(right_sent)
            rows = own_tokens
            right = jnp.concatenate(
                [right[:rows], right_sent[:rows], right[rows:], right_sent[rows:]], axis=0
            )
            if last:
                last()
            left_sent = c.start(left, "core")
            right_sent = c.start(right, "core")
            return stack2(left, c.sync(left_sent)), stack2(right, c.sync(right_sent))

        def gather_rows(value, between=None, last=None):
            left, right = value[:, :half_width], value[:, half_width:]
            left_sent = c.start(left, "tensor")
            right_sent = c.start(right, "zl")
            left = stack2(left, c.sync(left_sent))
            right = stack2(right, c.sync(right_sent))
            return rows_second(left, right, between, last)

        ffn_sent = c.sync(ffn_sent)
        width = ffn_sent.shape[1] // 3
        gate_w, up_w, down_w = [
            Weight([s[0]], ffn_sent[:, i * width : (i + 1) * width])
            for i, s in enumerate(ffn_split)
        ]

        def tokens_between():
            vo.end_line()
            gate_w.start_line()
            gain_steps()
            qk.end_x(0)
            vo.start_x(0)
            qk.end_high()
            qk.start_x(1)
            vo.start_high()

        in0, in1 = rows_second(left, right, tokens_between)
        seq_ids = stack2(seq_ids, c.sync(ids_sent))
        gate_w.end_line()
        gains = gain_steps.finish()
        qk.end_x(1)

        attn_scale = gains[2]
        ffn_scale = gains[3]
        head_gains = to_natural(gains[:2])
        head_start = (bit("tensor") * 4 + bit("core") * 2 + bit("zl")) * head_width
        head_gains = lax.dynamic_slice_in_dim(head_gains, head_start, head_width, axis=1)
        query_scale, key_scale = head_gains[0], head_gains[1]
        tokens_f = tokens_rel.astype(F32)
        d_out = to_relative(cotangent).astype(F32)
        places = jnp.arange(own_tokens)
        positions = jnp.concatenate(
            [places + bit("tensor") * own_tokens, places + (1 - bit("tensor")) * own_tokens]
        )
        visible = (positions[:, None] >= positions[None, :])[None] & (
            seq_ids[:, :, None] == seq_ids[:, None, :]
        )
        visible = visible[:, None]

        wqk0, wqk1 = qk.rows(0), qk.rows(1)
        projected = dot(in0, wqk0) + dot(in1, wqk1)
        query, key_proj = projected[:, :head_width], projected[:, head_width:]

        def squares_between():
            vo.end_high()
            vo.end_x(0)
            vo.start_x(1)
            gate_w.start_high()
            up_w.start_line()

        squares = pair_sum(
            c,
            jnp.stack([jnp.sum(query * query, axis=1), jnp.sum(key_proj * key_proj, axis=1)]),
            squares_between,
        )
        q_rms = lax.rsqrt(squares[0] / model_width + EPSILON)[:, None]
        k_rms = lax.rsqrt(squares[1] / model_width + EPSILON)[:, None]
        normed_query = (query * q_rms * query_scale).astype(BF)
        normed_key = (key_proj * k_rms * key_scale).astype(BF)
        gate_w.start_x(0)
        down_w.start_line()
        vo.end_x(1)
        normed_query, normed_key = c.sync(normed_query, normed_key)
        wvo0, wvo1 = vo.rows(0), vo.rows(1)
        wv0, wo0 = wvo0[:, :head_width], wvo0[:, head_width:]
        wv1, wo1 = wvo1[:, :head_width], wvo1[:, head_width:]
        value_bf = (dot(in0, wv0) + dot(in1, wv1)).astype(BF)
        heads = (4, seq_length, local_heads, HD)
        query_heads = normed_query.reshape(heads)
        key_heads = normed_key.reshape(heads)
        value_heads = value_bf.reshape(heads)
        scores = (
            jnp.einsum("bqhd,bkhd->bhqk", query_heads, key_heads, preferred_element_type=F32)
            * score_scale
        )
        scores = jnp.where(visible, scores, NEGATIVE)
        peak = jnp.max(scores, axis=-1, keepdims=True)
        expo = jnp.exp(scores - peak)
        total = jnp.sum(expo, axis=-1, keepdims=True)
        prob = expo / total
        prob_bf = prob.astype(BF)
        attn_heads = jnp.einsum(
            "bhqk,bkhd->bqhd", prob_bf, value_heads, preferred_element_type=F32
        ).astype(BF)
        attn = attn_heads.reshape(group_tokens, head_width)
        attn = c.sync(attn)
        up_w.end_line()
        gate_w.end_x(0)
        up_w.start_x(0)
        down_w.end_line()
        gate_w.end_high()
        gate_w.start_x(1)
        up_w.start_high()

        def halve(total, axis):
            half = total.shape[0] // 2
            return total[:half], c.start(total[half:].astype(BF), axis)

        def added(pair):
            return pair[0] + c.sync(pair[1]).astype(F32)

        def cross(total):
            rows = own_tokens
            own = stack2(total[:rows], total[2 * rows : 3 * rows])
            sent = stack2(total[rows : 2 * rows], total[3 * rows :])
            return own, c.start(sent.astype(BF), "tensor")

        def scatter_rows(left_of, right_of, first=None, second=None):
            left_sent = c.start(left_of(other).astype(BF), "core")
            right_sent = c.start(right_of(other).astype(BF), "core")
            left = halve(left_of(own) + c.sync(left_sent).astype(F32), "zl")
            right = cross(right_of(own) + c.sync(right_sent).astype(F32))
            if first:
                first()
            left, right = added(left), added(right)
            left, right = halve(left, "tensor"), halve(right, "zl")
            if second:
                second()
            return added(left), added(right)

        def proj_second():
            up_w.end_x(0)
            up_w.end_high()
            gate_w.end_x(1)
            up_w.start_x(1)
            down_w.start_high()
            down_w.start_x(0)

        proj = columns(
            scatter_rows(
                lambda rows: dot_nt(attn[rows], wo0), lambda rows: dot_nt(attn[rows], wo1), None, proj_second
            )
        )
        attn_rms = rms_scale(proj)
        resid = tokens_f + proj * attn_rms * attn_scale

        def resid_last():
            up_w.end_x(1)
            down_w.end_high()
            down_w.end_x(0)
            down_w.start_x(1)

        h0, h1 = gather_rows(resid.astype(BF), None, resid_last)
        wg0, wg1 = gate_w.rows(0), gate_w.rows(1)
        gate = dot(h0, wg0) + dot(h1, wg1)
        sigma = jax.nn.sigmoid(gate)
        wu0, wu1 = up_w.rows(0), up_w.rows(1)
        up = dot(h0, wu0) + dot(h1, wu1)
        act = (gate * sigma * up).astype(BF)

        wd0 = down_w.rows(0)
        down_w.end_x(1)
        wd1 = down_w.rows(1)
        ffn = columns(
            scatter_rows(lambda rows: dot_nt(act[rows], wd0), lambda rows: dot_nt(act[rows], wd1))
        )

        ffn_rms = rms_scale(ffn)
        output = to_natural((resid + ffn * ffn_rms * ffn_scale).astype(BF))
        ffn_gain_term = jnp.sum(d_out * ffn * ffn_rms, axis=0)
        scaled_out = d_out * ffn_scale
        d_ffn = (
            ffn_rms
            * (
                scaled_out
                - ffn * ffn_rms * ffn_rms * jnp.mean(scaled_out * ffn, axis=1, keepdims=True)
            )
        ).astype(BF)
        f0, f1 = gather_rows(d_ffn)

        class Grad:
            def __init__(self, *terms):
                self.terms = terms
                self.x, self.total = [None, None], [None, None]

            def product(self, side, block):
                cols = slice(block * block_width, (block + 1) * block_width)
                return columns([dot_tn(halves[side][:, cols], r) for halves, r in self.terms])

            def start_x(self, block):
                self.x[block] = c.start(self.product(1, block).astype(BF), "x")

            def end_x(self, block):
                moved = c.sync(self.x[block])
                self.total[block] = self.product(0, block) + moved.astype(F32)

            def start_high(self):
                self.high = c.start(self.total[1].astype(BF), high_bits[0])

            def end_high(self):
                total = self.total[0] + c.sync(self.high).astype(F32)
                for name in high_bits[1:]:
                    total = added(halve(total, name))
                self.own, self.sent = split(total, "zl", 0)

            def start_line(self):
                self.line = c.start(self.sent.astype(BF), "zl")

            def joined(self, axis, moved, low=None):
                width = moved.shape[1] // len(self.terms)
                cols = [slice(i * width, (i + 1) * width) for i in range(len(self.terms))]
                if low is None:
                    return [ordered(axis, self.own[:, s], moved[:, s], dim=1) for s in cols]
                pairs = [(self.own[:, s], moved[:, s]) for s in cols]
                return [columns([jnp.where(low, a, b), jnp.where(low, b, a)]) for a, b in pairs]

            def end_line(self):
                moved = c.sync(self.line).astype(F32)
                self.own, sent = split(columns(self.joined("zl", moved)), "core", 0)
                self.core = c.start(sent.astype(BF), "core")

            def end(self):
                moved = c.sync(self.core).astype(F32)
                self.results = self.joined("core", moved, c.token[0, 0] == 0)

        down_grad = Grad(((f0, f1), act))
        down_grad.start_x(1)
        down_grad.start_x(0)
        f0, f1 = c.fence(f0, f1)
        d_act = dot(f0, wd0) + dot(f1, wd1)
        d_gate = (d_act * up * sigma * (1.0 + gate * (1.0 - sigma))).astype(BF)
        d_up = (d_act * gate * sigma).astype(BF)
        gate_grad = Grad(((h0, h1), d_gate))
        up_grad = Grad(((h0, h1), d_up))
        down_grad.end_x(1)
        down_grad.start_high()
        gate_grad.start_x(1)
        d_gate, d_up = c.fence(d_gate, d_up)

        def hidden_first():
            down_grad.end_x(0)
            gate_grad.start_x(0)

        def hidden_second():
            gate_grad.end_x(1)
            up_grad.start_x(1)
            down_grad.end_high()
            gate_grad.start_high()

        d_resid = d_out + columns(
            scatter_rows(
                lambda rows: dot_nt(d_gate[rows], wg0) + dot_nt(d_up[rows], wu0),
                lambda rows: dot_nt(d_gate[rows], wg1) + dot_nt(d_up[rows], wu1),
                hidden_first,
                hidden_second,
            )
        )
        attn_gain_term = jnp.sum(d_resid * proj * attn_rms, axis=0)
        scaled_resid = d_resid * attn_scale
        d_proj = (
            attn_rms
            * (
                scaled_resid
                - proj * attn_rms * attn_rms * jnp.mean(scaled_resid * proj, axis=1, keepdims=True)
            )
        ).astype(BF)

        def proj_between():
            down_grad.start_line()
            gate_grad.end_x(0)
            up_grad.start_x(0)

        def proj_last():
            up_grad.end_x(1)
            gate_grad.end_high()
            up_grad.start_high()
            gate_grad.start_line()

        p0, p1 = gather_rows(d_proj, proj_between, proj_last)
        up_grad.end_x(0)
        d_attn = (dot(p0, wo0) + dot(p1, wo1)).astype(BF)

        d_attn_heads = d_attn.reshape(heads)
        d_value = (
            jnp.einsum("bhqk,bqhd->bkhd", prob_bf, d_attn_heads, preferred_element_type=F32)
            .reshape(group_tokens, head_width)
            .astype(BF)
        )
        ov_grad = Grad(((p0, p1), attn), ((in0, in1), d_value))
        ov_grad.start_x(1)
        d_attn = c.fence(d_attn)
        d_attn_heads = d_attn.reshape(heads)
        d_prob = jnp.einsum(
            "bqhd,bkhd->bhqk", d_attn_heads, value_heads, preferred_element_type=F32
        )
        delta = jnp.einsum(
            "bqhd,bqhd->bhq", d_attn_heads, attn.reshape(heads), preferred_element_type=F32
        )[..., None]
        d_score = (prob * (d_prob - delta)).astype(BF)
        d_nq = (
            jnp.einsum("bhqk,bkhd->bqhd", d_score, key_heads, preferred_element_type=F32).reshape(
                group_tokens, head_width
            )
            * score_scale
        )
        d_nk = (
            jnp.einsum("bhqk,bqhd->bkhd", d_score, query_heads, preferred_element_type=F32).reshape(
                group_tokens, head_width
            )
            * score_scale
        )
        query_gain_term = jnp.sum(d_nq * query * q_rms, axis=0)
        key_gain_term = jnp.sum(d_nk * key_proj * k_rms, axis=0)
        scaled_q = d_nq * query_scale
        scaled_k = d_nk * key_scale
        zero = jnp.zeros((2, model_width), F32)
        placed = lax.dynamic_update_slice_in_dim(
            zero, jnp.stack([query_gain_term, key_gain_term]), head_start + c.zero, 1
        )
        gain_parts = jnp.concatenate(
            [to_relative(placed), jnp.stack([attn_gain_term, ffn_gain_term])], axis=0
        )
        gain_steps = Steps(scatter_gains(c, gain_parts))
        inner = c.sync(
            jnp.stack([jnp.sum(scaled_q * query, axis=1), jnp.sum(scaled_k * key_proj, axis=1)])
        )
        up_grad.end_high()
        ov_grad.end_x(1)
        ov_grad.start_high()
        down_grad.end_line()
        inner = pair_sum(c, inner, up_grad.start_line)
        gain_steps()
        d_query = (
            q_rms * (scaled_q - query * q_rms * q_rms * (inner[0] / model_width)[:, None])
        ).astype(BF)
        d_key = (
            k_rms * (scaled_k - key_proj * k_rms * k_rms * (inner[1] / model_width)[:, None])
        ).astype(BF)
        d_qk = columns([d_query, d_key])
        qk_grad = Grad(((in0, in1), d_query), ((in0, in1), d_key))
        qk_grad.start_x(1)
        gate_grad.end_line()
        down_grad.end()

        def tokens_first():
            ov_grad.high = c.sync(ov_grad.high)
            qk_grad.end_x(1)
            qk_grad.start_high()
            ov_grad.start_x(0)
            qk_grad.start_x(0)

        def tokens_second():
            qk_grad.end_x(0)
            qk_grad.end_high()
            qk_grad.start_line()
            gain_steps()

        d_tokens = columns(
            scatter_rows(
                lambda rows: dot_nt(d_qk[rows], wqk0) + dot_nt(d_value[rows], wv0),
                lambda rows: dot_nt(d_qk[rows], wqk1) + dot_nt(d_value[rows], wv1),
                tokens_first,
                tokens_second,
            )
        )
        grad_tokens = to_natural(d_resid + d_tokens)
        ov_grad.end_x(0)
        ov_grad.end_high()
        ov_grad.start_line()
        gain_steps()
        up_grad.end_line()
        gate_grad.end()
        gain_steps()
        qk_grad.end_line()
        ov_grad.end_line()
        gain_parts = gain_steps.finish()
        up_grad.end()
        qk_grad.end()
        ov_grad.end()
        grad_output, grad_value = ov_grad.results
        grad_query, grad_key = qk_grad.results
        return (
            output,
            grad_tokens,
            grad_query,
            grad_key,
            grad_value,
            grad_output,
            gate_grad.results[0],
            up_grad.results[0],
            down_grad.results[0],
            gain_parts[0],
            gain_parts[1],
            gain_parts[2],
            gain_parts[3],
        )

    return shards


def solution(mesh):
    dp = mesh.shape["dp"]
    high = max(dp.bit_length() - 4, 0)
    high_bits = tuple(f"z{i}" for i in range(high))
    names = high_bits + ("zl", "x", "core", "tensor")
    fine = Mesh(mesh.devices.reshape((2,) * len(names)), names)
    rows = names[:-1]
    both = names
    mapped = jax.shard_map(
        build(high_bits),
        mesh=fine,
        in_specs=(
            P(both, None),
            P(rows, None),
            P(rows, "tensor"),
            P(rows, "tensor"),
            P(rows, "tensor"),
            P(rows, "tensor"),
            P(rows, "tensor"),
            P(rows, "tensor"),
            P(rows, "tensor"),
            P(both),
            P(both),
            P(both),
            P(both),
            P(both, None),
        ),
        out_specs=(
            P(both, None),
            P(both, None),
            P(rows, "tensor"),
            P(rows, "tensor"),
            P(rows, "tensor"),
            P(rows, "tensor"),
            P(rows, "tensor"),
            P(rows, "tensor"),
            P(rows, "tensor"),
            P(both),
            P(both),
            P(both),
            P(both),
        ),
        check_vma=False,
    )
    return mapped
```

```python
import math

import jax
import jax.numpy as jnp
from jax import lax
from jax.sharding import Mesh, PartitionSpec as P

HD = 128

EPSILON = 1e-06
NEGATIVE = -1e30
FLIP = [(0, 1), (1, 0)]
BF = jnp.bfloat16
F32 = jnp.float32


def swap(value, axis):
    return lax.ppermute(value, axis, FLIP)


def bit(axis):
    return lax.axis_index(axis)


def pick(axis, low, high):
    return jnp.where(bit(axis) == 0, low, high)


def ordered(axis, own, other, dim=0):
    return jnp.concatenate([pick(axis, own, other), pick(axis, other, own)], axis=dim)


def split(value, axis, dim):
    half = value.shape[dim] // 2
    low = lax.slice_in_dim(value, 0, half, axis=dim)
    high = lax.slice_in_dim(value, half, 2 * half, axis=dim)
    return pick(axis, low, high), pick(axis, high, low)


def dot(a, b):
    return jnp.dot(a, b, preferred_element_type=F32)


def dot_nt(a, b):
    return jnp.einsum("sc,rc->sr", a, b, preferred_element_type=F32)


def dot_tn(a, b):
    return jnp.einsum("sr,sc->rc", a, b, preferred_element_type=F32)


def rms_scale(values):
    return lax.rsqrt(jnp.mean(values * values, axis=1, keepdims=True) + EPSILON)


def build(high_bits):
    def to_relative(value):
        rows, width = value.shape
        count = 2 ** (len(high_bits) + 2)
        run = width // count
        pieces = [value[:, i * run : (i + 1) * run] for i in range(count)]
        names = list(high_bits) + ["zl", "x"]
        for position, name in enumerate(names):
            if name == "zl":
                continue
            mask = 1 << (len(names) - 1 - position)
            pieces = [pick(name, pieces[i], pieces[i ^ mask]) for i in range(count)]
        order = []
        for xr in range(2):
            for rest in range(count // 2):
                order.append(rest * 2 + xr)
        return jnp.concatenate([pieces[i] for i in order], axis=1)

    def to_natural(value):
        rows, width = value.shape
        count = 2 ** (len(high_bits) + 2)
        run = width // count
        moved = [value[:, i * run : (i + 1) * run] for i in range(count)]
        pieces = [None] * count
        place = 0
        for xr in range(2):
            for rest in range(count // 2):
                pieces[rest * 2 + xr] = moved[place]
                place += 1
        names = list(high_bits) + ["zl", "x"]
        for position, name in enumerate(names):
            if name == "zl":
                continue
            mask = 1 << (len(names) - 1 - position)
            pieces = [pick(name, pieces[i], pieces[i ^ mask]) for i in range(count)]
        return jnp.concatenate(pieces, axis=1)

    class Chain:
        def __init__(self, token):
            self.token = token
            self.zero = jnp.int32(0)

        def sync(self, *values):
            out = lax.optimization_barrier((self.token,) + values)
            self.token = out[0]
            return out[1] if len(values) == 1 else out[1:]

        def start(self, value, axis):
            return swap(self.sync(value), axis)

        def fence(self, *values):
            moved = self.sync(self.start(jnp.full((1, HD), bit("core"), jnp.int32), "core"))
            self.zero = self.zero + (moved[0, 0] + bit("core") - 1)
            return self.sync(*values)

    def gather_gains(c, gains):
        for name in ("tensor", "core", "zl"):
            sent = c.start(gains, name)
            yield
            gains = ordered(name, gains, c.sync(sent), dim=1)
        for name in list(high_bits)[::-1] + ["x"]:
            sent = c.start(gains, name)
            yield
            gains = jnp.concatenate([gains, c.sync(sent)], axis=1)
        return gains

    def pair_sum(c, values, between=None):
        count, width = values.shape
        for level, axis in ((1, "zl"), (2, "tensor"), (0, "core")):
            run = width >> (level + 1)
            other = c.sync(c.start(values, axis))
            blocks = [other[:, i * run : (i + 1) * run] for i in range(width // run)]
            values = values + jnp.concatenate([blocks[i ^ 1] for i in range(len(blocks))], axis=1)
            if between and axis == "zl":
                between()
        return values

    def scatter_gains(c, gains):
        for name in ["x"] + list(high_bits):
            half = gains.shape[1] // 2
            sent = c.start(gains[:, half:], name)
            yield
            gains = gains[:, :half] + c.sync(sent)
        for name in ("zl", "core", "tensor"):
            own, sent = split(gains, name, 1)
            sent = c.start(sent, name)
            yield
            gains = own + c.sync(sent)
        return gains

    class Steps:
        def __init__(self, stages):
            self.stages, self.done = stages, False
            self()

        def __call__(self):
            if not self.done:
                try:
                    next(self.stages)
                except StopIteration as end:
                    self.value, self.done = end.value, True

        def finish(self):
            while not self.done:
                self()
            return self.value

    def stack2(low, high):
        return jnp.concatenate([low, high], axis=0)

    def shards(
        tokens,
        segment_ids,
        w_query,
        w_key,
        w_value,
        w_output,
        w_gate,
        w_up,
        w_down,
        query_gain,
        key_gain,
        attn_gain,
        ffn_gain,
        cotangent,
    ):
        own_tokens, model_width = tokens.shape
        half_width = model_width // 2
        block_width = half_width // 2
        seq_length = own_tokens * 2
        core_tokens = seq_length * 2
        group_tokens = core_tokens * 2
        head_width = w_query.shape[1] // 4
        local_heads = head_width // HD
        score_scale = 1.0 / math.sqrt(HD)
        own, other = slice(0, core_tokens), slice(core_tokens, group_tokens)
        c = Chain(jnp.full((1, HD), bit("core"), jnp.int32))

        def columns(parts):
            return parts[0] if len(parts) == 1 else jnp.concatenate(parts, axis=1)

        class Weight:
            def __init__(self, matrices, sent):
                width = sent.shape[1] // len(matrices)
                pairs = [
                    split(ordered("core", m, sent[:, i * width : (i + 1) * width]), "zl", 1)
                    for i, m in enumerate(matrices)
                ]
                self.own = columns([p[0] for p in pairs])
                self.sent = columns([p[1] for p in pairs])
                self.blocks = [[None, None], [None, None]]

            def start_line(self):
                self.line = c.start(self.sent, "zl")

            def end_line(self):
                rows = ordered("zl", self.own, c.sync(self.line))
                for name in high_bits[:0:-1]:
                    rows = stack2(rows, c.sync(c.start(rows, name)))
                self.blocks[0][0] = rows

            def start_high(self):
                self.high = c.start(self.blocks[0][0], high_bits[0])

            def end_high(self):
                self.blocks[0][1] = c.sync(self.high)

            def start_x(self, block):
                self.blocks[1][block] = c.start(self.blocks[0][block], "x")

            def end_x(self, block):
                self.blocks[1][block] = c.sync(self.blocks[1][block])

            def rows(self, side):
                return stack2(*self.blocks[side])

        attn_split = [split(w, "core", 1) for w in (w_query, w_key, w_value, w_output)]
        attn_sent = c.start(columns([s[1] for s in attn_split]), "core")
        gains = jnp.stack([query_gain, key_gain, attn_gain, ffn_gain])
        gain_steps = Steps(gather_gains(c, gains))
        tokens_rel = to_relative(tokens)
        left, right = tokens_rel[:, :half_width], tokens_rel[:, half_width:]
        left_sent = c.start(left, "tensor")
        gain_steps()

        attn_sent = c.sync(attn_sent)
        pair_width = 4 * head_width
        qk = Weight([s[0] for s in attn_split[:2]], attn_sent[:, :pair_width])
        vo = Weight([s[0] for s in attn_split[2:]], attn_sent[:, pair_width:])
        qk.start_line()
        gain_steps()
        ids = jnp.concatenate(
            [
                pick("tensor", segment_ids[:, :own_tokens], segment_ids[:, own_tokens:]),
                pick("tensor", segment_ids[:, own_tokens:], segment_ids[:, :own_tokens]),
            ],
            axis=1,
        )
        ids_sent = c.start(ids, "zl")
        ffn_split = [split(w, "core", 1) for w in (w_gate, w_up, w_down)]
        ffn_sent = c.start(columns([s[1] for s in ffn_split]), "core")
        qk.end_line()
        gain_steps()
        qk.start_x(0)
        qk.start_high()
        right_sent = c.start(right, "zl")
        vo.start_line()
        left = stack2(left, c.sync(left_sent))
        seq_ids = stack2(ids, c.sync(ids_sent))
        ids_sent = c.start(seq_ids, "core")
        right = stack2(right, c.sync(right_sent))

        def rows_second(left, right, between=None, last=None):
            left_sent = c.start(left, "zl")
            right_sent = c.start(right, "tensor")
            if between:
                between()
            left = stack2(left, c.sync(left_sent))
            right_sent = c.sync(right_sent)
            rows = own_tokens
            right = jnp.concatenate(
                [right[:rows], right_sent[:rows], right[rows:], right_sent[rows:]], axis=0
            )
            if last:
                last()
            left_sent = c.start(left, "core")
            right_sent = c.start(right, "core")
            return stack2(left, c.sync(left_sent)), stack2(right, c.sync(right_sent))

        def gather_rows(value, between=None, last=None):
            left, right = value[:, :half_width], value[:, half_width:]
            left_sent = c.start(left, "tensor")
            right_sent = c.start(right, "zl")
            left = stack2(left, c.sync(left_sent))
            right = stack2(right, c.sync(right_sent))
            return rows_second(left, right, between, last)

        ffn_sent = c.sync(ffn_sent)
        width = ffn_sent.shape[1] // 3
        gate_w, up_w, down_w = [
            Weight([s[0]], ffn_sent[:, i * width : (i + 1) * width])
            for i, s in enumerate(ffn_split)
        ]

        def tokens_between():
            vo.end_line()
            gate_w.start_line()
            gain_steps()
            qk.end_x(0)
            vo.start_x(0)
            qk.end_high()
            qk.start_x(1)
            vo.start_high()

        in0, in1 = rows_second(left, right, tokens_between)
        seq_ids = stack2(seq_ids, c.sync(ids_sent))
        gate_w.end_line()
        gains = gain_steps.finish()
        qk.end_x(1)

        attn_scale = gains[2]
        ffn_scale = gains[3]
        head_gains = to_natural(gains[:2])
        head_start = (bit("tensor") * 4 + bit("core") * 2 + bit("zl")) * head_width
        head_gains = lax.dynamic_slice_in_dim(head_gains, head_start, head_width, axis=1)
        query_scale, key_scale = head_gains[0], head_gains[1]
        tokens_f = tokens_rel.astype(F32)
        d_out = to_relative(cotangent).astype(F32)
        places = jnp.arange(own_tokens)
        positions = jnp.concatenate(
            [places + bit("tensor") * own_tokens, places + (1 - bit("tensor")) * own_tokens]
        )
        visible = (positions[:, None] >= positions[None, :])[None] & (
            seq_ids[:, :, None] == seq_ids[:, None, :]
        )
        visible = visible[:, None]

        wqk0, wqk1 = qk.rows(0), qk.rows(1)
        projected = dot(in0, wqk0) + dot(in1, wqk1)
        query, key_proj = projected[:, :head_width], projected[:, head_width:]

        def squares_between():
            vo.end_high()
            vo.end_x(0)
            vo.start_x(1)
            gate_w.start_high()
            up_w.start_line()

        squares = pair_sum(
            c,
            jnp.stack([jnp.sum(query * query, axis=1), jnp.sum(key_proj * key_proj, axis=1)]),
            squares_between,
        )
        q_rms = lax.rsqrt(squares[0] / model_width + EPSILON)[:, None]
        k_rms = lax.rsqrt(squares[1] / model_width + EPSILON)[:, None]
        normed_query = (query * q_rms * query_scale).astype(BF)
        normed_key = (key_proj * k_rms * key_scale).astype(BF)
        gate_w.start_x(0)
        down_w.start_line()
        vo.end_x(1)
        normed_query, normed_key = c.sync(normed_query, normed_key)
        wvo0, wvo1 = vo.rows(0), vo.rows(1)
        wv0, wo0 = wvo0[:, :head_width], wvo0[:, head_width:]
        wv1, wo1 = wvo1[:, :head_width], wvo1[:, head_width:]
        value_bf = (dot(in0, wv0) + dot(in1, wv1)).astype(BF)
        heads = (4, seq_length, local_heads, HD)
        query_heads = normed_query.reshape(heads)
        key_heads = normed_key.reshape(heads)
        value_heads = value_bf.reshape(heads)
        scores = (
            jnp.einsum("bqhd,bkhd->bhqk", query_heads, key_heads, preferred_element_type=F32)
            * score_scale
        )
        scores = jnp.where(visible, scores, NEGATIVE)
        peak = jnp.max(scores, axis=-1, keepdims=True)
        expo = jnp.exp(scores - peak)
        total = jnp.sum(expo, axis=-1, keepdims=True)
        prob = expo / total
        prob_bf = prob.astype(BF)
        attn_heads = jnp.einsum(
            "bhqk,bkhd->bqhd", prob_bf, value_heads, preferred_element_type=F32
        ).astype(BF)
        attn = attn_heads.reshape(group_tokens, head_width)
        attn = c.sync(attn)
        up_w.end_line()
        gate_w.end_x(0)
        up_w.start_x(0)
        down_w.end_line()
        gate_w.end_high()
        gate_w.start_x(1)
        up_w.start_high()

        def halve(total, axis):
            half = total.shape[0] // 2
            return total[:half], c.start(total[half:].astype(BF), axis)

        def added(pair):
            return pair[0] + c.sync(pair[1]).astype(F32)

        def cross(total):
            rows = own_tokens
            own = stack2(total[:rows], total[2 * rows : 3 * rows])
            sent = stack2(total[rows : 2 * rows], total[3 * rows :])
            return own, c.start(sent.astype(BF), "tensor")

        def scatter_rows(left_of, right_of, first=None, second=None):
            left_sent = c.start(left_of(other).astype(BF), "core")
            right_sent = c.start(right_of(other).astype(BF), "core")
            left = halve(left_of(own) + c.sync(left_sent).astype(F32), "zl")
            right = cross(right_of(own) + c.sync(right_sent).astype(F32))
            if first:
                first()
            left, right = added(left), added(right)
            left, right = halve(left, "tensor"), halve(right, "zl")
            if second:
                second()
            return added(left), added(right)

        def proj_second():
            up_w.end_x(0)
            up_w.end_high()
            gate_w.end_x(1)
            up_w.start_x(1)
            down_w.start_high()
            down_w.start_x(0)

        proj = columns(
            scatter_rows(
                lambda rows: dot_nt(attn[rows], wo0), lambda rows: dot_nt(attn[rows], wo1), None, proj_second
            )
        )
        attn_rms = rms_scale(proj)
        resid = tokens_f + proj * attn_rms * attn_scale

        def resid_last():
            up_w.end_x(1)
            down_w.end_high()
            down_w.end_x(0)
            down_w.start_x(1)

        h0, h1 = gather_rows(resid.astype(BF), None, resid_last)
        wg0, wg1 = gate_w.rows(0), gate_w.rows(1)
        gate = dot(h0, wg0) + dot(h1, wg1)
        sigma = jax.nn.sigmoid(gate)
        wu0, wu1 = up_w.rows(0), up_w.rows(1)
        up = dot(h0, wu0) + dot(h1, wu1)
        act = c.sync((gate * sigma * up).astype(BF))

        wd0 = down_w.rows(0)
        down_w.end_x(1)
        wd1 = down_w.rows(1)
        ffn = columns(
            scatter_rows(lambda rows: dot_nt(act[rows], wd0), lambda rows: dot_nt(act[rows], wd1))
        )

        ffn_rms = rms_scale(ffn)
        output = to_natural((resid + ffn * ffn_rms * ffn_scale).astype(BF))
        ffn_gain_term = jnp.sum(d_out * ffn * ffn_rms, axis=0)
        scaled_out = d_out * ffn_scale
        d_ffn = (
            ffn_rms
            * (
                scaled_out
                - ffn * ffn_rms * ffn_rms * jnp.mean(scaled_out * ffn, axis=1, keepdims=True)
            )
        ).astype(BF)
        f0, f1 = gather_rows(d_ffn)

        class Grad:
            def __init__(self, *terms):
                self.terms = terms
                self.x, self.total = [None, None], [None, None]

            def product(self, side, block):
                cols = slice(block * block_width, (block + 1) * block_width)
                return columns([dot_tn(halves[side][:, cols], r) for halves, r in self.terms])

            def start_x(self, block):
                self.x[block] = c.start(self.product(1, block).astype(BF), "x")

            def end_x(self, block):
                moved = c.sync(self.x[block])
                self.total[block] = self.product(0, block) + moved.astype(F32)

            def start_high(self):
                self.high = c.start(self.total[1].astype(BF), high_bits[0])

            def end_high(self):
                total = self.total[0] + c.sync(self.high).astype(F32)
                for name in high_bits[1:]:
                    total = added(halve(total, name))
                self.own, self.sent = split(total, "zl", 0)

            def start_line(self):
                self.line = c.start(self.sent.astype(BF), "zl")

            def joined(self, axis, moved, low=None):
                width = moved.shape[1] // len(self.terms)
                cols = [slice(i * width, (i + 1) * width) for i in range(len(self.terms))]
                if low is None:
                    return [ordered(axis, self.own[:, s], moved[:, s], dim=1) for s in cols]
                pairs = [(self.own[:, s], moved[:, s]) for s in cols]
                return [columns([jnp.where(low, a, b), jnp.where(low, b, a)]) for a, b in pairs]

            def end_line(self):
                moved = c.sync(self.line).astype(F32)
                self.own, sent = split(columns(self.joined("zl", moved)), "core", 0)
                self.core = c.start(sent.astype(BF), "core")

            def end(self):
                moved = c.sync(self.core).astype(F32)
                self.results = self.joined("core", moved, c.token[0, 0] == 0)

        down_grad = Grad(((f0, f1), act))
        down_grad.start_x(1)
        down_grad.start_x(0)
        f0, f1 = c.fence(f0, f1)
        d_act = dot(f0, wd0) + dot(f1, wd1)
        d_gate = (d_act * up * sigma * (1.0 + gate * (1.0 - sigma))).astype(BF)
        d_up = (d_act * gate * sigma).astype(BF)
        gate_grad = Grad(((h0, h1), d_gate))
        up_grad = Grad(((h0, h1), d_up))
        down_grad.end_x(1)
        down_grad.start_high()
        gate_grad.start_x(1)
        d_gate, d_up = c.fence(d_gate, d_up)

        def hidden_first():
            down_grad.end_x(0)
            gate_grad.start_x(0)

        def hidden_second():
            gate_grad.end_x(1)
            up_grad.start_x(1)
            down_grad.end_high()
            gate_grad.start_high()

        d_resid = d_out + columns(
            scatter_rows(
                lambda rows: dot_nt(d_gate[rows], wg0) + dot_nt(d_up[rows], wu0),
                lambda rows: dot_nt(d_gate[rows], wg1) + dot_nt(d_up[rows], wu1),
                hidden_first,
                hidden_second,
            )
        )
        attn_gain_term = jnp.sum(d_resid * proj * attn_rms, axis=0)
        scaled_resid = d_resid * attn_scale
        d_proj = (
            attn_rms
            * (
                scaled_resid
                - proj * attn_rms * attn_rms * jnp.mean(scaled_resid * proj, axis=1, keepdims=True)
            )
        ).astype(BF)

        def proj_between():
            down_grad.start_line()
            gate_grad.end_x(0)
            up_grad.start_x(0)

        def proj_last():
            up_grad.end_x(1)
            gate_grad.end_high()
            up_grad.start_high()
            gate_grad.start_line()

        p0, p1 = gather_rows(d_proj, proj_between, proj_last)
        up_grad.end_x(0)
        d_attn = (dot(p0, wo0) + dot(p1, wo1)).astype(BF)

        d_attn_heads = d_attn.reshape(heads)
        d_value = (
            jnp.einsum("bhqk,bqhd->bkhd", prob_bf, d_attn_heads, preferred_element_type=F32)
            .reshape(group_tokens, head_width)
            .astype(BF)
        )
        ov_grad = Grad(((p0, p1), attn), ((in0, in1), d_value))
        ov_grad.start_x(1)
        d_attn = c.fence(d_attn)
        d_attn_heads = d_attn.reshape(heads)
        d_prob = jnp.einsum(
            "bqhd,bkhd->bhqk", d_attn_heads, value_heads, preferred_element_type=F32
        )
        delta = jnp.einsum(
            "bqhd,bqhd->bhq", d_attn_heads, attn.reshape(heads), preferred_element_type=F32
        )[..., None]
        d_score = (prob * (d_prob - delta)).astype(BF)
        d_nq = (
            jnp.einsum("bhqk,bkhd->bqhd", d_score, key_heads, preferred_element_type=F32).reshape(
                group_tokens, head_width
            )
            * score_scale
        )
        d_nk = (
            jnp.einsum("bhqk,bqhd->bkhd", d_score, query_heads, preferred_element_type=F32).reshape(
                group_tokens, head_width
            )
            * score_scale
        )
        query_gain_term = jnp.sum(d_nq * query * q_rms, axis=0)
        key_gain_term = jnp.sum(d_nk * key_proj * k_rms, axis=0)
        scaled_q = d_nq * query_scale
        scaled_k = d_nk * key_scale
        zero = jnp.zeros((2, model_width), F32)
        placed = lax.dynamic_update_slice_in_dim(
            zero, jnp.stack([query_gain_term, key_gain_term]), head_start + c.zero, 1
        )
        gain_parts = jnp.concatenate(
            [to_relative(placed), jnp.stack([attn_gain_term, ffn_gain_term])], axis=0
        )
        gain_steps = Steps(scatter_gains(c, gain_parts))
        inner = c.sync(
            jnp.stack([jnp.sum(scaled_q * query, axis=1), jnp.sum(scaled_k * key_proj, axis=1)])
        )
        up_grad.end_high()
        ov_grad.end_x(1)
        ov_grad.start_high()
        down_grad.end_line()
        inner = pair_sum(c, inner, up_grad.start_line)
        gain_steps()
        d_query = (
            q_rms * (scaled_q - query * q_rms * q_rms * (inner[0] / model_width)[:, None])
        ).astype(BF)
        d_key = (
            k_rms * (scaled_k - key_proj * k_rms * k_rms * (inner[1] / model_width)[:, None])
        ).astype(BF)
        d_qk = columns([d_query, d_key])
        qk_grad = Grad(((in0, in1), d_query), ((in0, in1), d_key))
        qk_grad.start_x(1)
        gate_grad.end_line()
        down_grad.end()

        def tokens_first():
            ov_grad.high = c.sync(ov_grad.high)
            qk_grad.end_x(1)
            qk_grad.start_high()
            ov_grad.start_x(0)
            qk_grad.start_x(0)

        def tokens_second():
            gain_steps()
            up_grad.end_line()

        d_tokens = columns(
            scatter_rows(
                lambda rows: dot_nt(d_qk[rows], wqk0) + dot_nt(d_value[rows], wv0),
                lambda rows: dot_nt(d_qk[rows], wqk1) + dot_nt(d_value[rows], wv1),
                tokens_first,
                tokens_second,
            )
        )
        grad_tokens = to_natural(d_resid + d_tokens)
        qk_grad.end_x(0)
        qk_grad.end_high()
        qk_grad.start_line()
        ov_grad.end_x(0)
        ov_grad.end_high()
        ov_grad.start_line()
        gain_steps()
        gate_grad.end()
        gain_steps()
        qk_grad.end_line()
        ov_grad.end_line()
        gain_parts = gain_steps.finish()
        up_grad.end()
        qk_grad.end()
        ov_grad.end()
        grad_output, grad_value = ov_grad.results
        grad_query, grad_key = qk_grad.results
        return (
            output,
            grad_tokens,
            grad_query,
            grad_key,
            grad_value,
            grad_output,
            gate_grad.results[0],
            up_grad.results[0],
            down_grad.results[0],
            gain_parts[0],
            gain_parts[1],
            gain_parts[2],
            gain_parts[3],
        )

    return shards


def solution(mesh):
    dp = mesh.shape["dp"]
    high = max(dp.bit_length() - 4, 0)
    high_bits = tuple(f"z{i}" for i in range(high))
    names = high_bits + ("zl", "x", "core", "tensor")
    fine = Mesh(mesh.devices.reshape((2,) * len(names)), names)
    rows = names[:-1]
    both = names
    mapped = jax.shard_map(
        build(high_bits),
        mesh=fine,
        in_specs=(
            P(both, None),
            P(rows, None),
            P(rows, "tensor"),
            P(rows, "tensor"),
            P(rows, "tensor"),
            P(rows, "tensor"),
            P(rows, "tensor"),
            P(rows, "tensor"),
            P(rows, "tensor"),
            P(both),
            P(both),
            P(both),
            P(both),
            P(both, None),
        ),
        out_specs=(
            P(both, None),
            P(both, None),
            P(rows, "tensor"),
            P(rows, "tensor"),
            P(rows, "tensor"),
            P(rows, "tensor"),
            P(rows, "tensor"),
            P(rows, "tensor"),
            P(rows, "tensor"),
            P(both),
            P(both),
            P(both),
            P(both),
        ),
        check_vma=False,
    )
    return mapped
```

```python
import math

import jax
import jax.numpy as jnp
from jax import lax
from jax.sharding import Mesh, PartitionSpec as P

HD = 128

EPSILON = 1e-06
NEGATIVE = -1e30
FLIP = [(0, 1), (1, 0)]
BF = jnp.bfloat16
F32 = jnp.float32


def swap(value, axis):
    return lax.ppermute(value, axis, FLIP)


def bit(axis):
    return lax.axis_index(axis)


def pick(axis, low, high):
    return jnp.where(bit(axis) == 0, low, high)


def ordered(axis, own, other, dim=0):
    return jnp.concatenate([pick(axis, own, other), pick(axis, other, own)], axis=dim)


def split(value, axis, dim):
    half = value.shape[dim] // 2
    low = lax.slice_in_dim(value, 0, half, axis=dim)
    high = lax.slice_in_dim(value, half, 2 * half, axis=dim)
    return pick(axis, low, high), pick(axis, high, low)


def dot(a, b):
    return jnp.dot(a, b, preferred_element_type=F32)


def dot_nt(a, b):
    return jnp.einsum("sc,rc->sr", a, b, preferred_element_type=F32)


def dot_tn(a, b):
    return jnp.einsum("sr,sc->rc", a, b, preferred_element_type=F32)


def rms_scale(values):
    return lax.rsqrt(jnp.mean(values * values, axis=1, keepdims=True) + EPSILON)


def build(high_bits):
    def to_relative(value):
        rows, width = value.shape
        count = 2 ** (len(high_bits) + 2)
        run = width // count
        pieces = [value[:, i * run : (i + 1) * run] for i in range(count)]
        names = list(high_bits) + ["zl", "x"]
        for position, name in enumerate(names):
            if name == "zl":
                continue
            mask = 1 << (len(names) - 1 - position)
            pieces = [pick(name, pieces[i], pieces[i ^ mask]) for i in range(count)]
        order = []
        for xr in range(2):
            for rest in range(count // 2):
                order.append(rest * 2 + xr)
        return jnp.concatenate([pieces[i] for i in order], axis=1)

    def to_natural(value):
        rows, width = value.shape
        count = 2 ** (len(high_bits) + 2)
        run = width // count
        moved = [value[:, i * run : (i + 1) * run] for i in range(count)]
        pieces = [None] * count
        place = 0
        for xr in range(2):
            for rest in range(count // 2):
                pieces[rest * 2 + xr] = moved[place]
                place += 1
        names = list(high_bits) + ["zl", "x"]
        for position, name in enumerate(names):
            if name == "zl":
                continue
            mask = 1 << (len(names) - 1 - position)
            pieces = [pick(name, pieces[i], pieces[i ^ mask]) for i in range(count)]
        return jnp.concatenate(pieces, axis=1)

    class Chain:
        def __init__(self, token):
            self.token = token
            self.zero = jnp.int32(0)

        def sync(self, *values):
            out = lax.optimization_barrier((self.token,) + values)
            self.token = out[0]
            return out[1] if len(values) == 1 else out[1:]

        def start(self, value, axis):
            return swap(self.sync(value), axis)

        def fence(self, *values):
            moved = self.sync(self.start(jnp.full((1, HD), bit("core"), jnp.int32), "core"))
            self.zero = self.zero + (moved[0, 0] + bit("core") - 1)
            return self.sync(*values)

    def gather_gains(c, gains):
        for name in ("tensor", "core", "zl"):
            sent = c.start(gains, name)
            yield
            gains = ordered(name, gains, c.sync(sent), dim=1)
        for name in list(high_bits)[::-1] + ["x"]:
            sent = c.start(gains, name)
            yield
            gains = jnp.concatenate([gains, c.sync(sent)], axis=1)
        return gains

    def pair_sum(c, values, between=None):
        count, width = values.shape
        for level, axis in ((1, "zl"), (2, "tensor"), (0, "core")):
            run = width >> (level + 1)
            other = c.sync(c.start(values, axis))
            blocks = [other[:, i * run : (i + 1) * run] for i in range(width // run)]
            values = values + jnp.concatenate([blocks[i ^ 1] for i in range(len(blocks))], axis=1)
            if between and axis == "zl":
                between()
        return values

    def scatter_gains(c, gains):
        for name in ["x"] + list(high_bits):
            half = gains.shape[1] // 2
            sent = c.start(gains[:, half:], name)
            yield
            gains = gains[:, :half] + c.sync(sent)
        for name in ("zl", "core", "tensor"):
            own, sent = split(gains, name, 1)
            sent = c.start(sent, name)
            yield
            gains = own + c.sync(sent)
        return gains

    class Steps:
        def __init__(self, stages):
            self.stages, self.done = stages, False
            self()

        def __call__(self):
            if not self.done:
                try:
                    next(self.stages)
                except StopIteration as end:
                    self.value, self.done = end.value, True

        def finish(self):
            while not self.done:
                self()
            return self.value

    def stack2(low, high):
        return jnp.concatenate([low, high], axis=0)

    def shards(
        tokens,
        segment_ids,
        w_query,
        w_key,
        w_value,
        w_output,
        w_gate,
        w_up,
        w_down,
        query_gain,
        key_gain,
        attn_gain,
        ffn_gain,
        cotangent,
    ):
        own_tokens, model_width = tokens.shape
        half_width = model_width // 2
        block_width = half_width // 2
        seq_length = own_tokens * 2
        core_tokens = seq_length * 2
        group_tokens = core_tokens * 2
        head_width = w_query.shape[1] // 4
        local_heads = head_width // HD
        score_scale = 1.0 / math.sqrt(HD)
        own, other = slice(0, core_tokens), slice(core_tokens, group_tokens)
        c = Chain(jnp.full((1, HD), bit("core"), jnp.int32))

        def columns(parts):
            return parts[0] if len(parts) == 1 else jnp.concatenate(parts, axis=1)

        class Weight:
            def __init__(self, matrices, sent):
                width = sent.shape[1] // len(matrices)
                pairs = [
                    split(ordered("core", m, sent[:, i * width : (i + 1) * width]), "zl", 1)
                    for i, m in enumerate(matrices)
                ]
                self.own = columns([p[0] for p in pairs])
                self.sent = columns([p[1] for p in pairs])
                self.blocks = [[None, None], [None, None]]

            def start_line(self):
                self.line = c.start(self.sent, "zl")

            def end_line(self):
                rows = ordered("zl", self.own, c.sync(self.line))
                for name in high_bits[:0:-1]:
                    rows = stack2(rows, c.sync(c.start(rows, name)))
                self.blocks[0][0] = rows

            def start_high(self):
                self.high = c.start(self.blocks[0][0], high_bits[0])

            def end_high(self):
                self.blocks[0][1] = c.sync(self.high)

            def start_x(self, block):
                self.blocks[1][block] = c.start(self.blocks[0][block], "x")

            def end_x(self, block):
                self.blocks[1][block] = c.sync(self.blocks[1][block])

            def rows(self, side):
                return stack2(*self.blocks[side])

        attn_split = [split(w, "core", 1) for w in (w_query, w_key, w_value, w_output)]
        attn_sent = c.start(columns([s[1] for s in attn_split]), "core")
        gains = jnp.stack([query_gain, key_gain, attn_gain, ffn_gain])
        gain_steps = Steps(gather_gains(c, gains))
        tokens_rel = to_relative(tokens)
        left, right = tokens_rel[:, :half_width], tokens_rel[:, half_width:]
        left_sent = c.start(left, "tensor")
        gain_steps()

        attn_sent = c.sync(attn_sent)
        pair_width = 4 * head_width
        qk = Weight([s[0] for s in attn_split[:2]], attn_sent[:, :pair_width])
        vo = Weight([s[0] for s in attn_split[2:]], attn_sent[:, pair_width:])
        qk.start_line()
        gain_steps()
        ids = jnp.concatenate(
            [
                pick("tensor", segment_ids[:, :own_tokens], segment_ids[:, own_tokens:]),
                pick("tensor", segment_ids[:, own_tokens:], segment_ids[:, :own_tokens]),
            ],
            axis=1,
        )
        ids_sent = c.start(ids, "zl")
        ffn_split = [split(w, "core", 1) for w in (w_gate, w_up, w_down)]
        ffn_sent = c.start(columns([s[1] for s in ffn_split]), "core")
        qk.end_line()
        gain_steps()
        qk.start_x(0)
        qk.start_high()
        right_sent = c.start(right, "zl")
        vo.start_line()
        left = stack2(left, c.sync(left_sent))
        seq_ids = stack2(ids, c.sync(ids_sent))
        ids_sent = c.start(seq_ids, "core")
        right = stack2(right, c.sync(right_sent))

        def rows_second(left, right, between=None, last=None):
            left_sent = c.start(left, "zl")
            right_sent = c.start(right, "tensor")
            if between:
                between()
            left = stack2(left, c.sync(left_sent))
            right_sent = c.sync(right_sent)
            rows = own_tokens
            right = jnp.concatenate(
                [right[:rows], right_sent[:rows], right[rows:], right_sent[rows:]], axis=0
            )
            if last:
                last()
            left_sent = c.start(left, "core")
            right_sent = c.start(right, "core")
            return stack2(left, c.sync(left_sent)), stack2(right, c.sync(right_sent))

        def gather_rows(value, between=None, last=None):
            left, right = value[:, :half_width], value[:, half_width:]
            left_sent = c.start(left, "tensor")
            right_sent = c.start(right, "zl")
            left = stack2(left, c.sync(left_sent))
            right = stack2(right, c.sync(right_sent))
            return rows_second(left, right, between, last)

        ffn_sent = c.sync(ffn_sent)
        width = ffn_sent.shape[1] // 3
        gate_w, up_w, down_w = [
            Weight([s[0]], ffn_sent[:, i * width : (i + 1) * width])
            for i, s in enumerate(ffn_split)
        ]

        def tokens_between():
            vo.end_line()
            gate_w.start_line()
            gain_steps()
            qk.end_x(0)
            vo.start_x(0)
            qk.end_high()
            qk.start_x(1)
            vo.start_high()

        in0, in1 = rows_second(left, right, tokens_between)
        seq_ids = stack2(seq_ids, c.sync(ids_sent))
        gate_w.end_line()
        gains = gain_steps.finish()
        qk.end_x(1)

        attn_scale = gains[2]
        ffn_scale = gains[3]
        head_gains = to_natural(gains[:2])
        head_start = (bit("tensor") * 4 + bit("core") * 2 + bit("zl")) * head_width
        head_gains = lax.dynamic_slice_in_dim(head_gains, head_start, head_width, axis=1)
        query_scale, key_scale = head_gains[0], head_gains[1]
        tokens_f = tokens_rel.astype(F32)
        d_out = to_relative(cotangent).astype(F32)
        places = jnp.arange(own_tokens)
        positions = jnp.concatenate(
            [places + bit("tensor") * own_tokens, places + (1 - bit("tensor")) * own_tokens]
        )
        visible = (positions[:, None] >= positions[None, :])[None] & (
            seq_ids[:, :, None] == seq_ids[:, None, :]
        )
        visible = visible[:, None]

        wqk0, wqk1 = qk.rows(0), qk.rows(1)
        projected = dot(in0, wqk0) + dot(in1, wqk1)
        query, key_proj = projected[:, :head_width], projected[:, head_width:]

        def squares_between():
            vo.end_high()
            vo.end_x(0)
            vo.start_x(1)
            gate_w.start_high()
            up_w.start_line()

        squares = pair_sum(
            c,
            jnp.stack([jnp.sum(query * query, axis=1), jnp.sum(key_proj * key_proj, axis=1)]),
            squares_between,
        )
        q_rms = lax.rsqrt(squares[0] / model_width + EPSILON)[:, None]
        k_rms = lax.rsqrt(squares[1] / model_width + EPSILON)[:, None]
        normed_query = (query * q_rms * query_scale).astype(BF)
        normed_key = (key_proj * k_rms * key_scale).astype(BF)
        gate_w.start_x(0)
        down_w.start_line()
        vo.end_x(1)
        normed_query, normed_key = c.sync(normed_query, normed_key)
        wvo0, wvo1 = vo.rows(0), vo.rows(1)
        wv0, wo0 = wvo0[:, :head_width], wvo0[:, head_width:]
        wv1, wo1 = wvo1[:, :head_width], wvo1[:, head_width:]
        value_bf = (dot(in0, wv0) + dot(in1, wv1)).astype(BF)
        heads = (4, seq_length, local_heads, HD)
        query_heads = normed_query.reshape(heads)
        key_heads = normed_key.reshape(heads)
        value_heads = value_bf.reshape(heads)
        scores = (
            jnp.einsum("bqhd,bkhd->bhqk", query_heads, key_heads, preferred_element_type=F32)
            * score_scale
        )
        scores = jnp.where(visible, scores, NEGATIVE)
        peak = jnp.max(scores, axis=-1, keepdims=True)
        expo = jnp.exp(scores - peak)
        total = jnp.sum(expo, axis=-1, keepdims=True)
        prob = expo / total
        prob_bf = prob.astype(BF)
        attn_heads = jnp.einsum(
            "bhqk,bkhd->bqhd", prob_bf, value_heads, preferred_element_type=F32
        ).astype(BF)
        attn = attn_heads.reshape(group_tokens, head_width)
        attn = c.sync(attn)
        up_w.end_line()
        gate_w.end_x(0)
        up_w.start_x(0)
        down_w.end_line()
        gate_w.end_high()
        gate_w.start_x(1)
        up_w.start_high()

        def halve(total, axis):
            half = total.shape[0] // 2
            return total[:half], c.start(total[half:].astype(BF), axis)

        def added(pair):
            return pair[0] + c.sync(pair[1]).astype(F32)

        def cross(total):
            rows = own_tokens
            own = stack2(total[:rows], total[2 * rows : 3 * rows])
            sent = stack2(total[rows : 2 * rows], total[3 * rows :])
            return own, c.start(sent.astype(BF), "tensor")

        def scatter_rows(left_of, right_of, first=None, second=None):
            left_sent = c.start(left_of(other).astype(BF), "core")
            right_sent = c.start(right_of(other).astype(BF), "core")
            left = halve(left_of(own) + c.sync(left_sent).astype(F32), "zl")
            right = cross(right_of(own) + c.sync(right_sent).astype(F32))
            if first:
                first()
            left, right = added(left), added(right)
            left, right = halve(left, "tensor"), halve(right, "zl")
            if second:
                second()
            return added(left), added(right)

        def proj_second():
            up_w.end_x(0)
            up_w.end_high()
            gate_w.end_x(1)
            up_w.start_x(1)
            down_w.start_high()
            down_w.start_x(0)

        proj = columns(
            scatter_rows(
                lambda rows: dot_nt(attn[rows], wo0), lambda rows: dot_nt(attn[rows], wo1), None, proj_second
            )
        )
        attn_rms = rms_scale(proj)
        resid = tokens_f + proj * attn_rms * attn_scale

        def resid_last():
            up_w.end_x(1)
            down_w.end_high()
            down_w.end_x(0)
            down_w.start_x(1)

        h0, h1 = gather_rows(resid.astype(BF), None, resid_last)
        wg0, wg1 = gate_w.rows(0), gate_w.rows(1)
        gate = dot(h0, wg0) + dot(h1, wg1)
        sigma = jax.nn.sigmoid(gate)
        wu0, wu1 = up_w.rows(0), up_w.rows(1)
        up = dot(h0, wu0) + dot(h1, wu1)
        act = c.sync((gate * sigma * up).astype(BF))

        wd0 = down_w.rows(0)
        down_w.end_x(1)
        wd1 = down_w.rows(1)
        ffn = columns(
            scatter_rows(lambda rows: dot_nt(act[rows], wd0), lambda rows: dot_nt(act[rows], wd1))
        )

        ffn_rms = rms_scale(ffn)
        output = to_natural((resid + ffn * ffn_rms * ffn_scale).astype(BF))
        ffn_gain_term = jnp.sum(d_out * ffn * ffn_rms, axis=0)
        scaled_out = d_out * ffn_scale
        d_ffn = (
            ffn_rms
            * (
                scaled_out
                - ffn * ffn_rms * ffn_rms * jnp.mean(scaled_out * ffn, axis=1, keepdims=True)
            )
        ).astype(BF)
        f0, f1 = gather_rows(d_ffn)

        class Grad:
            def __init__(self, *terms):
                self.terms = terms
                self.x, self.total = [None, None], [None, None]

            def product(self, side, block):
                cols = slice(block * block_width, (block + 1) * block_width)
                return columns([dot_tn(halves[side][:, cols], r) for halves, r in self.terms])

            def start_x(self, block):
                self.x[block] = c.start(self.product(1, block).astype(BF), "x")

            def end_x(self, block):
                moved = c.sync(self.x[block])
                self.total[block] = self.product(0, block) + moved.astype(F32)

            def start_high(self):
                self.high = c.start(self.total[1].astype(BF), high_bits[0])

            def end_high(self):
                total = self.total[0] + c.sync(self.high).astype(F32)
                for name in high_bits[1:]:
                    total = added(halve(total, name))
                self.own, self.sent = split(total, "zl", 0)

            def start_line(self):
                self.line = c.start(self.sent.astype(BF), "zl")

            def joined(self, axis, moved, low=None):
                width = moved.shape[1] // len(self.terms)
                cols = [slice(i * width, (i + 1) * width) for i in range(len(self.terms))]
                if low is None:
                    return [ordered(axis, self.own[:, s], moved[:, s], dim=1) for s in cols]
                pairs = [(self.own[:, s], moved[:, s]) for s in cols]
                return [columns([jnp.where(low, a, b), jnp.where(low, b, a)]) for a, b in pairs]

            def end_line(self):
                moved = c.sync(self.line).astype(F32)
                self.own, sent = split(columns(self.joined("zl", moved)), "core", 0)
                self.core = c.start(sent.astype(BF), "core")

            def end(self):
                moved = c.sync(self.core).astype(F32)
                self.results = self.joined("core", moved, c.token[0, 0] == 0)

        down_grad = Grad(((f0, f1), act))
        down_grad.start_x(1)
        down_grad.start_x(0)
        f0, f1 = c.fence(f0, f1)
        d_act = dot(f0, wd0) + dot(f1, wd1)
        d_gate = (d_act * up * sigma * (1.0 + gate * (1.0 - sigma))).astype(BF)
        d_up = (d_act * gate * sigma).astype(BF)
        gate_grad = Grad(((h0, h1), d_gate))
        up_grad = Grad(((h0, h1), d_up))
        down_grad.end_x(1)
        down_grad.start_high()
        gate_grad.start_x(1)
        d_gate, d_up = c.fence(d_gate, d_up)

        def hidden_first():
            down_grad.end_x(0)
            gate_grad.start_x(0)

        def hidden_second():
            gate_grad.end_x(1)
            up_grad.start_x(1)
            down_grad.end_high()
            gate_grad.start_high()

        d_resid = d_out + columns(
            scatter_rows(
                lambda rows: dot_nt(d_gate[rows], wg0) + dot_nt(d_up[rows], wu0),
                lambda rows: dot_nt(d_gate[rows], wg1) + dot_nt(d_up[rows], wu1),
                hidden_first,
                hidden_second,
            )
        )
        attn_gain_term = jnp.sum(d_resid * proj * attn_rms, axis=0)
        scaled_resid = d_resid * attn_scale
        d_proj = (
            attn_rms
            * (
                scaled_resid
                - proj * attn_rms * attn_rms * jnp.mean(scaled_resid * proj, axis=1, keepdims=True)
            )
        ).astype(BF)

        def proj_between():
            down_grad.start_line()
            gate_grad.end_x(0)
            up_grad.start_x(0)

        def proj_last():
            up_grad.end_x(1)
            gate_grad.end_high()
            up_grad.start_high()
            gate_grad.start_line()

        p0, p1 = gather_rows(d_proj, proj_between, proj_last)
        up_grad.end_x(0)
        d_attn = (dot(p0, wo0) + dot(p1, wo1)).astype(BF)

        d_attn_heads = d_attn.reshape(heads)
        d_value = (
            jnp.einsum("bhqk,bqhd->bkhd", prob_bf, d_attn_heads, preferred_element_type=F32)
            .reshape(group_tokens, head_width)
            .astype(BF)
        )
        ov_grad = Grad(((p0, p1), attn), ((in0, in1), d_value))
        ov_grad.start_x(1)
        d_attn = c.fence(d_attn)
        d_attn_heads = d_attn.reshape(heads)
        d_prob = jnp.einsum(
            "bqhd,bkhd->bhqk", d_attn_heads, value_heads, preferred_element_type=F32
        )
        delta = jnp.einsum(
            "bqhd,bqhd->bhq", d_attn_heads, attn.reshape(heads), preferred_element_type=F32
        )[..., None]
        d_score = (prob * (d_prob - delta)).astype(BF)
        d_nq = (
            jnp.einsum("bhqk,bkhd->bqhd", d_score, key_heads, preferred_element_type=F32).reshape(
                group_tokens, head_width
            )
            * score_scale
        )
        d_nk = (
            jnp.einsum("bhqk,bqhd->bkhd", d_score, query_heads, preferred_element_type=F32).reshape(
                group_tokens, head_width
            )
            * score_scale
        )
        query_gain_term = jnp.sum(d_nq * query * q_rms, axis=0)
        key_gain_term = jnp.sum(d_nk * key_proj * k_rms, axis=0)
        scaled_q = d_nq * query_scale
        scaled_k = d_nk * key_scale
        zero = jnp.zeros((2, model_width), F32)
        placed = lax.dynamic_update_slice_in_dim(
            zero, jnp.stack([query_gain_term, key_gain_term]), head_start + c.zero, 1
        )
        gain_parts = jnp.concatenate(
            [to_relative(placed), jnp.stack([attn_gain_term, ffn_gain_term])], axis=0
        )
        gain_steps = Steps(scatter_gains(c, gain_parts))
        inner = c.sync(
            jnp.stack([jnp.sum(scaled_q * query, axis=1), jnp.sum(scaled_k * key_proj, axis=1)])
        )
        up_grad.end_high()
        ov_grad.end_x(1)
        ov_grad.start_high()
        down_grad.end_line()
        inner = pair_sum(c, inner, up_grad.start_line)
        gain_steps()
        d_query = (
            q_rms * (scaled_q - query * q_rms * q_rms * (inner[0] / model_width)[:, None])
        ).astype(BF)
        d_key = (
            k_rms * (scaled_k - key_proj * k_rms * k_rms * (inner[1] / model_width)[:, None])
        ).astype(BF)
        d_qk = columns([d_query, d_key])
        qk_grad = Grad(((in0, in1), d_query), ((in0, in1), d_key))
        qk_grad.start_x(1)
        gate_grad.end_line()
        down_grad.end()

        def tokens_first():
            ov_grad.high = c.sync(ov_grad.high)
            qk_grad.end_x(1)
            qk_grad.start_high()
            ov_grad.start_x(0)
            qk_grad.start_x(0)

        def tokens_second():
            gain_steps()
            up_grad.end_line()

        d_tokens = columns(
            scatter_rows(
                lambda rows: dot_nt(d_qk[rows], wqk0) + dot_nt(d_value[rows], wv0),
                lambda rows: dot_nt(d_qk[rows], wqk1) + dot_nt(d_value[rows], wv1),
                tokens_first,
                tokens_second,
            )
        )
        grad_tokens = to_natural(d_resid + d_tokens)
        ov_grad.end_x(0)
        ov_grad.end_high()
        ov_grad.start_line()
        qk_grad.end_x(0)
        qk_grad.end_high()
        qk_grad.start_line()
        gain_steps()
        gate_grad.end()
        ov_grad.end_line()
        gain_steps()
        up_grad.end()
        ov_grad.end()
        qk_grad.end_line()
        gain_parts = gain_steps.finish()
        qk_grad.end()
        grad_output, grad_value = ov_grad.results
        grad_query, grad_key = qk_grad.results
        return (
            output,
            grad_tokens,
            grad_query,
            grad_key,
            grad_value,
            grad_output,
            gate_grad.results[0],
            up_grad.results[0],
            down_grad.results[0],
            gain_parts[0],
            gain_parts[1],
            gain_parts[2],
            gain_parts[3],
        )

    return shards


def solution(mesh):
    dp = mesh.shape["dp"]
    high = max(dp.bit_length() - 4, 0)
    high_bits = tuple(f"z{i}" for i in range(high))
    names = high_bits + ("zl", "x", "core", "tensor")
    fine = Mesh(mesh.devices.reshape((2,) * len(names)), names)
    rows = names[:-1]
    both = names
    mapped = jax.shard_map(
        build(high_bits),
        mesh=fine,
        in_specs=(
            P(both, None),
            P(rows, None),
            P(rows, "tensor"),
            P(rows, "tensor"),
            P(rows, "tensor"),
            P(rows, "tensor"),
            P(rows, "tensor"),
            P(rows, "tensor"),
            P(rows, "tensor"),
            P(both),
            P(both),
            P(both),
            P(both),
            P(both, None),
        ),
        out_specs=(
            P(both, None),
            P(both, None),
            P(rows, "tensor"),
            P(rows, "tensor"),
            P(rows, "tensor"),
            P(rows, "tensor"),
            P(rows, "tensor"),
            P(rows, "tensor"),
            P(rows, "tensor"),
            P(both),
            P(both),
            P(both),
            P(both),
        ),
        check_vma=False,
    )
    return mapped
```

```python
import math

import jax
import jax.numpy as jnp
from jax import lax
from jax.sharding import Mesh, PartitionSpec as P

HD = 128

EPSILON = 1e-06
NEGATIVE = -1e30
FLIP = [(0, 1), (1, 0)]
BF = jnp.bfloat16
F32 = jnp.float32


def swap(value, axis):
    return lax.ppermute(value, axis, FLIP)


def bit(axis):
    return lax.axis_index(axis)


def pick(axis, low, high):
    return jnp.where(bit(axis) == 0, low, high)


def ordered(axis, own, other, dim=0):
    return jnp.concatenate([pick(axis, own, other), pick(axis, other, own)], axis=dim)


def split(value, axis, dim):
    half = value.shape[dim] // 2
    low = lax.slice_in_dim(value, 0, half, axis=dim)
    high = lax.slice_in_dim(value, half, 2 * half, axis=dim)
    return pick(axis, low, high), pick(axis, high, low)


def dot(a, b):
    return jnp.dot(a, b, preferred_element_type=F32)


def dot_nt(a, b):
    return jnp.einsum("sc,rc->sr", a, b, preferred_element_type=F32)


def dot_tn(a, b):
    return jnp.einsum("sr,sc->rc", a, b, preferred_element_type=F32)


def rms_scale(values):
    return lax.rsqrt(jnp.mean(values * values, axis=1, keepdims=True) + EPSILON)


def build(high_bits):
    def to_relative(value):
        rows, width = value.shape
        count = 2 ** (len(high_bits) + 2)
        run = width // count
        pieces = [value[:, i * run : (i + 1) * run] for i in range(count)]
        names = list(high_bits) + ["zl", "x"]
        for position, name in enumerate(names):
            if name == "zl":
                continue
            mask = 1 << (len(names) - 1 - position)
            pieces = [pick(name, pieces[i], pieces[i ^ mask]) for i in range(count)]
        order = []
        for xr in range(2):
            for rest in range(count // 2):
                order.append(rest * 2 + xr)
        return jnp.concatenate([pieces[i] for i in order], axis=1)

    def to_natural(value):
        rows, width = value.shape
        count = 2 ** (len(high_bits) + 2)
        run = width // count
        moved = [value[:, i * run : (i + 1) * run] for i in range(count)]
        pieces = [None] * count
        place = 0
        for xr in range(2):
            for rest in range(count // 2):
                pieces[rest * 2 + xr] = moved[place]
                place += 1
        names = list(high_bits) + ["zl", "x"]
        for position, name in enumerate(names):
            if name == "zl":
                continue
            mask = 1 << (len(names) - 1 - position)
            pieces = [pick(name, pieces[i], pieces[i ^ mask]) for i in range(count)]
        return jnp.concatenate(pieces, axis=1)

    class Chain:
        def __init__(self, token):
            self.token = token
            self.zero = jnp.int32(0)

        def sync(self, *values):
            out = lax.optimization_barrier((self.token,) + values)
            self.token = out[0]
            return out[1] if len(values) == 1 else out[1:]

        def start(self, value, axis):
            return swap(self.sync(value), axis)

        def fence(self, *values):
            moved = self.sync(self.start(jnp.full((1, HD), bit("core"), jnp.int32), "core"))
            self.zero = self.zero + (moved[0, 0] + bit("core") - 1)
            return self.sync(*values)

    def gather_gains(c, gains):
        for name in ("tensor", "core", "zl"):
            sent = c.start(gains, name)
            yield
            gains = ordered(name, gains, c.sync(sent), dim=1)
        for name in list(high_bits)[::-1] + ["x"]:
            sent = c.start(gains, name)
            yield
            gains = jnp.concatenate([gains, c.sync(sent)], axis=1)
        return gains

    def pair_sum(c, values, between=None):
        count, width = values.shape
        for level, axis in ((1, "zl"), (2, "tensor"), (0, "core")):
            run = width >> (level + 1)
            other = c.sync(c.start(values, axis))
            blocks = [other[:, i * run : (i + 1) * run] for i in range(width // run)]
            values = values + jnp.concatenate([blocks[i ^ 1] for i in range(len(blocks))], axis=1)
            if between and axis == "zl":
                between()
        return values

    def scatter_gains(c, gains):
        for name in ["x"] + list(high_bits):
            half = gains.shape[1] // 2
            sent = c.start(gains[:, half:], name)
            yield
            gains = gains[:, :half] + c.sync(sent)
        for name in ("zl", "core", "tensor"):
            own, sent = split(gains, name, 1)
            sent = c.start(sent, name)
            yield
            gains = own + c.sync(sent)
        return gains

    class Steps:
        def __init__(self, stages):
            self.stages, self.done = stages, False
            self()

        def __call__(self):
            if not self.done:
                try:
                    next(self.stages)
                except StopIteration as end:
                    self.value, self.done = end.value, True

        def finish(self):
            while not self.done:
                self()
            return self.value

    def stack2(low, high):
        return jnp.concatenate([low, high], axis=0)

    def shards(
        tokens,
        segment_ids,
        w_query,
        w_key,
        w_value,
        w_output,
        w_gate,
        w_up,
        w_down,
        query_gain,
        key_gain,
        attn_gain,
        ffn_gain,
        cotangent,
    ):
        own_tokens, model_width = tokens.shape
        half_width = model_width // 2
        block_width = half_width // 2
        seq_length = own_tokens * 2
        core_tokens = seq_length * 2
        group_tokens = core_tokens * 2
        head_width = w_query.shape[1] // 4
        local_heads = head_width // HD
        score_scale = 1.0 / math.sqrt(HD)
        own, other = slice(0, core_tokens), slice(core_tokens, group_tokens)
        c = Chain(jnp.full((1, HD), bit("core"), jnp.int32))

        def columns(parts):
            return parts[0] if len(parts) == 1 else jnp.concatenate(parts, axis=1)

        class Weight:
            def __init__(self, matrices, sent):
                width = sent.shape[1] // len(matrices)
                pairs = [
                    split(ordered("core", m, sent[:, i * width : (i + 1) * width]), "zl", 1)
                    for i, m in enumerate(matrices)
                ]
                self.own = columns([p[0] for p in pairs])
                self.sent = columns([p[1] for p in pairs])
                self.blocks = [[None, None], [None, None]]

            def start_line(self):
                self.line = c.start(self.sent, "zl")

            def end_line(self):
                rows = ordered("zl", self.own, c.sync(self.line))
                for name in high_bits[:0:-1]:
                    rows = stack2(rows, c.sync(c.start(rows, name)))
                self.blocks[0][0] = rows

            def start_high(self):
                self.high = c.start(self.blocks[0][0], high_bits[0])

            def end_high(self):
                self.blocks[0][1] = c.sync(self.high)

            def start_x(self, block):
                self.blocks[1][block] = c.start(self.blocks[0][block], "x")

            def end_x(self, block):
                self.blocks[1][block] = c.sync(self.blocks[1][block])

            def rows(self, side):
                return stack2(*self.blocks[side])

        attn_split = [split(w, "core", 1) for w in (w_query, w_key, w_value, w_output)]
        attn_sent = c.start(columns([s[1] for s in attn_split]), "core")
        gains = jnp.stack([query_gain, key_gain, attn_gain, ffn_gain])
        gain_steps = Steps(gather_gains(c, gains))
        tokens_rel = to_relative(tokens)
        left, right = tokens_rel[:, :half_width], tokens_rel[:, half_width:]
        left_sent = c.start(left, "tensor")
        gain_steps()

        attn_sent = c.sync(attn_sent)
        pair_width = 4 * head_width
        qk = Weight([s[0] for s in attn_split[:2]], attn_sent[:, :pair_width])
        vo = Weight([s[0] for s in attn_split[2:]], attn_sent[:, pair_width:])
        qk.start_line()
        gain_steps()
        ids = jnp.concatenate(
            [
                pick("tensor", segment_ids[:, :own_tokens], segment_ids[:, own_tokens:]),
                pick("tensor", segment_ids[:, own_tokens:], segment_ids[:, :own_tokens]),
            ],
            axis=1,
        )
        ids_sent = c.start(ids, "zl")
        ffn_split = [split(w, "core", 1) for w in (w_gate, w_up, w_down)]
        ffn_sent = c.start(columns([s[1] for s in ffn_split]), "core")
        qk.end_line()
        gain_steps()
        qk.start_x(0)
        qk.start_high()
        right_sent = c.start(right, "zl")
        vo.start_line()
        left = stack2(left, c.sync(left_sent))
        seq_ids = stack2(ids, c.sync(ids_sent))
        ids_sent = c.start(seq_ids, "core")
        right = stack2(right, c.sync(right_sent))

        def rows_second(left, right, between=None, last=None):
            left_sent = c.start(left, "zl")
            right_sent = c.start(right, "tensor")
            if between:
                between()
            left = stack2(left, c.sync(left_sent))
            right_sent = c.sync(right_sent)
            rows = own_tokens
            right = jnp.concatenate(
                [right[:rows], right_sent[:rows], right[rows:], right_sent[rows:]], axis=0
            )
            if last:
                last()
            left_sent = c.start(left, "core")
            right_sent = c.start(right, "core")
            return stack2(left, c.sync(left_sent)), stack2(right, c.sync(right_sent))

        def gather_rows(value, between=None, last=None):
            left, right = value[:, :half_width], value[:, half_width:]
            left_sent = c.start(left, "tensor")
            right_sent = c.start(right, "zl")
            left = stack2(left, c.sync(left_sent))
            right = stack2(right, c.sync(right_sent))
            return rows_second(left, right, between, last)

        ffn_sent = c.sync(ffn_sent)
        width = ffn_sent.shape[1] // 3
        gate_w, up_w, down_w = [
            Weight([s[0]], ffn_sent[:, i * width : (i + 1) * width])
            for i, s in enumerate(ffn_split)
        ]

        def tokens_between():
            vo.end_line()
            gate_w.start_line()
            gain_steps()
            qk.end_x(0)
            vo.start_x(0)
            qk.end_high()
            qk.start_x(1)
            vo.start_high()

        in0, in1 = rows_second(left, right, tokens_between)
        seq_ids = stack2(seq_ids, c.sync(ids_sent))
        gate_w.end_line()
        gains = gain_steps.finish()
        qk.end_x(1)
        vo.end_high()
        vo.end_x(0)
        vo.start_x(1)
        gate_w.start_high()

        attn_scale = gains[2]
        ffn_scale = gains[3]
        head_gains = to_natural(gains[:2])
        head_start = (bit("tensor") * 4 + bit("core") * 2 + bit("zl")) * head_width
        head_gains = lax.dynamic_slice_in_dim(head_gains, head_start, head_width, axis=1)
        query_scale, key_scale = head_gains[0], head_gains[1]
        tokens_f = tokens_rel.astype(F32)
        d_out = to_relative(cotangent).astype(F32)
        places = jnp.arange(own_tokens)
        positions = jnp.concatenate(
            [places + bit("tensor") * own_tokens, places + (1 - bit("tensor")) * own_tokens]
        )
        visible = (positions[:, None] >= positions[None, :])[None] & (
            seq_ids[:, :, None] == seq_ids[:, None, :]
        )
        visible = visible[:, None]

        wqk0, wqk1 = qk.rows(0), qk.rows(1)
        projected = dot(in0, wqk0) + dot(in1, wqk1)
        query, key_proj = projected[:, :head_width], projected[:, head_width:]

        def squares_between():
            up_w.start_line()

        squares = pair_sum(
            c,
            jnp.stack([jnp.sum(query * query, axis=1), jnp.sum(key_proj * key_proj, axis=1)]),
            squares_between,
        )
        q_rms = lax.rsqrt(squares[0] / model_width + EPSILON)[:, None]
        k_rms = lax.rsqrt(squares[1] / model_width + EPSILON)[:, None]
        normed_query = (query * q_rms * query_scale).astype(BF)
        normed_key = (key_proj * k_rms * key_scale).astype(BF)
        gate_w.start_x(0)
        down_w.start_line()
        vo.end_x(1)
        normed_query, normed_key = c.sync(normed_query, normed_key)
        wvo0, wvo1 = vo.rows(0), vo.rows(1)
        wv0, wo0 = wvo0[:, :head_width], wvo0[:, head_width:]
        wv1, wo1 = wvo1[:, :head_width], wvo1[:, head_width:]
        value_bf = (dot(in0, wv0) + dot(in1, wv1)).astype(BF)
        heads = (4, seq_length, local_heads, HD)
        query_heads = normed_query.reshape(heads)
        key_heads = normed_key.reshape(heads)
        value_heads = value_bf.reshape(heads)
        scores = (
            jnp.einsum("bqhd,bkhd->bhqk", query_heads, key_heads, preferred_element_type=F32)
            * score_scale
        )
        scores = jnp.where(visible, scores, NEGATIVE)
        peak = jnp.max(scores, axis=-1, keepdims=True)
        expo = jnp.exp(scores - peak)
        total = jnp.sum(expo, axis=-1, keepdims=True)
        prob = expo / total
        prob_bf = prob.astype(BF)
        attn_heads = jnp.einsum(
            "bhqk,bkhd->bqhd", prob_bf, value_heads, preferred_element_type=F32
        ).astype(BF)
        attn = attn_heads.reshape(group_tokens, head_width)
        attn = c.sync(attn)
        up_w.end_line()
        gate_w.end_x(0)
        up_w.start_x(0)
        down_w.end_line()
        gate_w.end_high()
        gate_w.start_x(1)
        up_w.start_high()

        def halve(total, axis):
            half = total.shape[0] // 2
            return total[:half], c.start(total[half:].astype(BF), axis)

        def added(pair):
            return pair[0] + c.sync(pair[1]).astype(F32)

        def cross(total):
            rows = own_tokens
            own = stack2(total[:rows], total[2 * rows : 3 * rows])
            sent = stack2(total[rows : 2 * rows], total[3 * rows :])
            return own, c.start(sent.astype(BF), "tensor")

        def scatter_rows(left_of, right_of, first=None, second=None):
            left_sent = c.start(left_of(other).astype(BF), "core")
            right_sent = c.start(right_of(other).astype(BF), "core")
            left = halve(left_of(own) + c.sync(left_sent).astype(F32), "zl")
            right = cross(right_of(own) + c.sync(right_sent).astype(F32))
            if first:
                first()
            left, right = added(left), added(right)
            left, right = halve(left, "tensor"), halve(right, "zl")
            if second:
                second()
            return added(left), added(right)

        def proj_second():
            up_w.end_x(0)
            up_w.end_high()
            gate_w.end_x(1)
            up_w.start_x(1)
            down_w.start_high()
            down_w.start_x(0)

        proj = columns(
            scatter_rows(
                lambda rows: dot_nt(attn[rows], wo0), lambda rows: dot_nt(attn[rows], wo1), None, proj_second
            )
        )
        attn_rms = rms_scale(proj)
        resid = tokens_f + proj * attn_rms * attn_scale

        def resid_last():
            up_w.end_x(1)
            down_w.end_high()
            down_w.end_x(0)
            down_w.start_x(1)

        h0, h1 = gather_rows(resid.astype(BF), None, resid_last)
        wg0, wg1 = gate_w.rows(0), gate_w.rows(1)
        gate = dot(h0, wg0) + dot(h1, wg1)
        sigma = jax.nn.sigmoid(gate)
        wu0, wu1 = up_w.rows(0), up_w.rows(1)
        up = dot(h0, wu0) + dot(h1, wu1)
        act = c.sync((gate * sigma * up).astype(BF))

        wd0 = down_w.rows(0)
        down_w.end_x(1)
        wd1 = down_w.rows(1)
        ffn = columns(
            scatter_rows(lambda rows: dot_nt(act[rows], wd0), lambda rows: dot_nt(act[rows], wd1))
        )

        ffn_rms = rms_scale(ffn)
        output = to_natural((resid + ffn * ffn_rms * ffn_scale).astype(BF))
        ffn_gain_term = jnp.sum(d_out * ffn * ffn_rms, axis=0)
        scaled_out = d_out * ffn_scale
        d_ffn = (
            ffn_rms
            * (
                scaled_out
                - ffn * ffn_rms * ffn_rms * jnp.mean(scaled_out * ffn, axis=1, keepdims=True)
            )
        ).astype(BF)
        f0, f1 = gather_rows(d_ffn)

        class Grad:
            def __init__(self, *terms):
                self.terms = terms
                self.x, self.total = [None, None], [None, None]

            def product(self, side, block):
                cols = slice(block * block_width, (block + 1) * block_width)
                return columns([dot_tn(halves[side][:, cols], r) for halves, r in self.terms])

            def start_x(self, block):
                self.x[block] = c.start(self.product(1, block).astype(BF), "x")

            def end_x(self, block):
                moved = c.sync(self.x[block])
                self.total[block] = self.product(0, block) + moved.astype(F32)

            def start_high(self):
                self.high = c.start(self.total[1].astype(BF), high_bits[0])

            def end_high(self):
                total = self.total[0] + c.sync(self.high).astype(F32)
                for name in high_bits[1:]:
                    total = added(halve(total, name))
                self.own, self.sent = split(total, "zl", 0)

            def start_line(self):
                self.line = c.start(self.sent.astype(BF), "zl")

            def joined(self, axis, moved, low=None):
                width = moved.shape[1] // len(self.terms)
                cols = [slice(i * width, (i + 1) * width) for i in range(len(self.terms))]
                if low is None:
                    return [ordered(axis, self.own[:, s], moved[:, s], dim=1) for s in cols]
                pairs = [(self.own[:, s], moved[:, s]) for s in cols]
                return [columns([jnp.where(low, a, b), jnp.where(low, b, a)]) for a, b in pairs]

            def end_line(self):
                moved = c.sync(self.line).astype(F32)
                self.own, sent = split(columns(self.joined("zl", moved)), "core", 0)
                self.core = c.start(sent.astype(BF), "core")

            def end(self):
                moved = c.sync(self.core).astype(F32)
                self.results = self.joined("core", moved, c.token[0, 0] == 0)

        down_grad = Grad(((f0, f1), act))
        down_grad.start_x(1)
        down_grad.start_x(0)
        f0, f1 = c.fence(f0, f1)
        d_act = dot(f0, wd0) + dot(f1, wd1)
        d_gate = (d_act * up * sigma * (1.0 + gate * (1.0 - sigma))).astype(BF)
        d_up = (d_act * gate * sigma).astype(BF)
        gate_grad = Grad(((h0, h1), d_gate))
        up_grad = Grad(((h0, h1), d_up))
        down_grad.end_x(1)
        down_grad.start_high()
        gate_grad.start_x(1)
        d_gate, d_up = c.fence(d_gate, d_up)

        def hidden_first():
            down_grad.end_x(0)
            gate_grad.start_x(0)

        def hidden_second():
            gate_grad.end_x(1)
            up_grad.start_x(1)
            down_grad.end_high()
            gate_grad.start_high()

        d_resid = d_out + columns(
            scatter_rows(
                lambda rows: dot_nt(d_gate[rows], wg0) + dot_nt(d_up[rows], wu0),
                lambda rows: dot_nt(d_gate[rows], wg1) + dot_nt(d_up[rows], wu1),
                hidden_first,
                hidden_second,
            )
        )
        attn_gain_term = jnp.sum(d_resid * proj * attn_rms, axis=0)
        scaled_resid = d_resid * attn_scale
        d_proj = (
            attn_rms
            * (
                scaled_resid
                - proj * attn_rms * attn_rms * jnp.mean(scaled_resid * proj, axis=1, keepdims=True)
            )
        ).astype(BF)

        def proj_between():
            down_grad.start_line()
            gate_grad.end_x(0)
            up_grad.start_x(0)

        def proj_last():
            up_grad.end_x(1)
            gate_grad.end_high()
            up_grad.start_high()
            gate_grad.start_line()

        p0, p1 = gather_rows(d_proj, proj_between, proj_last)
        up_grad.end_x(0)
        d_attn = (dot(p0, wo0) + dot(p1, wo1)).astype(BF)

        d_attn_heads = d_attn.reshape(heads)
        d_value = (
            jnp.einsum("bhqk,bqhd->bkhd", prob_bf, d_attn_heads, preferred_element_type=F32)
            .reshape(group_tokens, head_width)
            .astype(BF)
        )
        ov_grad = Grad(((p0, p1), attn), ((in0, in1), d_value))
        ov_grad.start_x(1)
        d_attn = c.fence(d_attn)
        d_attn_heads = d_attn.reshape(heads)
        d_prob = jnp.einsum(
            "bqhd,bkhd->bhqk", d_attn_heads, value_heads, preferred_element_type=F32
        )
        delta = jnp.einsum(
            "bqhd,bqhd->bhq", d_attn_heads, attn.reshape(heads), preferred_element_type=F32
        )[..., None]
        d_score = (prob * (d_prob - delta)).astype(BF)
        d_nq = (
            jnp.einsum("bhqk,bkhd->bqhd", d_score, key_heads, preferred_element_type=F32).reshape(
                group_tokens, head_width
            )
            * score_scale
        )
        d_nk = (
            jnp.einsum("bhqk,bqhd->bkhd", d_score, query_heads, preferred_element_type=F32).reshape(
                group_tokens, head_width
            )
            * score_scale
        )
        query_gain_term = jnp.sum(d_nq * query * q_rms, axis=0)
        key_gain_term = jnp.sum(d_nk * key_proj * k_rms, axis=0)
        scaled_q = d_nq * query_scale
        scaled_k = d_nk * key_scale
        zero = jnp.zeros((2, model_width), F32)
        placed = lax.dynamic_update_slice_in_dim(
            zero, jnp.stack([query_gain_term, key_gain_term]), head_start + c.zero, 1
        )
        gain_parts = jnp.concatenate(
            [to_relative(placed), jnp.stack([attn_gain_term, ffn_gain_term])], axis=0
        )
        gain_steps = Steps(scatter_gains(c, gain_parts))
        inner = c.sync(
            jnp.stack([jnp.sum(scaled_q * query, axis=1), jnp.sum(scaled_k * key_proj, axis=1)])
        )
        up_grad.end_high()
        ov_grad.end_x(1)
        ov_grad.start_high()
        down_grad.end_line()
        inner = pair_sum(c, inner, up_grad.start_line)
        gain_steps()
        d_query = (
            q_rms * (scaled_q - query * q_rms * q_rms * (inner[0] / model_width)[:, None])
        ).astype(BF)
        d_key = (
            k_rms * (scaled_k - key_proj * k_rms * k_rms * (inner[1] / model_width)[:, None])
        ).astype(BF)
        d_qk = columns([d_query, d_key])
        qk_grad = Grad(((in0, in1), d_query), ((in0, in1), d_key))
        qk_grad.start_x(1)
        gate_grad.end_line()
        down_grad.end()

        def tokens_first():
            ov_grad.high = c.sync(ov_grad.high)
            qk_grad.end_x(1)
            qk_grad.start_high()
            ov_grad.start_x(0)
            qk_grad.start_x(0)

        def tokens_second():
            gain_steps()
            up_grad.end_line()

        d_tokens = columns(
            scatter_rows(
                lambda rows: dot_nt(d_qk[rows], wqk0) + dot_nt(d_value[rows], wv0),
                lambda rows: dot_nt(d_qk[rows], wqk1) + dot_nt(d_value[rows], wv1),
                tokens_first,
                tokens_second,
            )
        )
        grad_tokens = to_natural(d_resid + d_tokens)
        ov_grad.end_x(0)
        ov_grad.end_high()
        ov_grad.start_line()
        qk_grad.end_x(0)
        qk_grad.end_high()
        qk_grad.start_line()
        gain_steps()
        gate_grad.end()
        ov_grad.end_line()
        gain_steps()
        up_grad.end()
        ov_grad.end()
        qk_grad.end_line()
        gain_parts = gain_steps.finish()
        qk_grad.end()
        grad_output, grad_value = ov_grad.results
        grad_query, grad_key = qk_grad.results
        return (
            output,
            grad_tokens,
            grad_query,
            grad_key,
            grad_value,
            grad_output,
            gate_grad.results[0],
            up_grad.results[0],
            down_grad.results[0],
            gain_parts[0],
            gain_parts[1],
            gain_parts[2],
            gain_parts[3],
        )

    return shards


def solution(mesh):
    dp = mesh.shape["dp"]
    high = max(dp.bit_length() - 4, 0)
    high_bits = tuple(f"z{i}" for i in range(high))
    names = high_bits + ("zl", "x", "core", "tensor")
    fine = Mesh(mesh.devices.reshape((2,) * len(names)), names)
    rows = names[:-1]
    both = names
    mapped = jax.shard_map(
        build(high_bits),
        mesh=fine,
        in_specs=(
            P(both, None),
            P(rows, None),
            P(rows, "tensor"),
            P(rows, "tensor"),
            P(rows, "tensor"),
            P(rows, "tensor"),
            P(rows, "tensor"),
            P(rows, "tensor"),
            P(rows, "tensor"),
            P(both),
            P(both),
            P(both),
            P(both),
            P(both, None),
        ),
        out_specs=(
            P(both, None),
            P(both, None),
            P(rows, "tensor"),
            P(rows, "tensor"),
            P(rows, "tensor"),
            P(rows, "tensor"),
            P(rows, "tensor"),
            P(rows, "tensor"),
            P(rows, "tensor"),
            P(both),
            P(both),
            P(both),
            P(both),
        ),
        check_vma=False,
    )
    return mapped
```
